768 devices in a mesh: ctx: 24 (over z, core), tp: 4 (over x), pp: 8 (over y).
Axes of the slice: x: 4, y: 8, z: 12, core: 2. Of those that a mesh axis runs over, the one named last changes fastest.
Arguments:
- queries: bfloat16 [8, 3072, 4096], P('pp', 'ctx', 'tp'), may hold values from -0.59765625 to 0.59765625
- key_input: bfloat16 [8, 3072, 4096], P('pp', 'ctx', 'tp'), may hold values from -6 to 6
- values: bfloat16 [8, 3072, 4096], P('pp', 'ctx', 'tp'), may hold values from -6 to 6
- log_decay: float32 [8, 3072, 32], P('pp', 'ctx', 'tp'), may hold values from -1 to 0
- conv_weight: float32 [8, 4, 4096], P('pp', None, 'tp'), may hold values from -3 to 3
- out_grad: bfloat16 [8, 3072, 4096], P('pp', 'ctx', 'tp'), may hold values from -6 to 6
Outputs:
- layer_output: bfloat16 [8, 3072, 4096], P('pp', 'ctx', 'tp')
- input_grad_next: bfloat16 [8, 3072, 4096], P('pp', 'ctx', 'tp')
The draws below stay inside these ranges and needn't reach their ends.
All inputs are finite; a program needn't handle non-finite values.
Results may differ from the reference program's by a relative error of at most 0.006.
The reference program's roundings to bfloat16 on the way count: a program that leaves them out, or rounds other values in their place, can miss the bound.
Values may be sent and summed in bfloat16 or wider, within the bound.
A program may use at most 32 MiB of HBM per device.

```python
import math
import jax
import jax.numpy as jnp
from jax import lax

HEAD_COUNT = 32
HEAD_DIM = 128
KERNEL = 4
TOK_DEV = 128
SEQUENCE_LENGTH = 3072
SECTION_COUNT = 8


def draw_log_decay(key, part):
    random_subkeys = jax.random.split(key, 7)
    slow_share = 0.5
    slow_heads = jax.random.uniform(random_subkeys[0], (SECTION_COUNT, 1, HEAD_COUNT)) < slow_share
    fast_scale = jnp.exp(jax.random.uniform(random_subkeys[1], (SECTION_COUNT, 1, HEAD_COUNT), minval=math.log(30.0), maxval=math.log(50.0)))
    slow_scale = SEQUENCE_LENGTH * jnp.exp(jax.random.uniform(random_subkeys[2], (SECTION_COUNT, 1, HEAD_COUNT), minval=math.log(2.0), maxval=math.log(6.0)))
    time_scale = jnp.where(slow_heads, slow_scale, fast_scale)
    block_count = SEQUENCE_LENGTH // TOK_DEV
    block_factor = jnp.exp(jax.random.uniform(random_subkeys[3], (SECTION_COUNT, block_count, 1, HEAD_COUNT), minval=math.log(0.5), maxval=math.log(2.0)))
    block_factor = jnp.broadcast_to(block_factor, (SECTION_COUNT, block_count, TOK_DEV, HEAD_COUNT)).reshape(SECTION_COUNT, SEQUENCE_LENGTH, HEAD_COUNT)
    position_factor = jnp.exp(jax.random.uniform(random_subkeys[4], (SECTION_COUNT, SEQUENCE_LENGTH, HEAD_COUNT), minval=math.log(0.5), maxval=math.log(2.0)))
    spike_impact = jax.random.uniform(random_subkeys[5], (SECTION_COUNT, SEQUENCE_LENGTH, HEAD_COUNT)) < 3.0 / SEQUENCE_LENGTH
    spike_penalty = jax.random.uniform(random_subkeys[6], (SECTION_COUNT, SEQUENCE_LENGTH, HEAD_COUNT), minval=0.2, maxval=0.5)
    stable_portion = -(block_factor * position_factor) / time_scale
    return (stable_portion + jnp.where(spike_impact, jnp.log(1.0 - spike_penalty), 0.0)).astype(jnp.float32)


def levels(stream_key, extent, pieces, low, high):
    level = 1.0
    for position, parts in pieces:
        steps = jax.random.uniform(jax.random.fold_in(jax.random.fold_in(stream_key, 6), position), (parts,), jnp.float32, low / len(pieces), high / len(pieces))
        level = level * jnp.repeat(jnp.exp(steps), extent[position] // parts).reshape((-1,) + (1,) * (len(extent) - 1 - position))
    return level


def normal_values(own_key, extent, deviation, limit, cuts=(), kind=jnp.bfloat16):
    entries = deviation * jax.random.normal(own_key, extent, jnp.float32)
    if cuts:
        entries = entries * levels(own_key, extent, cuts, -0.22, 0.18)
    return jnp.clip(entries, -limit, limit).astype(kind)


def setup_inputs(seed: int = 0) -> dict:
    arg_keys = jax.random.split(jax.random.key(seed), 7)
    queries = normal_values(arg_keys[0], (SECTION_COUNT, SEQUENCE_LENGTH, HEAD_COUNT * HEAD_DIM), 0.1, 0.59765625, ((0, 8), (1, 24), (2, 4)))
    key_input = normal_values(arg_keys[1], (SECTION_COUNT, SEQUENCE_LENGTH, HEAD_COUNT * HEAD_DIM), 1.0, 6.0, ((0, 8), (1, 24), (2, 4)))
    values = normal_values(arg_keys[2], (SECTION_COUNT, SEQUENCE_LENGTH, HEAD_COUNT * HEAD_DIM), 1.0, 6.0, ((0, 8), (1, 24), (2, 4)))
    log_decay = draw_log_decay(jax.random.fold_in(arg_keys[6], 71), 0)
    conv_weight = normal_values(arg_keys[4], (SECTION_COUNT, KERNEL, HEAD_COUNT * HEAD_DIM), KERNEL ** -0.5, 3.0, ((0, 8), (2, 4)), jnp.float32)
    out_grad = normal_values(arg_keys[5], (SECTION_COUNT, SEQUENCE_LENGTH, HEAD_COUNT * HEAD_DIM), 1.0, 6.0, ((0, 8), (1, 24), (2, 4)))
    return dict(queries=queries, key_input=key_input, values=values, log_decay=log_decay, conv_weight=conv_weight, out_grad=out_grad)


def to_half(value):
    return lax.optimization_barrier(value.astype(jnp.bfloat16)).astype(jnp.float32)

def decay_table(cum_decay):
    transposed = jnp.swapaxes(cum_decay, -1, -2)
    differ = transposed[..., :, None] - transposed[..., None, :]
    tok_rows = cum_decay.shape[-2]
    causal = jnp.arange(tok_rows)[:, None] >= jnp.arange(tok_rows)[None, :]
    return jnp.where(causal, jnp.exp(jnp.where(causal, differ, 0.0)), 0.0)

def one_section(section_in):
    queries, key_input, values, log_decay, conv_weight, out_grad = section_in
    seq_len = key_input.shape[0]
    feat_width = key_input.shape[1]
    blocks = seq_len // TOK_DEV
    tap_count = conv_weight.shape[0]
    width_all = HEAD_COUNT * HEAD_DIM
    padded = jnp.concatenate([jnp.zeros((tap_count - 1, feat_width), jnp.float32), key_input.astype(jnp.float32)], 0)
    conv_sum = jnp.zeros((seq_len, feat_width), jnp.float32)
    for tap_index in range(tap_count):
        start_row = tap_count - 1 - tap_index
        conv_sum = conv_sum + conv_weight[tap_index] * padded[start_row:start_row + seq_len]
    head_shape = (blocks, TOK_DEV, HEAD_COUNT, HEAD_DIM)
    key_blk = to_half(conv_sum).reshape(head_shape)
    query_tile_block = queries.astype(jnp.float32).reshape(head_shape)
    value_tile_block = values.astype(jnp.float32).reshape(head_shape)
    grad_blk = out_grad.astype(jnp.float32).reshape(head_shape)
    cum_decay = jnp.cumsum(log_decay.reshape(blocks, TOK_DEV, HEAD_COUNT), axis=1)
    block_total = cum_decay[:, -1]
    mixing = decay_table(cum_decay)
    scores = jnp.einsum('cthk,cshk->chts', query_tile_block, key_blk)
    weights = to_half(scores * mixing)
    weight_after = jnp.exp(block_total[:, None, :] - cum_decay)[..., None]
    keys_times_decay = to_half(key_blk * weight_after)
    block_state = jnp.einsum('cshk,cshv->chkv', keys_times_decay, value_tile_block)

    def forward_step(running, scan_item):
        decay_sum, block_sum = scan_item
        return (jnp.exp(decay_sum)[:, None, None] * running + block_sum, running)
    zero_state = jnp.zeros(block_state.shape[1:], jnp.float32)
    _, leading_rows = lax.scan(forward_step, zero_state, (block_total, block_state))
    opening_half = to_half(leading_rows)
    attended = jnp.einsum('chts,cshv->cthv', weights, value_tile_block)
    attended = attended + jnp.exp(cum_decay)[..., None] * jnp.einsum('cthk,chkv->cthv', query_tile_block, opening_half, precision=lax.Precision.HIGHEST)
    squares = lax.optimization_barrier(jnp.sum((attended * attended).reshape(blocks, TOK_DEV, width_all), -1))
    root_mean = jnp.sqrt(squares / width_all + 1e-06)
    normed = attended / root_mean[..., None, None]
    layer_output = normed.astype(jnp.bfloat16).reshape(seq_len, feat_width)
    shift_mean = lax.optimization_barrier(jnp.sum((grad_blk * normed).reshape(blocks, TOK_DEV, width_all), -1)) / width_all
    gradient_of_attended = to_half((grad_blk - normed * shift_mean[..., None, None]) / root_mean[..., None, None])
    queries_times_decay = to_half(query_tile_block * jnp.exp(cum_decay)[..., None])
    block_adjoint = jnp.einsum('cthk,cthv->chkv', queries_times_decay, gradient_of_attended)

    def backward_step(running, scan_item):
        decay_sum, adjoint = scan_item
        return (adjoint + jnp.exp(decay_sum)[:, None, None] * running, running)
    _, state_following = lax.scan(backward_step, zero_state, (block_total, block_adjoint), reverse=True)
    trailing_half = to_half(state_following)
    score_grad = to_half(jnp.einsum('cthv,cshv->chts', gradient_of_attended, value_tile_block) * mixing)
    query_grad = jnp.einsum('chts,cshk->cthk', score_grad, key_blk)
    query_grad = query_grad + jnp.exp(cum_decay)[..., None] * jnp.einsum('cthv,chkv->cthk', gradient_of_attended, opening_half, precision=lax.Precision.HIGHEST)
    ckey_grad = jnp.einsum('chts,cthk->cshk', score_grad, query_tile_block)
    ckey_grad = ckey_grad + weight_after * jnp.einsum('cshv,chkv->cshk', value_tile_block, trailing_half, precision=lax.Precision.HIGHEST)
    value_grad = jnp.einsum('chts,cthv->cshv', weights, gradient_of_attended)
    value_grad = value_grad + weight_after * jnp.einsum('cshk,chkv->cshv', key_blk, trailing_half, precision=lax.Precision.HIGHEST)
    grad_flat = ckey_grad.reshape(seq_len, feat_width)
    padded_grad = jnp.concatenate([grad_flat, jnp.zeros((tap_count - 1, feat_width), jnp.float32)], 0)
    key_grad = jnp.zeros((seq_len, feat_width), jnp.float32)
    for tap_index in range(tap_count):
        key_grad = key_grad + conv_weight[tap_index] * padded_grad[tap_index:tap_index + seq_len]
    input_grad = query_grad.reshape(seq_len, feat_width) + key_grad + value_grad.reshape(seq_len, feat_width)
    return (layer_output, input_grad.astype(jnp.bfloat16))

def send_back(section_grad):
    return jnp.concatenate([section_grad[1:], jnp.zeros_like(section_grad[:1])], 0)

def reference(queries, key_input, values, log_decay, conv_weight, out_grad):
    layer_output, input_grad = lax.map(one_section, (queries, key_input, values, log_decay, conv_weight, out_grad))
    return (layer_output, send_back(input_grad))
```

```python
import jax
import jax.numpy as jnp
from jax import lax
from jax.experimental import pallas as pl
from jax.experimental.pallas import tpu as pltpu
from jax.sharding import PartitionSpec as P

MESH = pl.DeviceIdType.MESH
F32 = jnp.float32
BF16 = jnp.bfloat16
HALO = 8
CHUNK = 32
GROUP = 2


def remote(src, dst, send_sem, recv_sem, where):
    return pltpu.make_async_remote_copy(
        src_ref=src,
        dst_ref=dst,
        send_sem=send_sem,
        recv_sem=recv_sem,
        device_id=where,
        device_id_type=MESH,
    )


def dot(a, b, dims):
    return lax.dot_general(a, b, (dims, ((), ())), preferred_element_type=F32)


NN = ((1,), (0,))
NT = ((1,), (1,))
TN = ((0,), (0,))


def kernel(
    ctx_n, tp_n, pp_n,
    q_hbm, k_hbm, v_hbm, ld_ref, w_ref, og_hbm,
    out_ref, gin_ref,
    q_ref, k_ref, v_ref, og_ref, halo_ref, kext, kc, grow, after, mix, wts, att, ag, acc, ckg, gst,
    cdt, bt, bt_p, acc_sq, acc_dot, tpbuf,
    s_m, s_t, f_in, f_out, p_half, p_stage,
    b_m, b_t, r_in, r_out, a_half, a_stage,
    load_sem, halo_s, halo_r, bt_s, bt_r, sx_s, sx_r, fc_s, fc_r, px_s, px_r,
    tp_s, tp_r, bx_s, bx_r, rc_s, rc_r, ax_s, ax_r, ch_s, ch_r, pp_s, pp_r,
):
    toks, feats = q_hbm.shape
    heads = ld_ref.shape[1]
    hd = feats // heads
    half = heads // 2
    taps = w_ref.shape[0]
    chunks = hd // CHUNK
    width_all = feats * tp_n
    ctx = lax.axis_index("ctx")
    tp = lax.axis_index("tp")
    pp = lax.axis_index("pp")
    core = lax.rem(ctx, 2)
    partner = ctx + 1 - 2 * core
    own0 = half * core
    their0 = half * (1 - core)
    z_first = ctx < 2
    z_last = ctx >= ctx_n - 2

    def lanes(h):
        return pl.ds(pl.multiple_of(h * hd, hd), hd)

    barrier = pltpu.get_barrier_semaphore()
    greet = []
    for step in (1, ctx_n - 1, 2, ctx_n - 2):
        greet.append({"ctx": lax.rem(ctx + step, ctx_n)})
    for step in range(1, tp_n):
        greet.append({"tp": lax.rem(tp + step, tp_n)})
    for step in (1, pp_n - 1):
        greet.append({"pp": lax.rem(pp + step, pp_n)})
    for where in greet:
        pl.semaphore_signal(barrier, inc=1, device_id=where, device_id_type=MESH)

    loads = [
        pltpu.make_async_copy(src, dst, load_sem.at[n])
        for n, (src, dst) in enumerate(
            ((k_hbm, k_ref), (v_hbm, v_ref), (q_hbm, q_ref), (og_hbm, og_ref))
        )
    ]
    for load in loads:
        load.start()

    rows_i = lax.broadcasted_iota(jnp.int32, (toks, toks), 0)
    cols_i = lax.broadcasted_iota(jnp.int32, (toks, toks), 1)
    causal = rows_i >= cols_i
    tri = causal.astype(F32)
    ld = ld_ref[...]
    cd = lax.dot_general(
        tri, ld, (NN, ((), ())), precision=lax.Precision.HIGHEST, preferred_element_type=F32
    )
    cdt[...] = lax.dot_general(
        ld, tri, (((0,), (1,)), ((), ())), precision=lax.Precision.HIGHEST,
        preferred_element_type=F32,
    )
    for h in range(heads):
        wide = jnp.broadcast_to(cd[:, h : h + 1], (toks, hd))
        total = wide[toks - 1 : toks, :]
        bt[h : h + 1, :] = total
        grow[:, h * hd : (h + 1) * hd] = jnp.exp(wide)
        after[:, h * hd : (h + 1) * hd] = jnp.exp(total - wide)
        differ = wide - cdt[h : h + 1, :]
        mix[h] = jnp.where(causal, jnp.exp(jnp.where(causal, differ, 0.0)), 0.0)

    pl.semaphore_wait(barrier, len(greet))

    tail = halo_ref.shape[0]
    halo = remote(
        k_hbm.at[pl.ds(toks - tail, tail), :], halo_ref, halo_s, halo_r,
        {"ctx": lax.rem(ctx + 1, ctx_n)},
    )

    @pl.when(ctx < ctx_n - 1)
    def _():
        halo.start()

    @pl.when(ctx == 0)
    def _():
        halo_ref[...] = jnp.zeros_like(halo_ref)

    swap_bt = remote(bt, bt_p, bt_s, bt_r, {"ctx": partner})
    swap_bt.start()

    @pl.when(z_first)
    def _():
        f_in[...] = jnp.zeros_like(f_in)

    @pl.when(z_last)
    def _():
        r_in[...] = jnp.zeros_like(r_in)

    @pl.when(ctx == ctx_n - 1)
    def _():
        ckg[pl.ds(toks, HALO), :] = jnp.zeros((HALO, feats), F32)

    @pl.when(pp == pp_n - 1)
    def _():
        gin_ref[...] = jnp.zeros_like(gin_ref)

    loads[0].wait()
    kext[pl.ds(HALO, toks), :] = k_ref[...].astype(F32)
    loads[1].wait()

    @pl.when(ctx > 0)
    def _():
        halo.wait_recv()

    kext[pl.ds(0, HALO), :] = halo_ref[pl.ds(tail - HALO, HALO), :].astype(F32)

    def swap(mine, theirs, send_sem, recv_sem, i):
        return remote(
            mine.at[their0 + i], theirs.at[i], send_sem.at[i], recv_sem.at[i], {"ctx": partner}
        )

    def states(g, _):
        for j in range(GROUP):
            idx = g * GROUP + j
            h = lax.rem(their0 + idx, heads)
            hs = lanes(h)
            conv = w_ref[pl.ds(0, 1), hs] * kext[pl.ds(HALO, toks), hs]
            for tap in range(1, taps):
                conv = conv + w_ref[pl.ds(tap, 1), hs] * kext[pl.ds(HALO - tap, toks), hs]
            keys = conv.astype(BF16)
            kc[:, hs] = keys
            scaled = (keys.astype(F32) * after[:, hs]).astype(BF16)
            s_m[h] = dot(scaled, v_ref[:, hs], TN)

        @pl.when(g < half // GROUP)
        def _():
            for j in range(GROUP):
                swap(s_m, s_t, sx_s, sx_r, g * GROUP + j).start()

        return 0

    lax.fori_loop(0, heads // GROUP, states, 0)
    swap_bt.wait_recv()

    def forward_hop(n, i, c):
        piece = pl.ds(c * CHUNK, CHUNK)
        return remote(
            f_out.at[i, piece], f_in.at[i, piece], fc_s.at[n], fc_r.at[n],
            {"ctx": lax.rem(ctx + 2, ctx_n)},
        )

    def backward_hop(n, i, c):
        piece = pl.ds(c * CHUNK, CHUNK)
        return remote(
            r_out.at[i, piece], r_in.at[i, piece], rc_s.at[n], rc_r.at[n],
            {"ctx": lax.rem(ctx + ctx_n - 2, ctx_n)},
        )

    def hand(stage, dest, send_sem, recv_sem, i, h):
        return remote(
            stage.at[i], dest.at[h], send_sem.at[i], recv_sem.at[i], {"ctx": partner}
        )

    def relay(lead, first, last, hop, mine, theirs, into, out, dest, stage, xs, xr, hs_, hr_):
        lf = lead.astype(F32)

        def one(i, _):
            h = own0 + i
            e_m = jnp.exp(bt[pl.ds(h, 1), :])
            e_t = jnp.exp(bt_p[pl.ds(h, 1), :])
            both = e_m * e_t
            ca = lf * e_t + (1.0 - lf)
            cb = lf + (1.0 - lf) * e_m
            c1 = lf + (1.0 - lf) * e_t
            s1 = 1.0 - lf
            c2 = lf * e_m + (1.0 - lf)
            s2 = lf
            swap(mine, theirs, xs, xr, i).wait_recv()
            for c in range(chunks):
                piece = pl.ds(c * CHUNK, CHUNK)
                copy = hop(i * chunks + c, i, c)

                @pl.when(jnp.logical_not(first))
                def _():
                    copy.wait_recv()

                carry = into[i, piece, :]
                sm = mine[h, piece, :]
                st = theirs[i, piece, :]
                out[i, piece, :] = both * carry + (ca * sm + cb * st)

                @pl.when(jnp.logical_not(last))
                def _():
                    copy.start()

                stage[i, piece, :] = (c2 * carry + s2 * sm).astype(BF16)
                dest[h, piece, :] = (c1 * carry + s1 * st).astype(BF16)
            hand(stage, dest, hs_, hr_, i, h).start()
            return 0

        lax.fori_loop(0, half, one, 0)

    def forward_relay():
        relay(
            core == 0, z_first, z_last, forward_hop, s_m, s_t, f_in, f_out, p_half, p_stage,
            sx_s, sx_r, px_s, px_r,
        )

    early_f = ctx < 2 * max(1, ctx_n // 8)

    @pl.when(early_f)
    def _():
        forward_relay()

    loads[2].wait()

    def inside(g, _):
        for j in range(GROUP):
            h = g * GROUP + j
            hs = lanes(h)
            scores = dot(q_ref[:, hs], kc[:, hs], NT)
            w = (scores * mix[h]).astype(BF16)
            wts[h] = w
            att[:, hs] = dot(w, v_ref[:, hs], NN)
        return 0

    lax.fori_loop(0, heads // GROUP, inside, 0)

    @pl.when(jnp.logical_not(early_f))
    def _():
        forward_relay()

    loads[3].wait()
    acc_sq[...] = jnp.zeros_like(acc_sq)
    acc_dot[...] = jnp.zeros_like(acc_dot)

    def attend(g, _):
        @pl.when(g >= half // GROUP)
        def _():
            for j in range(GROUP):
                i = g * GROUP + j - half
                hand(p_stage, p_half, px_s, px_r, i, their0 + i).wait_recv()

        for j in range(GROUP):
            h = lax.rem(own0 + g * GROUP + j, heads)
            hs = lanes(h)
            a = att[:, hs] + grow[:, hs] * dot(q_ref[:, hs], p_half[h], NN)
            att[:, hs] = a
            acc_sq[...] += a * a
            acc_dot[...] += a * og_ref[:, hs].astype(F32)
        return 0

    lax.fori_loop(0, heads // GROUP, attend, 0)

    sq_row = jnp.sum(acc_sq[...].T, axis=0, keepdims=True)
    dot_row = jnp.sum(acc_dot[...].T, axis=0, keepdims=True)
    first_row = lax.broadcasted_iota(jnp.int32, (8, toks), 0) == 0
    tpbuf[0] = jnp.where(first_row, sq_row, dot_row)

    def sums(step):
        return remote(
            tpbuf.at[0], tpbuf.at[step], tp_s.at[step - 1], tp_r.at[step - 1],
            {"tp": lax.rem(tp + step, tp_n)},
        )

    for step in range(1, tp_n):
        sums(step).start()
    for step in range(1, tp_n):
        sums(step).wait_recv()
    sums_all = tpbuf[0]
    for step in range(1, tp_n):
        sums_all = sums_all + tpbuf[step]
    inv_row = 1.0 / jnp.sqrt(sums_all[0:1, :] / width_all + 1e-06)
    shift_row = (sums_all[1:2, :] / width_all) * inv_row
    inv = jnp.broadcast_to(inv_row, (hd, toks)).T
    shift = jnp.broadcast_to(shift_row, (hd, toks)).T

    def adjoints(g, _):
        for j in range(GROUP):
            idx = g * GROUP + j
            h = lax.rem(their0 + idx, heads)
            hs = lanes(h)
            normed = att[:, hs] * inv
            out_ref[:, hs] = normed.astype(BF16)
            grad = ((og_ref[:, hs].astype(F32) - normed * shift) * inv).astype(BF16)
            ag[:, hs] = grad
            sq = (q_ref[:, hs].astype(F32) * grow[:, hs]).astype(BF16)
            b_m[h] = dot(sq, grad, TN)

        @pl.when(g < half // GROUP)
        def _():
            for j in range(GROUP):
                swap(b_m, b_t, bx_s, bx_r, g * GROUP + j).start()

        return 0

    lax.fori_loop(0, heads // GROUP, adjoints, 0)

    def backward_relay():
        relay(
            core == 1, z_last, z_first, backward_hop, b_m, b_t, r_in, r_out, a_half, a_stage,
            bx_s, bx_r, ax_s, ax_r,
        )

    early_r = ctx >= ctx_n - 2 * max(1, ctx_n // 8)

    @pl.when(early_r)
    def _():
        backward_relay()

    def inside_grads(g, _):
        for j in range(GROUP):
            h = g * GROUP + j
            hs = lanes(h)
            grad = ag[:, hs]
            sg = (dot(grad, v_ref[:, hs], NT) * mix[h]).astype(BF16)
            qg = dot(sg, kc[:, hs], NN) + grow[:, hs] * dot(grad, p_half[h], NT)
            acc[:, hs] = qg + dot(wts[h], grad, TN)
            ckg[pl.ds(0, toks), hs] = dot(sg, q_ref[:, hs], TN)
        return 0

    lax.fori_loop(0, heads // GROUP, inside_grads, 0)

    @pl.when(jnp.logical_not(early_r))
    def _():
        backward_relay()

    def edge(h):
        hs = lanes(h)
        return remote(
            ckg.at[pl.ds(0, HALO), hs], ckg.at[pl.ds(toks, HALO), hs], ch_s.at[h], ch_r.at[h],
            {"ctx": lax.rem(ctx + ctx_n - 1, ctx_n)},
        )

    def outside_grads(g, _):
        @pl.when(g >= half // GROUP)
        def _():
            for j in range(GROUP):
                i = g * GROUP + j - half
                hand(a_stage, a_half, ax_s, ax_r, i, their0 + i).wait_recv()

        for j in range(GROUP):
            h = lax.rem(own0 + g * GROUP + j, heads)
            hs = lanes(h)
            wa = after[:, hs]
            state = a_half[h]
            ckg[pl.ds(0, toks), hs] += wa * dot(v_ref[:, hs], state, NT)
            acc[:, hs] += wa * dot(kc[:, hs], state, NN)

        @pl.when(ctx > 0)
        def _():
            for j in range(GROUP):
                edge(lax.rem(own0 + g * GROUP + j, heads)).start()

        return 0

    lax.fori_loop(0, heads // GROUP, outside_grads, 0)

    def back(h):
        hs = lanes(h)
        return remote(
            gst.at[:, hs], gin_ref.at[:, hs], pp_s.at[h], pp_r.at[h],
            {"pp": lax.rem(pp + pp_n - 1, pp_n)},
        )

    def finish(g, _):
        @pl.when(ctx < ctx_n - 1)
        def _():
            for j in range(GROUP):
                edge(lax.rem(own0 + g * GROUP + j, heads)).wait_recv()

        for j in range(GROUP):
            h = lax.rem(own0 + g * GROUP + j, heads)
            hs = lanes(h)
            total = acc[:, hs]
            for tap in range(taps):
                total = total + w_ref[pl.ds(tap, 1), hs] * ckg[pl.ds(tap, toks), hs]
            gst[:, hs] = total.astype(BF16)

        @pl.when(pp > 0)
        def _():
            for j in range(GROUP):
                back(lax.rem(own0 + g * GROUP + j, heads)).start()

        return 0

    lax.fori_loop(0, heads // GROUP, finish, 0)

    @pl.when(pp < pp_n - 1)
    def _():
        def arrive(h, _):
            back(h).wait_recv()
            return 0

        lax.fori_loop(0, heads, arrive, 0)

    @pl.when(pp > 0)
    def _():
        def leave(h, _):
            back(h).wait_send()
            return 0

        lax.fori_loop(0, heads, leave, 0)

    @pl.when(ctx < ctx_n - 1)
    def _():
        halo.wait_send()

    swap_bt.wait_send()
    for step in range(1, tp_n):
        sums(step).wait_send()

    @pl.when(ctx > 0)
    def _():
        def leave(h, _):
            edge(h).wait_send()
            return 0

        lax.fori_loop(0, heads, leave, 0)

    def leave(i, _):
        swap(s_m, s_t, sx_s, sx_r, i).wait_send()
        swap(b_m, b_t, bx_s, bx_r, i).wait_send()
        hand(p_stage, p_half, px_s, px_r, i, own0 + i).wait_send()
        hand(a_stage, a_half, ax_s, ax_r, i, own0 + i).wait_send()
        return 0

    lax.fori_loop(0, half, leave, 0)

    @pl.when(jnp.logical_not(z_last))
    def _():
        def leave(n, _):
            forward_hop(n, n // chunks, lax.rem(n, chunks)).wait_send()
            return 0

        lax.fori_loop(0, half * chunks, leave, 0)

    @pl.when(jnp.logical_not(z_first))
    def _():
        def leave(n, _):
            backward_hop(n, n // chunks, lax.rem(n, chunks)).wait_send()
            return 0

        lax.fori_loop(0, half * chunks, leave, 0)


def solution(mesh):
    ctx_n, tp_n, pp_n = mesh.shape["ctx"], mesh.shape["tp"], mesh.shape["pp"]

    def per_device(queries, key_input, values, log_decay, conv_weight, out_grad):
        toks, feats = queries.shape[1:]
        heads = log_decay.shape[2]
        hd = feats // heads
        half = heads // 2
        pieces = half * (hd // CHUNK)
        dma = pltpu.SemaphoreType.DMA
        flat_b = pltpu.VMEM((toks, feats), BF16)
        flat_f = pltpu.VMEM((toks, feats), F32)
        per_head_f = pltpu.VMEM((heads, hd, hd), F32)
        per_head_b = pltpu.VMEM((heads, hd, hd), BF16)
        half_f = pltpu.VMEM((half, hd, hd), F32)
        half_b = pltpu.VMEM((half, hd, hd), BF16)
        longer = pltpu.VMEM((toks + HALO, feats), F32)
        square = pltpu.VMEM((toks, hd), F32)
        rows = pltpu.VMEM((heads, hd), F32)
        scratch = [
            flat_b, flat_b, flat_b, flat_b, pltpu.VMEM((16, feats), BF16), longer, flat_b,
            flat_f, flat_f, pltpu.VMEM((heads, toks, toks), F32),
            pltpu.VMEM((heads, toks, toks), BF16), flat_f, flat_b, flat_f, longer, flat_b,
            pltpu.VMEM((heads, toks), F32), rows, rows, square, square,
            pltpu.VMEM((tp_n, 8, toks), F32),
            per_head_f, half_f, half_f, half_f, per_head_b, half_b,
            per_head_f, half_f, half_f, half_f, per_head_b, half_b,
            dma((4,)), dma, dma, dma, dma, dma((half,)), dma((half,)),
            dma((pieces,)), dma((pieces,)), dma((half,)), dma((half,)),
            dma((tp_n - 1,)), dma((tp_n - 1,)), dma((half,)), dma((half,)),
            dma((pieces,)), dma((pieces,)), dma((half,)), dma((half,)),
            dma((heads,)), dma((heads,)), dma((heads,)), dma((heads,)),
        ]
        whole = pl.BlockSpec(memory_space=pltpu.VMEM)
        there = pl.BlockSpec(memory_space=pl.ANY)

        def body(*refs):
            kernel(ctx_n, tp_n, pp_n, *refs)

        shape = jax.ShapeDtypeStruct((toks, feats), BF16)
        out, gin = pl.pallas_call(
            body,
            out_shape=(shape, shape),
            in_specs=[there, there, there, whole, whole, there],
            out_specs=(whole, whole),
            scratch_shapes=scratch,
            compiler_params=pltpu.CompilerParams(
                collective_id=0, has_side_effects=True, vmem_limit_bytes=40 * 1024 * 1024
            ),
        )(queries[0], key_input[0], values[0], log_decay[0], conv_weight[0], out_grad[0])
        return out[None], gin[None]

    placed = (
        P("pp", "ctx", "tp"),
        P("pp", "ctx", "tp"),
        P("pp", "ctx", "tp"),
        P("pp", "ctx", "tp"),
        P("pp", None, "tp"),
        P("pp", "ctx", "tp"),
    )
    return jax.shard_map(
        per_device,
        mesh=mesh,
        in_specs=placed,
        out_specs=(P("pp", "ctx", "tp"), P("pp", "ctx", "tp")),
        check_vma=False,
    )
```

```python
import jax
import jax.numpy as jnp
from jax import lax
from jax.experimental import pallas as pl
from jax.experimental.pallas import tpu as pltpu
from jax.sharding import PartitionSpec as P

MESH = pl.DeviceIdType.MESH
F32 = jnp.float32
BF16 = jnp.bfloat16
HALO = 8
GROUP = 2


def remote(src, dst, send_sem, recv_sem, where):
    return pltpu.make_async_remote_copy(
        src_ref=src,
        dst_ref=dst,
        send_sem=send_sem,
        recv_sem=recv_sem,
        device_id=where,
        device_id_type=MESH,
    )


def dot(a, b, dims):
    return lax.dot_general(a, b, (dims, ((), ())), preferred_element_type=F32)


NN = ((1,), (0,))
NT = ((1,), (1,))
TN = ((0,), (0,))


def kernel(
    ctx_n, tp_n, pp_n,
    q_hbm, k_hbm, v_hbm, ld_ref, w_ref, og_hbm,
    out_ref, gin_ref,
    q_ref, k_ref, v_ref, og_ref, halo_ref, kext, kc, grow, after, mix, wts, att, ag, acc, ckg, gst,
    bt, bt_all, acc_sq, acc_dot, tpbuf,
    s_out, s_in, p_out, p_in, b_out, b_in, a_out, a_in,
    load_sem, halo_s, halo_r, bt_s, bt_r, tp_s, tp_r,
    s_s, s_r, p_s, p_r, b_s, b_r, a_s, a_r, ch_s, ch_r, pp_s, pp_r,
):
    toks, feats = q_hbm.shape
    heads = ld_ref.shape[0]
    hd = feats // heads
    taps = w_ref.shape[0]
    width_all = feats * tp_n
    parts = ctx_n // heads
    rows = s_in.shape[1]
    group = min(GROUP, heads)
    steps = heads // group
    ctx = lax.axis_index("ctx")
    tp = lax.axis_index("tp")
    pp = lax.axis_index("pp")
    my_head = ctx // parts
    my_part = lax.rem(ctx, parts)
    far_head = lax.rem(ctx + ctx_n // 2, ctx_n) // parts

    def lanes(h):
        return pl.ds(pl.multiple_of(h * hd, hd), hd)

    def begin(part):
        return part * rows - (part // (parts - 1)) * (parts * rows - hd)

    def fan(idx):
        return ((idx + 1) // 2) * (2 * lax.rem(idx, 2) - 1)

    def far_first(idx):
        return lax.rem(far_head + fan(idx) + heads, heads)

    def near_first(idx):
        return lax.rem(my_head + fan(idx) + heads, heads)

    barrier = pltpu.get_barrier_semaphore()
    greet = [{"ctx": lax.rem(ctx + step, ctx_n)} for step in range(1, ctx_n)]
    greet += [{"tp": lax.rem(tp + step, tp_n)} for step in range(1, tp_n)]
    if pp_n > 1:
        greet += [{"pp": lax.rem(pp + step, pp_n)} for step in (1, pp_n - 1)]
    for where in greet:
        pl.semaphore_signal(barrier, inc=1, device_id=where, device_id_type=MESH)

    loads = [
        pltpu.make_async_copy(src, dst, load_sem.at[n])
        for n, (src, dst) in enumerate(
            ((k_hbm, k_ref), (v_hbm, v_ref), (q_hbm, q_ref), (og_hbm, og_ref))
        )
    ]
    for load in loads:
        load.start()

    rows_i = lax.broadcasted_iota(jnp.int32, (toks, toks), 0)
    cols_i = lax.broadcasted_iota(jnp.int32, (toks, toks), 1)
    causal = rows_i >= cols_i
    tri = causal.astype(F32)
    ld = ld_ref[...]
    cd = lax.dot_general(
        tri, ld, (NT, ((), ())), precision=lax.Precision.HIGHEST, preferred_element_type=F32
    )
    cdt = lax.dot_general(
        ld, tri, (NT, ((), ())), precision=lax.Precision.HIGHEST, preferred_element_type=F32
    )
    for h in range(heads):
        wide = jnp.broadcast_to(cd[:, h : h + 1], (toks, hd))
        total = wide[toks - 1 : toks, :]
        bt[h] = total
        grow[:, h * hd : (h + 1) * hd] = jnp.exp(wide)
        after[:, h * hd : (h + 1) * hd] = jnp.exp(total - wide)
        differ = wide - cdt[h : h + 1, :]
        mix[h] = jnp.where(causal, jnp.exp(jnp.where(causal, differ, 0.0)), 0.0)

    pl.semaphore_wait(barrier, len(greet))

    tail = halo_ref.shape[0]
    halo = remote(
        k_hbm.at[pl.ds(toks - tail, tail), :], halo_ref, halo_s, halo_r,
        {"ctx": lax.rem(ctx + 1, ctx_n)},
    )

    @pl.when(ctx < ctx_n - 1)
    def _():
        halo.start()

    def total_to(step):
        peer = lax.rem(ctx + step, ctx_n)
        return remote(
            bt.at[peer // parts], bt_all.at[ctx], bt_s.at[step - 1], bt_r.at[step - 1],
            {"ctx": peer},
        )

    def send_total(step, _):
        total_to(step).start()
        return 0

    lax.fori_loop(1, ctx_n, send_total, 0)
    bt_all[ctx] = bt[my_head]

    @pl.when(ctx == 0)
    def _():
        halo_ref[...] = jnp.zeros_like(halo_ref)

    @pl.when(ctx == ctx_n - 1)
    def _():
        ckg[pl.ds(toks, HALO), :] = jnp.zeros((HALO, feats), F32)

    @pl.when(pp == pp_n - 1)
    def _():
        gin_ref[...] = jnp.zeros_like(gin_ref)

    loads[0].wait()
    kext[pl.ds(HALO, toks), :] = k_ref[...].astype(F32)
    loads[1].wait()

    @pl.when(ctx > 0)
    def _():
        halo.wait_recv()

    kext[pl.ds(0, HALO), :] = halo_ref[pl.ds(tail - HALO, HALO), :].astype(F32)

    def spread(src, dst, send_sem, recv_sem, h, part):
        owner = h * parts + part
        first = pl.multiple_of(begin(part), 16)
        return remote(
            src.at[h, pl.ds(first, rows)], dst.at[ctx], send_sem.at[owner], recv_sem.at[ctx],
            {"ctx": owner},
        )

    def spread_head(src, dst, send_sem, recv_sem, h):
        for part in range(parts):
            @pl.when(h * parts + part != ctx)
            def _():
                spread(src, dst, send_sem, recv_sem, h, part).start()

    def keep(src, dst):
        dst[ctx] = src[my_head, pl.ds(pl.multiple_of(begin(my_part), 16), rows), :]

    def deliver(src, dst, send_sem, recv_sem, c):
        return remote(
            src.at[c], dst.at[ctx], send_sem.at[c], recv_sem.at[ctx], {"ctx": c}
        )

    def arrive(src, recv_sem, n):
        return remote(src.at[n], src.at[n], recv_sem.at[n], recv_sem.at[n], {"ctx": ctx})

    def scan(into, recv_sem, out, home, send_sem, home_sem, order):
        def ready(step, _):
            n = lax.rem(ctx + step, ctx_n)
            arrive(into, recv_sem, n).wait_recv()
            return 0

        lax.fori_loop(1, ctx_n, ready, 0)
        carry = jnp.zeros((rows, hd), F32)
        for c in order:
            out[c] = carry.astype(BF16)
            carry = jnp.exp(bt_all[c]) * carry + into[c].astype(F32)

        def give(idx, _):
            c = lax.rem(ctx + ctx_n // 2 + fan(idx) + ctx_n, ctx_n)
            deliver(out, home, send_sem, home_sem, c).start()
            return 0

        lax.fori_loop(0, ctx_n - 1, give, 0)
        home[ctx] = out[ctx]

    def collect(home, home_sem, h):
        for part in range(parts):
            @pl.when(h * parts + part != ctx)
            def _():
                arrive(home, home_sem, h * parts + part).wait_recv()

    def whole(home, h):
        pieces = []
        for part in range(parts):
            piece = home[h * parts + part]
            pieces.append(piece[part * rows - begin(part) :, :])
        return jnp.concatenate(pieces, axis=0)

    def states(g, _):
        for j in range(group):
            h = far_first(g * group + j)
            hs = lanes(h)
            conv = w_ref[pl.ds(0, 1), hs] * kext[pl.ds(HALO, toks), hs]
            for tap in range(1, taps):
                conv = conv + w_ref[pl.ds(tap, 1), hs] * kext[pl.ds(HALO - tap, toks), hs]
            keys = conv.astype(BF16)
            kc[:, hs] = keys
            scaled = (keys.astype(F32) * after[:, hs]).astype(BF16)
            s_out[h] = dot(scaled, v_ref[:, hs], TN).astype(BF16)
        for j in range(group):
            spread_head(s_out, s_in, s_s, s_r, far_first(g * group + j))
        return 0

    lax.fori_loop(0, steps, states, 0)
    keep(s_out, s_in)
    loads[2].wait()

    def inside(g, _):
        for j in range(group):
            h = g * group + j
            hs = lanes(h)
            scores = dot(q_ref[:, hs], kc[:, hs], NT)
            w = (scores * mix[h]).astype(BF16)
            wts[h] = w
            att[:, hs] = dot(w, v_ref[:, hs], NN)
        return 0

    lax.fori_loop(0, steps, inside, 0)

    def total_in(step, _):
        total_to(step).wait_recv()
        return 0

    lax.fori_loop(1, ctx_n, total_in, 0)
    scan(s_in, s_r, p_out, p_in, p_s, p_r, range(ctx_n))

    loads[3].wait()
    acc_sq[...] = jnp.zeros_like(acc_sq)
    acc_dot[...] = jnp.zeros_like(acc_dot)

    def attend(g, _):
        for j in range(group):
            collect(p_in, p_r, near_first(g * group + j))
        for j in range(group):
            h = near_first(g * group + j)
            hs = lanes(h)
            a = att[:, hs] + grow[:, hs] * dot(q_ref[:, hs], whole(p_in, h), NN)
            att[:, hs] = a
            acc_sq[...] += a * a
            acc_dot[...] += a * og_ref[:, hs].astype(F32)
        return 0

    lax.fori_loop(0, steps, attend, 0)

    sq_row = jnp.sum(acc_sq[...].T, axis=0, keepdims=True)
    dot_row = jnp.sum(acc_dot[...].T, axis=0, keepdims=True)
    first_row = lax.broadcasted_iota(jnp.int32, (8, toks), 0) == 0
    tpbuf[0] = jnp.where(first_row, sq_row, dot_row)

    def sums(step):
        return remote(
            tpbuf.at[0], tpbuf.at[step], tp_s.at[step - 1], tp_r.at[step - 1],
            {"tp": lax.rem(tp + step, tp_n)},
        )

    for step in range(1, tp_n):
        sums(step).start()
    for step in range(1, tp_n):
        sums(step).wait_recv()
    sums_all = tpbuf[0]
    for step in range(1, tp_n):
        sums_all = sums_all + tpbuf[step]
    inv_row = 1.0 / jnp.sqrt(sums_all[0:1, :] / width_all + 1e-06)
    shift_row = (sums_all[1:2, :] / width_all) * inv_row
    inv = jnp.broadcast_to(inv_row, (hd, toks)).T
    shift = jnp.broadcast_to(shift_row, (hd, toks)).T

    def adjoints(g, _):
        for j in range(group):
            h = far_first(g * group + j)
            hs = lanes(h)
            normed = att[:, hs] * inv
            out_ref[:, hs] = normed.astype(BF16)
            grad = ((og_ref[:, hs].astype(F32) - normed * shift) * inv).astype(BF16)
            ag[:, hs] = grad
            sq = (q_ref[:, hs].astype(F32) * grow[:, hs]).astype(BF16)
            b_out[h] = dot(sq, grad, TN).astype(BF16)
        for j in range(group):
            spread_head(b_out, b_in, b_s, b_r, far_first(g * group + j))
        return 0

    lax.fori_loop(0, steps, adjoints, 0)
    keep(b_out, b_in)

    def inside_grads(g, _):
        for j in range(group):
            h = g * group + j
            hs = lanes(h)
            grad = ag[:, hs]
            sg = (dot(grad, v_ref[:, hs], NT) * mix[h]).astype(BF16)
            qg = dot(sg, kc[:, hs], NN) + grow[:, hs] * dot(grad, whole(p_in, h), NT)
            acc[:, hs] = qg + dot(wts[h], grad, TN)
            ckg[pl.ds(0, toks), hs] = dot(sg, q_ref[:, hs], TN)
        return 0

    lax.fori_loop(0, steps, inside_grads, 0)
    scan(b_in, b_r, a_out, a_in, a_s, a_r, range(ctx_n - 1, -1, -1))

    def edge(h):
        hs = lanes(h)
        return remote(
            ckg.at[pl.ds(0, HALO), hs], ckg.at[pl.ds(toks, HALO), hs], ch_s.at[h], ch_r.at[h],
            {"ctx": lax.rem(ctx + ctx_n - 1, ctx_n)},
        )

    def outside_grads(g, _):
        for j in range(group):
            collect(a_in, a_r, near_first(g * group + j))
        for j in range(group):
            h = near_first(g * group + j)
            hs = lanes(h)
            wa = after[:, hs]
            state = whole(a_in, h)
            ckg[pl.ds(0, toks), hs] += wa * dot(v_ref[:, hs], state, NT)
            acc[:, hs] += wa * dot(kc[:, hs], state, NN)

        @pl.when(ctx > 0)
        def _():
            for j in range(group):
                edge(near_first(g * group + j)).start()

        return 0

    lax.fori_loop(0, steps, outside_grads, 0)

    def back(h):
        hs = lanes(h)
        return remote(
            gst.at[:, hs], gin_ref.at[:, hs], pp_s.at[h], pp_r.at[h],
            {"pp": lax.rem(pp + pp_n - 1, pp_n)},
        )

    def finish(g, _):
        @pl.when(ctx < ctx_n - 1)
        def _():
            for j in range(group):
                edge(near_first(g * group + j)).wait_recv()

        for j in range(group):
            h = near_first(g * group + j)
            hs = lanes(h)
            total = acc[:, hs]
            for tap in range(taps):
                total = total + w_ref[pl.ds(tap, 1), hs] * ckg[pl.ds(tap, toks), hs]
            gst[:, hs] = total.astype(BF16)

        @pl.when(pp > 0)
        def _():
            for j in range(group):
                back(near_first(g * group + j)).start()

        return 0

    lax.fori_loop(0, steps, finish, 0)

    @pl.when(ctx < ctx_n - 1)
    def _():
        halo.wait_send()

    for step in range(1, tp_n):
        sums(step).wait_send()

    def left(step, _):
        peer = lax.rem(ctx + step, ctx_n)
        total_to(step).wait_send()
        h, part = peer // parts, lax.rem(peer, parts)
        spread(s_out, s_in, s_s, s_r, h, part).wait_send()
        spread(b_out, b_in, b_s, b_r, h, part).wait_send()
        deliver(p_out, p_in, p_s, p_r, peer).wait_send()
        deliver(a_out, a_in, a_s, a_r, peer).wait_send()
        return 0

    lax.fori_loop(1, ctx_n, left, 0)

    @pl.when(ctx > 0)
    def _():
        def leave(h, _):
            edge(h).wait_send()
            return 0

        lax.fori_loop(0, heads, leave, 0)

    @pl.when(pp > 0)
    def _():
        def leave(h, _):
            back(h).wait_send()
            return 0

        lax.fori_loop(0, heads, leave, 0)

    @pl.when(pp < pp_n - 1)
    def _():
        def land(h, _):
            back(h).wait_recv()
            return 0

        lax.fori_loop(0, heads, land, 0)


def solution(mesh):
    ctx_n, tp_n, pp_n = mesh.shape["ctx"], mesh.shape["tp"], mesh.shape["pp"]

    def per_device(queries, key_input, values, log_decay, conv_weight, out_grad):
        toks, feats = queries.shape[1:]
        heads = log_decay.shape[2]
        hd = feats // heads
        parts = ctx_n // heads
        rows = -(-hd // (16 * parts)) * 16
        dma = pltpu.SemaphoreType.DMA
        flat_b = pltpu.VMEM((toks, feats), BF16)
        flat_f = pltpu.VMEM((toks, feats), F32)
        states = pltpu.VMEM((heads, hd, hd), BF16)
        shares = pltpu.VMEM((ctx_n, rows, hd), BF16)
        longer = pltpu.VMEM((toks + HALO, feats), F32)
        square = pltpu.VMEM((toks, hd), F32)
        scratch = [
            flat_b, flat_b, flat_b, flat_b, pltpu.VMEM((16, feats), BF16), longer, flat_b,
            flat_f, flat_f, pltpu.VMEM((heads, toks, toks), F32),
            pltpu.VMEM((heads, toks, toks), BF16), flat_f, flat_b, flat_f, longer, flat_b,
            pltpu.VMEM((heads, 1, hd), F32), pltpu.VMEM((ctx_n, 1, hd), F32), square, square,
            pltpu.VMEM((tp_n, 8, toks), F32),
            states, shares, shares, shares, states, shares, shares, shares,
            dma((4,)), dma, dma, dma((ctx_n - 1,)), dma((ctx_n - 1,)),
            dma((tp_n - 1,)), dma((tp_n - 1,)),
        ]
        scratch += [dma((ctx_n,))] * 8 + [dma((heads,))] * 4
        whole = pl.BlockSpec(memory_space=pltpu.VMEM)
        there = pl.BlockSpec(memory_space=pl.ANY)

        def body(*refs):
            kernel(ctx_n, tp_n, pp_n, *refs)

        shape = jax.ShapeDtypeStruct((toks, feats), BF16)
        out, gin = pl.pallas_call(
            body,
            out_shape=(shape, shape),
            in_specs=[there, there, there, whole, whole, there],
            out_specs=(whole, whole),
            scratch_shapes=scratch,
            compiler_params=pltpu.CompilerParams(
                collective_id=0, has_side_effects=True, vmem_limit_bytes=63 * 1024 * 1024
            ),
        )(
            queries[0], key_input[0], values[0], log_decay[0].T, conv_weight[0], out_grad[0]
        )
        return out[None], gin[None]

    placed = (
        P("pp", "ctx", "tp"),
        P("pp", "ctx", "tp"),
        P("pp", "ctx", "tp"),
        P("pp", "ctx", "tp"),
        P("pp", None, "tp"),
        P("pp", "ctx", "tp"),
    )
    return jax.shard_map(
        per_device,
        mesh=mesh,
        in_specs=placed,
        out_specs=(P("pp", "ctx", "tp"), P("pp", "ctx", "tp")),
        check_vma=False,
    )
```

```python
import jax
import jax.numpy as jnp
from jax import lax
from jax.experimental import pallas as pl
from jax.experimental.pallas import tpu as pltpu
from jax.sharding import PartitionSpec as P

MESH = pl.DeviceIdType.MESH
F32 = jnp.float32
BF16 = jnp.bfloat16
HALO = 8
GROUP = 2


def remote(src, dst, send_sem, recv_sem, where):
    return pltpu.make_async_remote_copy(
        src_ref=src,
        dst_ref=dst,
        send_sem=send_sem,
        recv_sem=recv_sem,
        device_id=where,
        device_id_type=MESH,
    )


def dot(a, b, dims):
    return lax.dot_general(a, b, (dims, ((), ())), preferred_element_type=F32)


NN = ((1,), (0,))
NT = ((1,), (1,))
TN = ((0,), (0,))


def kernel(
    ctx_n, tp_n, pp_n,
    q_hbm, k_hbm, v_hbm, ld_ref, w_ref, og_hbm,
    out_ref, gin_ref,
    q_ref, k_ref, v_ref, og_ref, halo_ref, kext, kc, grow, after, mix, wts, att, ag, acc, ckg, gst,
    bt, bt_p, bt_all, acc_sq, acc_dot, tpbuf,
    s_m, s_t, s_out, s_in, p_out, p_in, p_half, p_stage,
    b_m, b_t, b_out, b_in, a_out, a_in, a_half, a_stage,
    load_sem, halo_s, halo_r, bp_s, bp_r, bt_s, bt_r, tp_s, tp_r,
    s_s, s_r, p_s, p_r, b_s, b_r, a_s, a_r,
    sx_s, sx_r, px_s, px_r, bx_s, bx_r, ax_s, ax_r, ch_s, ch_r, pp_s, pp_r,
):
    toks, feats = q_hbm.shape
    heads = ld_ref.shape[0]
    hd = feats // heads
    taps = w_ref.shape[0]
    width_all = feats * tp_n
    parts = ctx_n // heads
    rows = s_in.shape[1]
    short = hd - rows * (parts - 1)
    group = min(GROUP, heads // 2)
    steps = heads // group
    half = heads // 2
    half_steps = half // group
    chips = ctx_n // 2
    ctx = lax.axis_index("ctx")
    tp = lax.axis_index("tp")
    pp = lax.axis_index("pp")
    core = lax.rem(ctx, 2)
    chip = ctx // 2
    partner = ctx + 1 - 2 * core
    own0 = half * core
    their0 = half * (1 - core)
    my_head = ctx // parts
    my_part = lax.rem(ctx, parts)
    scan_core = my_head // half

    def lanes(h):
        return pl.ds(pl.multiple_of(h * hd, hd), hd)

    def fan(idx):
        return ((idx + 1) // 2) * (2 * lax.rem(idx, 2) - 1)

    def carried(side, n):
        place = lax.rem(2 * chip + side - chips * side + ctx_n, ctx_n)
        down = 1 - lax.rem(place + ctx_n // 4, ctx_n) // chips
        return n + down * (half - 1 - 2 * n)

    def own_first(idx):
        side = core + (idx // half) * (1 - 2 * core)
        return half * side + carried(side, lax.rem(idx, half))

    def own_last(idx):
        return own_first(lax.rem(idx + half, heads))

    barrier = pltpu.get_barrier_semaphore()
    greet = [{"ctx": lax.rem(ctx + step, ctx_n)} for step in range(1, ctx_n)]
    greet += [{"tp": lax.rem(tp + step, tp_n)} for step in range(1, tp_n)]
    if pp_n > 1:
        greet += [{"pp": lax.rem(pp + step, pp_n)} for step in (1, pp_n - 1)]
    for where in greet:
        pl.semaphore_signal(barrier, inc=1, device_id=where, device_id_type=MESH)

    loads = [
        pltpu.make_async_copy(src, dst, load_sem.at[n])
        for n, (src, dst) in enumerate(
            ((k_hbm, k_ref), (v_hbm, v_ref), (q_hbm, q_ref), (og_hbm, og_ref))
        )
    ]
    for load in loads:
        load.start()

    rows_i = lax.broadcasted_iota(jnp.int32, (toks, toks), 0)
    cols_i = lax.broadcasted_iota(jnp.int32, (toks, toks), 1)
    causal = rows_i >= cols_i
    tri = causal.astype(F32)
    ld = ld_ref[...]
    cd = lax.dot_general(
        tri, ld, (NT, ((), ())), precision=lax.Precision.HIGHEST, preferred_element_type=F32
    )
    cdt = lax.dot_general(
        ld, tri, (NT, ((), ())), precision=lax.Precision.HIGHEST, preferred_element_type=F32
    )
    for h in range(heads):
        wide = jnp.broadcast_to(cd[:, h : h + 1], (toks, hd))
        total = wide[toks - 1 : toks, :]
        bt[h] = total
        grow[:, h * hd : (h + 1) * hd] = jnp.exp(wide)
        after[:, h * hd : (h + 1) * hd] = jnp.exp(total - wide)
        differ = wide - cdt[h : h + 1, :]
        mix[h] = jnp.where(causal, jnp.exp(jnp.where(causal, differ, 0.0)), 0.0)

    pl.semaphore_wait(barrier, len(greet))

    tail = halo_ref.shape[0]
    halo = remote(
        k_hbm.at[pl.ds(toks - tail, tail), :], halo_ref, halo_s, halo_r,
        {"ctx": lax.rem(ctx + 1, ctx_n)},
    )

    @pl.when(ctx < ctx_n - 1)
    def _():
        halo.start()

    def total_to(step):
        peer = lax.rem(ctx + step, ctx_n)
        return remote(
            bt.at[peer // parts], bt_all.at[ctx], bt_s.at[step - 1], bt_r.at[step - 1],
            {"ctx": peer},
        )

    def send_total(step, _):
        total_to(step).start()
        return 0

    lax.fori_loop(1, ctx_n, send_total, 0)
    bt_all[ctx] = bt[my_head]

    @pl.when(ctx == 0)
    def _():
        halo_ref[...] = jnp.zeros_like(halo_ref)

    @pl.when(ctx == ctx_n - 1)
    def _():
        ckg[pl.ds(toks, HALO), :] = jnp.zeros((HALO, feats), F32)

    @pl.when(pp == pp_n - 1)
    def _():
        gin_ref[...] = jnp.zeros_like(gin_ref)

    loads[0].wait()
    kext[pl.ds(HALO, toks), :] = k_ref[...].astype(F32)
    loads[1].wait()

    @pl.when(ctx > 0)
    def _():
        halo.wait_recv()

    kext[pl.ds(0, HALO), :] = halo_ref[pl.ds(tail - HALO, HALO), :].astype(F32)

    swap_bt = remote(bt, bt_p, bp_s, bp_r, {"ctx": partner})
    swap_bt.start()

    def sized(call):
        @pl.when(my_part < parts - 1)
        def _():
            call(rows)

        @pl.when(my_part == parts - 1)
        def _():
            call(short)

    if short < rows:
        @pl.when(my_part == parts - 1)
        def _():
            s_in[:, pl.ds(short, rows - short), :] = jnp.zeros((chips, rows - short, hd), BF16)
            b_in[:, pl.ds(short, rows - short), :] = jnp.zeros((chips, rows - short, hd), BF16)

    def swap(mine, theirs, send_sem, recv_sem, i):
        return remote(
            mine.at[their0 + i], theirs.at[i], send_sem.at[i], recv_sem.at[i], {"ctx": partner}
        )

    def spread(src, dst, send_sem, recv_sem, i, part):
        size = rows if part < parts - 1 else short
        return remote(
            src.at[i, pl.ds(part * rows, size)], dst.at[chip, pl.ds(0, size)],
            send_sem.at[i * parts + part], recv_sem.at[chip],
            {"ctx": (own0 + i) * parts + part},
        )

    def deliver(src, dst, send_sem, recv_sem, z, size):
        slot = ctx - scan_core * chips
        return remote(
            src.at[z, pl.ds(0, size)], dst.at[slot, pl.ds(0, size)], send_sem.at[z],
            recv_sem.at[slot], {"ctx": 2 * z + scan_core},
        )

    def arrive(dst, recv_sem, n, size):
        piece = dst.at[n, pl.ds(0, size)]
        return remote(piece, piece, recv_sem.at[n], recv_sem.at[n], {"ctx": partner})

    def factors(h, lead):
        e_m = jnp.exp(bt[h])
        e_t = jnp.exp(bt_p[h])
        return e_m, e_t, lead.astype(F32)

    def join(mine, theirs, xs, xr, out, into, send_sem, recv_sem, lead):
        def one(n, _):
            i = carried(core, n)
            h = own0 + i
            e_m, e_t, lf = factors(h, lead)
            swap(mine, theirs, xs, xr, i).wait_recv()
            ca = lf * e_t + (1.0 - lf)
            cb = lf + (1.0 - lf) * e_m
            out[i] = (ca * mine[h] + cb * theirs[i]).astype(BF16)
            for part in range(parts):
                @pl.when(h * parts + part != ctx)
                def _():
                    spread(out, into, send_sem, recv_sem, i, part).start()

                @pl.when(h * parts + part == ctx)
                def _():
                    size = rows if part < parts - 1 else short
                    into[chip, pl.ds(0, size), :] = out[i, pl.ds(part * rows, size), :]
            return 0

        lax.fori_loop(0, half, one, 0)

    def scan(into, recv_sem, out, home, send_sem, home_sem, order):
        def ready(z, _):
            @pl.when(2 * z + scan_core != ctx)
            def _():
                sized(lambda size: arrive(into, recv_sem, z, size).wait_recv())

            return 0

        lax.fori_loop(0, chips, ready, 0)
        carry = jnp.zeros((rows, hd), F32)
        for z in order:
            out[z] = carry.astype(BF16)
            carry = jnp.exp(bt_all[2 * z] + bt_all[2 * z + 1]) * carry + into[z].astype(F32)

        def give(idx, _):
            z = lax.rem(chip + chips // 2 + fan(idx) + chips, chips)

            @pl.when(2 * z + scan_core != ctx)
            def _():
                sized(lambda size: deliver(out, home, send_sem, home_sem, z, size).start())

            return 0

        lax.fori_loop(0, chips, give, 0)

        @pl.when(scan_core == core)
        def _():
            home[ctx - scan_core * chips] = out[chip]

    def hand(stage, dest, send_sem, recv_sem, i, h):
        return remote(
            stage.at[i], dest.at[h], send_sem.at[i], recv_sem.at[i], {"ctx": partner}
        )

    def split(home, home_sem, mine, theirs, dest, stage, hs_, hr_, lead):
        def one(n, _):
            i = carried(core, n)
            h = own0 + i
            e_m, e_t, lf = factors(h, lead)
            pieces = []
            for part in range(parts):
                size = rows if part < parts - 1 else short

                @pl.when(h * parts + part != ctx)
                def _():
                    arrive(home, home_sem, i * parts + part, size).wait_recv()

                pieces.append(home[i * parts + part, pl.ds(0, size), :].astype(F32))
            carry = jnp.concatenate(pieces, axis=0)
            c1 = lf + (1.0 - lf) * e_t
            c2 = lf * e_m + (1.0 - lf)
            stage[i] = (c2 * carry + lf * mine[h]).astype(BF16)
            hand(stage, dest, hs_, hr_, i, h).start()
            dest[h] = (c1 * carry + (1.0 - lf) * theirs[i]).astype(BF16)
            return 0

        lax.fori_loop(0, half, one, 0)

    def handed(stage, dest, hs_, hr_, g):
        @pl.when(g >= half_steps)
        def _():
            for j in range(group):
                h = own_first(g * group + j)
                hand(stage, dest, hs_, hr_, h - their0, h).wait_recv()

    def states(g, _):
        for j in range(group):
            h = own_last(g * group + j)
            hs = lanes(h)
            conv = w_ref[pl.ds(0, 1), hs] * kext[pl.ds(HALO, toks), hs]
            for tap in range(1, taps):
                conv = conv + w_ref[pl.ds(tap, 1), hs] * kext[pl.ds(HALO - tap, toks), hs]
            keys = conv.astype(BF16)
            kc[:, hs] = keys
            scaled = (keys.astype(F32) * after[:, hs]).astype(BF16)
            s_m[h] = dot(scaled, v_ref[:, hs], TN)

        @pl.when(g < half_steps)
        def _():
            for j in range(group):
                swap(s_m, s_t, sx_s, sx_r, own_last(g * group + j) - their0).start()

        return 0

    lax.fori_loop(0, steps, states, 0)
    swap_bt.wait_recv()
    join(s_m, s_t, sx_s, sx_r, s_out, s_in, s_s, s_r, core == 0)
    loads[2].wait()

    def inside(g, _):
        for j in range(group):
            h = g * group + j
            hs = lanes(h)
            scores = dot(q_ref[:, hs], kc[:, hs], NT)
            w = (scores * mix[h]).astype(BF16)
            wts[h] = w
            att[:, hs] = dot(w, v_ref[:, hs], NN)
        return 0

    lax.fori_loop(0, steps, inside, 0)

    def total_in(step, _):
        total_to(step).wait_recv()
        return 0

    lax.fori_loop(1, ctx_n, total_in, 0)
    scan(s_in, s_r, p_out, p_in, p_s, p_r, range(chips))
    split(p_in, p_r, s_m, s_t, p_half, p_stage, px_s, px_r, core == 0)

    loads[3].wait()
    acc_sq[...] = jnp.zeros_like(acc_sq)
    acc_dot[...] = jnp.zeros_like(acc_dot)

    def attend(g, _):
        handed(p_stage, p_half, px_s, px_r, g)
        for j in range(group):
            h = own_first(g * group + j)
            hs = lanes(h)
            a = att[:, hs] + grow[:, hs] * dot(q_ref[:, hs], p_half[h], NN)
            att[:, hs] = a
            acc_sq[...] += a * a
            acc_dot[...] += a * og_ref[:, hs].astype(F32)
        return 0

    lax.fori_loop(0, steps, attend, 0)

    sq_row = jnp.sum(acc_sq[...].T, axis=0, keepdims=True)
    dot_row = jnp.sum(acc_dot[...].T, axis=0, keepdims=True)
    first_row = lax.broadcasted_iota(jnp.int32, (8, toks), 0) == 0
    tpbuf[0] = jnp.where(first_row, sq_row, dot_row)

    def sums(step):
        return remote(
            tpbuf.at[0], tpbuf.at[step], tp_s.at[step - 1], tp_r.at[step - 1],
            {"tp": lax.rem(tp + step, tp_n)},
        )

    for step in range(1, tp_n):
        sums(step).start()
    for step in range(1, tp_n):
        sums(step).wait_recv()
    sums_all = tpbuf[0]
    for step in range(1, tp_n):
        sums_all = sums_all + tpbuf[step]
    inv_row = 1.0 / jnp.sqrt(sums_all[0:1, :] / width_all + 1e-06)
    shift_row = (sums_all[1:2, :] / width_all) * inv_row
    inv = jnp.broadcast_to(inv_row, (hd, toks)).T
    shift = jnp.broadcast_to(shift_row, (hd, toks)).T

    def adjoints(g, _):
        for j in range(group):
            h = own_last(g * group + j)
            hs = lanes(h)
            normed = att[:, hs] * inv
            out_ref[:, hs] = normed.astype(BF16)
            grad = ((og_ref[:, hs].astype(F32) - normed * shift) * inv).astype(BF16)
            ag[:, hs] = grad
            sq = (q_ref[:, hs].astype(F32) * grow[:, hs]).astype(BF16)
            b_m[h] = dot(sq, grad, TN)

        @pl.when(g < half_steps)
        def _():
            for j in range(group):
                swap(b_m, b_t, bx_s, bx_r, own_last(g * group + j) - their0).start()

        return 0

    lax.fori_loop(0, steps, adjoints, 0)
    join(b_m, b_t, bx_s, bx_r, b_out, b_in, b_s, b_r, core == 1)

    def inside_grads(g, _):
        for j in range(group):
            h = g * group + j
            hs = lanes(h)
            grad = ag[:, hs]
            sg = (dot(grad, v_ref[:, hs], NT) * mix[h]).astype(BF16)
            qg = dot(sg, kc[:, hs], NN) + grow[:, hs] * dot(grad, p_half[h], NT)
            acc[:, hs] = qg + dot(wts[h], grad, TN)
            ckg[pl.ds(0, toks), hs] = dot(sg, q_ref[:, hs], TN)
        return 0

    lax.fori_loop(0, steps, inside_grads, 0)
    scan(b_in, b_r, a_out, a_in, a_s, a_r, range(chips - 1, -1, -1))
    split(a_in, a_r, b_m, b_t, a_half, a_stage, ax_s, ax_r, core == 1)

    def edge(h):
        hs = lanes(h)
        return remote(
            ckg.at[pl.ds(0, HALO), hs], ckg.at[pl.ds(toks, HALO), hs], ch_s.at[h], ch_r.at[h],
            {"ctx": lax.rem(ctx + ctx_n - 1, ctx_n)},
        )

    def outside_grads(g, _):
        handed(a_stage, a_half, ax_s, ax_r, g)
        for j in range(group):
            h = own_first(g * group + j)
            hs = lanes(h)
            wa = after[:, hs]
            state = a_half[h]
            ckg[pl.ds(0, toks), hs] += wa * dot(v_ref[:, hs], state, NT)
            acc[:, hs] += wa * dot(kc[:, hs], state, NN)

        @pl.when(ctx > 0)
        def _():
            for j in range(group):
                edge(own_first(g * group + j)).start()

        return 0

    lax.fori_loop(0, steps, outside_grads, 0)

    def back(h):
        hs = lanes(h)
        return remote(
            gst.at[:, hs], gin_ref.at[:, hs], pp_s.at[h], pp_r.at[h],
            {"pp": lax.rem(pp + pp_n - 1, pp_n)},
        )

    def finish(g, _):
        @pl.when(ctx < ctx_n - 1)
        def _():
            for j in range(group):
                edge(own_first(g * group + j)).wait_recv()

        for j in range(group):
            h = own_first(g * group + j)
            hs = lanes(h)
            total = acc[:, hs]
            for tap in range(taps):
                total = total + w_ref[pl.ds(tap, 1), hs] * ckg[pl.ds(tap, toks), hs]
            gst[:, hs] = total.astype(BF16)

        @pl.when(pp > 0)
        def _():
            for j in range(group):
                back(own_first(g * group + j)).start()

        return 0

    lax.fori_loop(0, steps, finish, 0)

    @pl.when(ctx < ctx_n - 1)
    def _():
        halo.wait_send()

    for step in range(1, tp_n):
        sums(step).wait_send()

    swap_bt.wait_send()

    def told(step, _):
        total_to(step).wait_send()
        return 0

    lax.fori_loop(1, ctx_n, told, 0)

    def left(i, _):
        h = own0 + i
        swap(s_m, s_t, sx_s, sx_r, i).wait_send()
        swap(b_m, b_t, bx_s, bx_r, i).wait_send()
        hand(p_stage, p_half, px_s, px_r, i, h).wait_send()
        hand(a_stage, a_half, ax_s, ax_r, i, h).wait_send()
        for part in range(parts):
            @pl.when(h * parts + part != ctx)
            def _():
                spread(s_out, s_in, s_s, s_r, i, part).wait_send()
                spread(b_out, b_in, b_s, b_r, i, part).wait_send()
        return 0

    lax.fori_loop(0, half, left, 0)

    def given(z, _):
        @pl.when(2 * z + scan_core != ctx)
        def _():
            sized(lambda size: deliver(p_out, p_in, p_s, p_r, z, size).wait_send())
            sized(lambda size: deliver(a_out, a_in, a_s, a_r, z, size).wait_send())

        return 0

    lax.fori_loop(0, chips, given, 0)

    @pl.when(ctx > 0)
    def _():
        def leave(h, _):
            edge(h).wait_send()
            return 0

        lax.fori_loop(0, heads, leave, 0)

    @pl.when(pp > 0)
    def _():
        def leave(h, _):
            back(h).wait_send()
            return 0

        lax.fori_loop(0, heads, leave, 0)

    @pl.when(pp < pp_n - 1)
    def _():
        def land(h, _):
            back(h).wait_recv()
            return 0

        lax.fori_loop(0, heads, land, 0)


def solution(mesh):
    ctx_n, tp_n, pp_n = mesh.shape["ctx"], mesh.shape["tp"], mesh.shape["pp"]

    def per_device(queries, key_input, values, log_decay, conv_weight, out_grad):
        toks, feats = queries.shape[1:]
        heads = log_decay.shape[2]
        hd = feats // heads
        parts = ctx_n // heads
        rows = -(-hd // (16 * parts)) * 16
        dma = pltpu.SemaphoreType.DMA
        flat_b = pltpu.VMEM((toks, feats), BF16)
        flat_f = pltpu.VMEM((toks, feats), F32)
        half = heads // 2
        chips = ctx_n // 2
        full_f = pltpu.VMEM((heads, hd, hd), F32)
        full_b = pltpu.VMEM((heads, hd, hd), BF16)
        half_f = pltpu.VMEM((half, hd, hd), F32)
        half_b = pltpu.VMEM((half, hd, hd), BF16)
        shares = pltpu.VMEM((chips, rows, hd), BF16)
        totals = pltpu.VMEM((heads, 1, hd), F32)
        scanned = [full_f, half_f, half_b, shares, shares, shares, full_b, half_b]
        longer = pltpu.VMEM((toks + HALO, feats), F32)
        square = pltpu.VMEM((toks, hd), F32)
        scratch = [
            flat_b, flat_b, flat_b, flat_b, pltpu.VMEM((16, feats), BF16), longer, flat_b,
            flat_f, flat_f, pltpu.VMEM((heads, toks, toks), F32),
            pltpu.VMEM((heads, toks, toks), BF16), flat_f, flat_b, flat_f, longer, flat_b,
            totals, totals, pltpu.VMEM((ctx_n, 1, hd), F32), square, square,
            pltpu.VMEM((tp_n, 8, toks), F32),
        ]
        scratch += scanned + scanned
        scratch += [dma((4,)), dma, dma, dma, dma, dma((ctx_n - 1,)), dma((ctx_n - 1,))]
        scratch += [dma((max(tp_n - 1, 1),))] * 2 + [dma((chips,))] * 8 + [dma((half,))] * 8
        scratch += [dma((heads,))] * 4
        whole = pl.BlockSpec(memory_space=pltpu.VMEM)
        there = pl.BlockSpec(memory_space=pl.ANY)

        def body(*refs):
            kernel(ctx_n, tp_n, pp_n, *refs)

        shape = jax.ShapeDtypeStruct((toks, feats), BF16)
        out, gin = pl.pallas_call(
            body,
            out_shape=(shape, shape),
            in_specs=[there, there, there, whole, whole, there],
            out_specs=(whole, whole),
            scratch_shapes=scratch,
            compiler_params=pltpu.CompilerParams(
                collective_id=0, has_side_effects=True, vmem_limit_bytes=63 * 1024 * 1024
            ),
        )(
            queries[0], key_input[0], values[0], log_decay[0].T, conv_weight[0], out_grad[0]
        )
        return out[None], gin[None]

    placed = (
        P("pp", "ctx", "tp"),
        P("pp", "ctx", "tp"),
        P("pp", "ctx", "tp"),
        P("pp", "ctx", "tp"),
        P("pp", None, "tp"),
        P("pp", "ctx", "tp"),
    )
    return jax.shard_map(
        per_device,
        mesh=mesh,
        in_specs=placed,
        out_specs=(P("pp", "ctx", "tp"), P("pp", "ctx", "tp")),
        check_vma=False,
    )
```

```python
import jax
import jax.numpy as jnp
from jax import lax
from jax.experimental import pallas as pl
from jax.experimental.pallas import tpu as pltpu
from jax.sharding import PartitionSpec as P

MESH = pl.DeviceIdType.MESH
F32 = jnp.float32
BF16 = jnp.bfloat16
HALO = 8
GROUP = 2


def remote(src, dst, send_sem, recv_sem, where):
    return pltpu.make_async_remote_copy(
        src_ref=src,
        dst_ref=dst,
        send_sem=send_sem,
        recv_sem=recv_sem,
        device_id=where,
        device_id_type=MESH,
    )


def dot(a, b, dims):
    return lax.dot_general(a, b, (dims, ((), ())), preferred_element_type=F32)


NN = ((1,), (0,))
NT = ((1,), (1,))
TN = ((0,), (0,))


def kernel(
    ctx_n, tp_n, pp_n,
    q_hbm, k_hbm, v_hbm, ld_ref, w_ref, og_hbm,
    out_ref, gin_ref,
    q_ref, k_ref, v_ref, og_ref, halo_ref, kext, kc, grow, after, mix, wts, att, ag, acc, ckg, gst,
    bt, bt_p, tot, bt_all, acc_sq, acc_dot, tpbuf,
    s_m, s_t, s_out, s_in, p_out, p_in, p_half, p_stage,
    b_m, b_t, b_out, b_in, a_out, a_in, a_half, a_stage,
    here, load_sem, halo_s, halo_r, bp_s, bp_r, bt_s, bt_r, tp_s, tp_r,
    s_s, s_r, p_s, p_r, b_s, b_r, a_s, a_r,
    sx_s, sx_r, px_s, px_r, bx_s, bx_r, ax_s, ax_r, ch_s, ch_r, pp_s, pp_r,
):
    toks, feats = q_hbm.shape
    heads = ld_ref.shape[0]
    hd = feats // heads
    taps = w_ref.shape[0]
    width_all = feats * tp_n
    parts = ctx_n // heads
    rows = s_in.shape[1]
    short = hd - rows * (parts - 1)
    group = min(GROUP, heads // 2)
    steps = heads // group
    half = heads // 2
    half_steps = half // group
    chips = ctx_n // 2
    ctx = lax.axis_index("ctx")
    tp = lax.axis_index("tp")
    pp = lax.axis_index("pp")
    core = lax.rem(ctx, 2)
    chip = ctx // 2
    partner = ctx + 1 - 2 * core
    own0 = half * core
    their0 = half * (1 - core)
    my_head = ctx // parts
    my_part = lax.rem(ctx, parts)
    scan_core = my_head // half

    def lanes(h):
        return pl.ds(pl.multiple_of(h * hd, hd), hd)

    def own_first(idx):
        return lax.rem(own0 + idx, heads)

    def own_last(idx):
        return lax.rem(their0 + idx, heads)

    barrier = pltpu.get_barrier_semaphore()
    greet = [{"ctx": partner}]
    greet += [{"tp": lax.rem(tp + step, tp_n)} for step in range(1, tp_n)]
    for where in greet:
        pl.semaphore_signal(barrier, inc=1, device_id=where, device_id_type=MESH)

    @pl.when(pp < pp_n - 1)
    def _():
        pl.semaphore_signal(
            barrier, inc=1, device_id={"pp": lax.rem(pp + 1, pp_n)}, device_id_type=MESH
        )

    def enter(peer, _):
        pl.semaphore_signal(barrier, inc=1, device_id={"ctx": peer}, device_id_type=MESH)
        return 0

    lax.fori_loop(2 * chip + 2, ctx_n, enter, 0)

    def meet(z):
        @pl.when(jnp.logical_and(z > chip, z != chip + core))
        def _():
            pl.semaphore_wait(here.at[z], 2)

    loads = [
        pltpu.make_async_copy(src, dst, load_sem.at[n])
        for n, (src, dst) in enumerate(
            ((k_hbm, k_ref), (v_hbm, v_ref), (q_hbm, q_ref), (og_hbm, og_ref))
        )
    ]
    for load in loads:
        load.start()

    pl.semaphore_wait(barrier, len(greet) + 2 * chip + (pp + pp_n - 1) // pp_n)

    def answer(peer, _):
        pl.semaphore_signal(here.at[chip], inc=1, device_id={"ctx": peer}, device_id_type=MESH)
        return 0

    lax.fori_loop(0, 2 * chip, answer, 0)

    rows_i = lax.broadcasted_iota(jnp.int32, (toks, toks), 0)
    cols_i = lax.broadcasted_iota(jnp.int32, (toks, toks), 1)
    causal = rows_i >= cols_i
    tri = causal.astype(F32)
    ld = ld_ref[...]
    cd = lax.dot_general(
        tri, ld, (NT, ((), ())), precision=lax.Precision.HIGHEST, preferred_element_type=F32
    )
    cdt = lax.dot_general(
        ld, tri, (NT, ((), ())), precision=lax.Precision.HIGHEST, preferred_element_type=F32
    )
    for h in range(heads):
        wide = jnp.broadcast_to(cd[:, h : h + 1], (toks, hd))
        total = wide[toks - 1 : toks, :]
        bt[h] = total
        grow[:, h * hd : (h + 1) * hd] = jnp.exp(wide)
        after[:, h * hd : (h + 1) * hd] = jnp.exp(total - wide)

    tail = halo_ref.shape[0]
    halo = remote(
        k_hbm.at[pl.ds(toks - tail, tail), :], halo_ref, halo_s, halo_r,
        {"ctx": lax.rem(ctx + 1, ctx_n)},
    )

    @pl.when(jnp.logical_and(core == 1, chip < chips - 1))
    def _():
        pl.semaphore_wait(here.at[chip + 1], 2)

    @pl.when(ctx < ctx_n - 1)
    def _():
        halo.start()

    swap_bt = remote(bt, bt_p, bp_s, bp_r, {"ctx": partner})
    swap_bt.start()
    for h in range(heads):
        wide = jnp.broadcast_to(cd[:, h : h + 1], (toks, hd))
        differ = wide - cdt[h : h + 1, :]
        mix[h] = jnp.where(causal, jnp.exp(jnp.where(causal, differ, 0.0)), 0.0)

    @pl.when(ctx == 0)
    def _():
        halo_ref[...] = jnp.zeros_like(halo_ref)

    @pl.when(ctx == ctx_n - 1)
    def _():
        ckg[pl.ds(toks, HALO), :] = jnp.zeros((HALO, feats), F32)

    @pl.when(pp == pp_n - 1)
    def _():
        gin_ref[...] = jnp.zeros_like(gin_ref)

    loads[0].wait()
    kext[pl.ds(HALO, toks), :] = k_ref[...].astype(F32)
    loads[1].wait()

    @pl.when(ctx > 0)
    def _():
        halo.wait_recv()

    kext[pl.ds(0, HALO), :] = halo_ref[pl.ds(tail - HALO, HALO), :].astype(F32)

    def sized(call):
        @pl.when(my_part < parts - 1)
        def _():
            call(rows)

        @pl.when(my_part == parts - 1)
        def _():
            call(short)

    if short < rows:
        @pl.when(my_part == parts - 1)
        def _():
            s_in[:, pl.ds(short, rows - short), :] = jnp.zeros((chips, rows - short, hd), BF16)
            b_in[:, pl.ds(short, rows - short), :] = jnp.zeros((chips, rows - short, hd), BF16)

    def swap(mine, theirs, send_sem, recv_sem, i):
        return remote(
            mine.at[their0 + i], theirs.at[i], send_sem.at[i], recv_sem.at[i], {"ctx": partner}
        )

    def spread(src, dst, send_sem, recv_sem, i, part):
        size = rows if part < parts - 1 else short
        return remote(
            src.at[i, pl.ds(part * rows, size)], dst.at[chip, pl.ds(0, size)],
            send_sem.at[i * parts + part], recv_sem.at[chip],
            {"ctx": (own0 + i) * parts + part},
        )

    def deliver(src, dst, send_sem, recv_sem, z, size):
        slot = ctx - scan_core * chips
        return remote(
            src.at[z, pl.ds(0, size)], dst.at[slot, pl.ds(0, size)], send_sem.at[z],
            recv_sem.at[slot], {"ctx": 2 * z + scan_core},
        )

    def arrive(dst, recv_sem, n, size):
        piece = dst.at[n, pl.ds(0, size)]
        return remote(piece, piece, recv_sem.at[n], recv_sem.at[n], {"ctx": partner})

    def factors(h, lead):
        e_m = jnp.exp(bt[h])
        e_t = jnp.exp(bt_p[h])
        return e_m, e_t, lead.astype(F32)

    def total_to(i, part):
        return remote(
            tot.at[i], bt_all.at[chip], bt_s.at[i * parts + part], bt_r.at[chip],
            {"ctx": (own0 + i) * parts + part},
        )

    def join(mine, theirs, xs, xr, out, into, send_sem, recv_sem, lead, needed, opening):
        def one(n, _):
            i = n
            h = own0 + i
            e_m, e_t, lf = factors(h, lead)
            swap(mine, theirs, xs, xr, i).wait_recv()
            ca = lf * e_t + (1.0 - lf)
            cb = lf + (1.0 - lf) * e_m
            out[i] = (ca * mine[h] + cb * theirs[i]).astype(BF16)
            if opening:
                tot[i] = bt[h] + bt_p[h]
                low = (h * parts + 1) // 2
                high = (h * parts + parts - 1) // 2
                meet(low)

                @pl.when(high > low)
                def _():
                    meet(high)

            for part in range(parts):
                @pl.when(h * parts + part != ctx)
                def _():
                    @pl.when(needed)
                    def _():
                        spread(out, into, send_sem, recv_sem, i, part).start()

                    if opening:
                        total_to(i, part).start()

                @pl.when(h * parts + part == ctx)
                def _():
                    size = rows if part < parts - 1 else short
                    into[chip, pl.ds(0, size), :] = out[i, pl.ds(part * rows, size), :]
                    if opening:
                        bt_all[chip] = tot[i]
            return 0

        lax.fori_loop(0, half, one, 0)

    def scan(into, recv_sem, out, home, send_sem, home_sem, opening):
        def give(z, carry):
            out[z] = carry.astype(BF16)
            if opening:
                late = jnp.where(z >= chips // 2, 1, 0)

                @pl.when(late != core)
                def _():
                    meet(z)

            @pl.when(2 * z + scan_core != ctx)
            def _():
                sized(lambda size: deliver(out, home, send_sem, home_sem, z, size).start())

            @pl.when(2 * z + scan_core == ctx)
            def _():
                home[ctx - scan_core * chips] = out[z]

        def total_in(z):
            @pl.when(2 * z + scan_core != ctx)
            def _():
                remote(
                    bt_all.at[z], bt_all.at[z], bt_r.at[z], bt_r.at[z], {"ctx": partner}
                ).wait_recv()

        if not opening:
            total_in(chips - 1)

        def one(n, carry):
            z = n if opening else chips - 1 - n
            give(z, carry)
            if opening:
                total_in(z)

            @pl.when(2 * z + scan_core != ctx)
            def _():
                sized(lambda size: arrive(into, recv_sem, z, size).wait_recv())

            return jnp.exp(bt_all[z]) * carry + into[z].astype(F32)

        carry = lax.fori_loop(0, chips - 1, one, jnp.zeros((rows, hd), F32))
        give(chips - 1 if opening else 0, carry)

    def hand(stage, dest, send_sem, recv_sem, i, h):
        return remote(
            stage.at[i], dest.at[h], send_sem.at[i], recv_sem.at[i], {"ctx": partner}
        )

    def split(home, home_sem, mine, theirs, dest, stage, hs_, hr_, lead):
        def one(n, _):
            i = n
            h = own0 + i
            e_m, e_t, lf = factors(h, lead)
            pieces = []
            for part in range(parts):
                size = rows if part < parts - 1 else short

                @pl.when(h * parts + part != ctx)
                def _():
                    arrive(home, home_sem, i * parts + part, size).wait_recv()

                pieces.append(home[i * parts + part, pl.ds(0, size), :].astype(F32))
            carry = jnp.concatenate(pieces, axis=0)
            c1 = lf + (1.0 - lf) * e_t
            c2 = lf * e_m + (1.0 - lf)
            stage[i] = (c2 * carry + lf * mine[h]).astype(BF16)
            hand(stage, dest, hs_, hr_, i, h).start()
            dest[h] = (c1 * carry + (1.0 - lf) * theirs[i]).astype(BF16)
            return 0

        lax.fori_loop(0, half, one, 0)

    def handed(stage, dest, hs_, hr_, g):
        @pl.when(g >= half_steps)
        def _():
            for j in range(group):
                h = own_first(g * group + j)
                hand(stage, dest, hs_, hr_, h - their0, h).wait_recv()

    def states(g, _):
        for j in range(group):
            h = own_last(g * group + j)
            hs = lanes(h)
            conv = w_ref[pl.ds(0, 1), hs] * kext[pl.ds(HALO, toks), hs]
            for tap in range(1, taps):
                conv = conv + w_ref[pl.ds(tap, 1), hs] * kext[pl.ds(HALO - tap, toks), hs]
            keys = conv.astype(BF16)
            kc[:, hs] = keys
            scaled = (keys.astype(F32) * after[:, hs]).astype(BF16)
            s_m[h] = dot(scaled, v_ref[:, hs], TN)

        @pl.when(g < half_steps)
        def _():
            for j in range(group):
                swap(s_m, s_t, sx_s, sx_r, own_last(g * group + j) - their0).start()

        return 0

    lax.fori_loop(0, steps, states, 0)
    swap_bt.wait_recv()
    join(s_m, s_t, sx_s, sx_r, s_out, s_in, s_s, s_r, core == 0, chip < chips - 1, True)
    loads[2].wait()

    def inside(g, _):
        for j in range(group):
            h = g * group + j
            hs = lanes(h)
            scores = dot(q_ref[:, hs], kc[:, hs], NT)
            w = (scores * mix[h]).astype(BF16)
            wts[h] = w
            att[:, hs] = dot(w, v_ref[:, hs], NN)
        return 0

    lax.fori_loop(0, steps, inside, 0)

    scan(s_in, s_r, p_out, p_in, p_s, p_r, True)
    split(p_in, p_r, s_m, s_t, p_half, p_stage, px_s, px_r, core == 0)

    loads[3].wait()
    acc_sq[...] = jnp.zeros_like(acc_sq)
    acc_dot[...] = jnp.zeros_like(acc_dot)

    def attend(g, _):
        handed(p_stage, p_half, px_s, px_r, g)
        for j in range(group):
            h = own_first(g * group + j)
            hs = lanes(h)
            a = att[:, hs] + grow[:, hs] * dot(q_ref[:, hs], p_half[h], NN)
            att[:, hs] = a
            acc_sq[...] += a * a
            acc_dot[...] += a * og_ref[:, hs].astype(F32)
        return 0

    lax.fori_loop(0, steps, attend, 0)

    sq_row = jnp.sum(acc_sq[...].T, axis=0, keepdims=True)
    dot_row = jnp.sum(acc_dot[...].T, axis=0, keepdims=True)
    first_row = lax.broadcasted_iota(jnp.int32, (8, toks), 0) == 0
    tpbuf[0] = jnp.where(first_row, sq_row, dot_row)

    def sums(step):
        return remote(
            tpbuf.at[0], tpbuf.at[step], tp_s.at[step - 1], tp_r.at[step - 1],
            {"tp": lax.rem(tp + step, tp_n)},
        )

    for step in range(1, tp_n):
        sums(step).start()
    for step in range(1, tp_n):
        sums(step).wait_recv()
    sums_all = tpbuf[0]
    for step in range(1, tp_n):
        sums_all = sums_all + tpbuf[step]
    inv_row = 1.0 / jnp.sqrt(sums_all[0:1, :] / width_all + 1e-06)
    shift_row = (sums_all[1:2, :] / width_all) * inv_row
    inv = jnp.broadcast_to(inv_row, (hd, toks)).T
    shift = jnp.broadcast_to(shift_row, (hd, toks)).T

    def adjoints(g, _):
        for j in range(group):
            h = own_last(g * group + j)
            hs = lanes(h)
            normed = att[:, hs] * inv
            out_ref[:, hs] = normed.astype(BF16)
            grad = ((og_ref[:, hs].astype(F32) - normed * shift) * inv).astype(BF16)
            ag[:, hs] = grad
            sq = (q_ref[:, hs].astype(F32) * grow[:, hs]).astype(BF16)
            b_m[h] = dot(sq, grad, TN)

        @pl.when(g < half_steps)
        def _():
            for j in range(group):
                swap(b_m, b_t, bx_s, bx_r, own_last(g * group + j) - their0).start()

        return 0

    lax.fori_loop(0, steps, adjoints, 0)
    join(b_m, b_t, bx_s, bx_r, b_out, b_in, b_s, b_r, core == 1, chip > 0, False)

    def inside_grads(g, _):
        for j in range(group):
            h = g * group + j
            hs = lanes(h)
            grad = ag[:, hs]
            sg = (dot(grad, v_ref[:, hs], NT) * mix[h]).astype(BF16)
            qg = dot(sg, kc[:, hs], NN) + grow[:, hs] * dot(grad, p_half[h], NT)
            acc[:, hs] = qg + dot(wts[h], grad, TN)
            ckg[pl.ds(0, toks), hs] = dot(sg, q_ref[:, hs], TN)
        return 0

    lax.fori_loop(0, steps, inside_grads, 0)
    scan(b_in, b_r, a_out, a_in, a_s, a_r, False)
    split(a_in, a_r, b_m, b_t, a_half, a_stage, ax_s, ax_r, core == 1)

    def edge(h):
        hs = lanes(h)
        return remote(
            ckg.at[pl.ds(0, HALO), hs], ckg.at[pl.ds(toks, HALO), hs], ch_s.at[h], ch_r.at[h],
            {"ctx": lax.rem(ctx + ctx_n - 1, ctx_n)},
        )

    def outside_grads(g, _):
        handed(a_stage, a_half, ax_s, ax_r, g)
        for j in range(group):
            h = own_first(g * group + j)
            hs = lanes(h)
            wa = after[:, hs]
            state = a_half[h]
            ckg[pl.ds(0, toks), hs] += wa * dot(v_ref[:, hs], state, NT)
            acc[:, hs] += wa * dot(kc[:, hs], state, NN)

        @pl.when(ctx > 0)
        def _():
            for j in range(group):
                edge(own_first(g * group + j)).start()

        return 0

    lax.fori_loop(0, steps, outside_grads, 0)

    def back(h):
        hs = lanes(h)
        return remote(
            gst.at[:, hs], gin_ref.at[:, hs], pp_s.at[h], pp_r.at[h],
            {"pp": lax.rem(pp + pp_n - 1, pp_n)},
        )

    def finish(g, _):
        @pl.when(ctx < ctx_n - 1)
        def _():
            for j in range(group):
                edge(own_first(g * group + j)).wait_recv()

        for j in range(group):
            h = own_first(g * group + j)
            hs = lanes(h)
            total = acc[:, hs]
            for tap in range(taps):
                total = total + w_ref[pl.ds(tap, 1), hs] * ckg[pl.ds(tap, toks), hs]
            gst[:, hs] = total.astype(BF16)

        @pl.when(pp > 0)
        def _():
            for j in range(group):
                back(own_first(g * group + j)).start()

        return 0

    lax.fori_loop(0, steps, finish, 0)

    @pl.when(ctx < ctx_n - 1)
    def _():
        halo.wait_send()

    for step in range(1, tp_n):
        sums(step).wait_send()

    swap_bt.wait_send()

    def left(i, _):
        h = own0 + i
        swap(s_m, s_t, sx_s, sx_r, i).wait_send()
        swap(b_m, b_t, bx_s, bx_r, i).wait_send()
        hand(p_stage, p_half, px_s, px_r, i, h).wait_send()
        hand(a_stage, a_half, ax_s, ax_r, i, h).wait_send()
        for part in range(parts):
            @pl.when(h * parts + part != ctx)
            def _():
                total_to(i, part).wait_send()

                @pl.when(chip < chips - 1)
                def _():
                    spread(s_out, s_in, s_s, s_r, i, part).wait_send()

                @pl.when(chip > 0)
                def _():
                    spread(b_out, b_in, b_s, b_r, i, part).wait_send()

        return 0

    lax.fori_loop(0, half, left, 0)

    def given(z, _):
        @pl.when(2 * z + scan_core != ctx)
        def _():
            sized(lambda size: deliver(p_out, p_in, p_s, p_r, z, size).wait_send())
            sized(lambda size: deliver(a_out, a_in, a_s, a_r, z, size).wait_send())

        return 0

    lax.fori_loop(0, chips, given, 0)

    @pl.when(ctx > 0)
    def _():
        def leave(h, _):
            edge(h).wait_send()
            return 0

        lax.fori_loop(0, heads, leave, 0)

    @pl.when(pp > 0)
    def _():
        def leave(h, _):
            back(h).wait_send()
            return 0

        lax.fori_loop(0, heads, leave, 0)

    @pl.when(pp < pp_n - 1)
    def _():
        def land(h, _):
            back(h).wait_recv()
            return 0

        lax.fori_loop(0, heads, land, 0)


def solution(mesh):
    ctx_n, tp_n, pp_n = mesh.shape["ctx"], mesh.shape["tp"], mesh.shape["pp"]

    def per_device(queries, key_input, values, log_decay, conv_weight, out_grad):
        toks, feats = queries.shape[1:]
        heads = log_decay.shape[2]
        hd = feats // heads
        parts = ctx_n // heads
        rows = -(-hd // (16 * parts)) * 16
        dma = pltpu.SemaphoreType.DMA
        flat_b = pltpu.VMEM((toks, feats), BF16)
        flat_f = pltpu.VMEM((toks, feats), F32)
        half = heads // 2
        chips = ctx_n // 2
        full_f = pltpu.VMEM((heads, hd, hd), F32)
        full_b = pltpu.VMEM((heads, hd, hd), BF16)
        half_f = pltpu.VMEM((half, hd, hd), F32)
        half_b = pltpu.VMEM((half, hd, hd), BF16)
        shares = pltpu.VMEM((chips, rows, hd), BF16)
        totals = pltpu.VMEM((heads, 1, hd), F32)
        scanned = [full_f, half_f, half_b, shares, shares, shares, full_b, half_b]
        longer = pltpu.VMEM((toks + HALO, feats), F32)
        square = pltpu.VMEM((toks, hd), F32)
        scratch = [
            flat_b, flat_b, flat_b, flat_b, pltpu.VMEM((16, feats), BF16), longer, flat_b,
            flat_f, flat_f, pltpu.VMEM((heads, toks, toks), F32),
            pltpu.VMEM((heads, toks, toks), BF16), flat_f, flat_b, flat_f, longer, flat_b,
            totals, totals, pltpu.VMEM((half, 1, hd), F32), pltpu.VMEM((chips, 1, hd), F32),
            square, square,
            pltpu.VMEM((tp_n, 8, toks), F32),
        ]
        scratch += scanned + scanned
        scratch += [pltpu.SemaphoreType.REGULAR((chips,))]
        scratch += [dma((4,)), dma, dma, dma, dma, dma((chips,)), dma((chips,))]
        scratch += [dma((max(tp_n - 1, 1),))] * 2 + [dma((chips,))] * 8 + [dma((half,))] * 8
        scratch += [dma((heads,))] * 4
        whole = pl.BlockSpec(memory_space=pltpu.VMEM)
        there = pl.BlockSpec(memory_space=pl.ANY)

        def body(*refs):
            kernel(ctx_n, tp_n, pp_n, *refs)

        shape = jax.ShapeDtypeStruct((toks, feats), BF16)
        out, gin = pl.pallas_call(
            body,
            out_shape=(shape, shape),
            in_specs=[there, there, there, whole, whole, there],
            out_specs=(whole, whole),
            scratch_shapes=scratch,
            compiler_params=pltpu.CompilerParams(
                collective_id=0, has_side_effects=True, vmem_limit_bytes=63 * 1024 * 1024
            ),
        )(
            queries[0], key_input[0], values[0], log_decay[0].T, conv_weight[0], out_grad[0]
        )
        return out[None], gin[None]

    placed = (
        P("pp", "ctx", "tp"),
        P("pp", "ctx", "tp"),
        P("pp", "ctx", "tp"),
        P("pp", "ctx", "tp"),
        P("pp", None, "tp"),
        P("pp", "ctx", "tp"),
    )
    return jax.shard_map(
        per_device,
        mesh=mesh,
        in_specs=placed,
        out_specs=(P("pp", "ctx", "tp"), P("pp", "ctx", "tp")),
        check_vma=False,
    )
```

```python
import jax
import jax.numpy as jnp
from jax import lax
from jax.experimental import pallas as pl
from jax.experimental.pallas import tpu as pltpu
from jax.sharding import PartitionSpec as P

MESH = pl.DeviceIdType.MESH
F32 = jnp.float32
BF16 = jnp.bfloat16
HALO = 8
LAST = 16
GROUP = 2


def remote(src, dst, send_sem, recv_sem, where):
    return pltpu.make_async_remote_copy(
        src_ref=src,
        dst_ref=dst,
        send_sem=send_sem,
        recv_sem=recv_sem,
        device_id=where,
        device_id_type=MESH,
    )


def dot(a, b, dims):
    return lax.dot_general(a, b, (dims, ((), ())), preferred_element_type=F32)


NN = ((1,), (0,))
NT = ((1,), (1,))
TN = ((0,), (0,))


def kernel(
    ctx_n, tp_n, pp_n,
    q_hbm, k_hbm, v_hbm, ld_ref, w_ref, og_hbm,
    out_ref, gin_ref,
    q_ref, k_ref, v_ref, og_ref, halo_ref, kext, kc, grow, after, mix, wts, att, ag, acc, ckg, gst, sq,
    bt, bt_p, tot, bt_all, acc_sq, acc_dot, tpbuf,
    s_m, s_t, s_out, s_in, p_out, p_in, p_half, p_stage,
    b_m, b_t, b_out, b_in, a_out, a_in, a_half, a_stage,
    here, load_sem, halo_s, halo_r, bp_s, bp_r, bt_s, bt_r, tp_s, tp_r,
    s_s, s_r, p_s, p_r, b_s, b_r, a_s, a_r,
    sx_s, sx_r, px_s, px_r, bx_s, bx_r, ax_s, ax_r, ch_s, ch_r, pp_s, pp_r, pl_s, pl_r,
):
    toks, feats = q_hbm.shape
    heads = ld_ref.shape[0]
    hd = feats // heads
    taps = w_ref.shape[0]
    width_all = feats * tp_n
    parts = ctx_n // heads
    rows = s_in.shape[1]
    short = hd - rows * (parts - 1)
    group = min(GROUP, heads // 2)
    steps = heads // group
    half = heads // 2
    half_steps = half // group
    chips = ctx_n // 2
    ctx = lax.axis_index("ctx")
    tp = lax.axis_index("tp")
    pp = lax.axis_index("pp")
    core = lax.rem(ctx, 2)
    chip = ctx // 2
    partner = ctx + 1 - 2 * core
    own0 = half * core
    their0 = half * (1 - core)
    my_head = ctx // parts
    my_part = lax.rem(ctx, parts)
    scan_core = my_head // half

    def lanes(h):
        return pl.ds(pl.multiple_of(h * hd, hd), hd)

    def own_first(idx):
        return lax.rem(own0 + idx, heads)

    def own_last(idx):
        return lax.rem(their0 + idx, heads)

    barrier = pltpu.get_barrier_semaphore()
    greet = [{"ctx": partner}]
    greet += [{"tp": lax.rem(tp + step, tp_n)} for step in range(1, tp_n)]
    for where in greet:
        pl.semaphore_signal(barrier, inc=1, device_id=where, device_id_type=MESH)

    @pl.when(pp < pp_n - 1)
    def _():
        pl.semaphore_signal(
            barrier, inc=1, device_id={"pp": lax.rem(pp + 1, pp_n)}, device_id_type=MESH
        )

    def enter(peer, _):
        pl.semaphore_signal(barrier, inc=1, device_id={"ctx": peer}, device_id_type=MESH)
        return 0

    lax.fori_loop(2 * chip + 2, ctx_n, enter, 0)

    def meet(z):
        @pl.when(jnp.logical_and(z > chip, z != chip + core))
        def _():
            pl.semaphore_wait(here.at[z], 2)

    loads = [
        pltpu.make_async_copy(src, dst, load_sem.at[n])
        for n, (src, dst) in enumerate(
            ((k_hbm, k_ref), (v_hbm, v_ref), (q_hbm, q_ref), (og_hbm, og_ref))
        )
    ]
    for load in loads:
        load.start()

    pl.semaphore_wait(barrier, len(greet) + 2 * chip + (pp + pp_n - 1) // pp_n)

    def answer(peer, _):
        pl.semaphore_signal(here.at[chip], inc=1, device_id={"ctx": peer}, device_id_type=MESH)
        return 0

    lax.fori_loop(0, 2 * chip, answer, 0)

    rows_i = lax.broadcasted_iota(jnp.int32, (toks, toks), 0)
    cols_i = lax.broadcasted_iota(jnp.int32, (toks, toks), 1)
    causal = rows_i >= cols_i
    tri = causal.astype(F32)
    ld = ld_ref[...]
    cd = lax.dot_general(
        tri, ld, (NT, ((), ())), precision=lax.Precision.HIGHEST, preferred_element_type=F32
    )
    cdt = lax.dot_general(
        ld, tri, (NT, ((), ())), precision=lax.Precision.HIGHEST, preferred_element_type=F32
    )
    for h in range(heads):
        wide = jnp.broadcast_to(cd[:, h : h + 1], (toks, hd))
        total = wide[toks - 1 : toks, :]
        bt[h] = total
        grow[:, h * hd : (h + 1) * hd] = jnp.exp(wide)
        after[:, h * hd : (h + 1) * hd] = jnp.exp(total - wide)

    tail = halo_ref.shape[0]
    halo = remote(
        k_hbm.at[pl.ds(toks - tail, tail), :], halo_ref, halo_s, halo_r,
        {"ctx": lax.rem(ctx + 1, ctx_n)},
    )

    @pl.when(jnp.logical_and(core == 1, chip < chips - 1))
    def _():
        pl.semaphore_wait(here.at[chip + 1], 2)

    @pl.when(ctx < ctx_n - 1)
    def _():
        halo.start()

    swap_bt = remote(bt, bt_p, bp_s, bp_r, {"ctx": partner})
    swap_bt.start()
    for h in range(heads):
        wide = jnp.broadcast_to(cd[:, h : h + 1], (toks, hd))
        differ = wide - cdt[h : h + 1, :]
        mix[h] = jnp.where(causal, jnp.exp(jnp.where(causal, differ, 0.0)), 0.0)

    @pl.when(ctx == 0)
    def _():
        halo_ref[...] = jnp.zeros_like(halo_ref)

    @pl.when(ctx == ctx_n - 1)
    def _():
        ckg[pl.ds(toks, HALO), :] = jnp.zeros((HALO, feats), F32)

    @pl.when(pp == pp_n - 1)
    def _():
        gin_ref[...] = jnp.zeros_like(gin_ref)

    loads[0].wait()
    kext[pl.ds(HALO, toks), :] = k_ref[...].astype(F32)
    loads[1].wait()

    @pl.when(ctx > 0)
    def _():
        halo.wait_recv()

    kext[pl.ds(0, HALO), :] = halo_ref[pl.ds(tail - HALO, HALO), :].astype(F32)

    def sized(call):
        @pl.when(my_part < parts - 1)
        def _():
            call(rows)

        @pl.when(my_part == parts - 1)
        def _():
            call(short)

    if short < rows:
        @pl.when(my_part == parts - 1)
        def _():
            s_in[:, pl.ds(short, rows - short), :] = jnp.zeros((chips, rows - short, hd), BF16)
            b_in[:, pl.ds(short, rows - short), :] = jnp.zeros((chips, rows - short, hd), BF16)

    def swap(mine, theirs, send_sem, recv_sem, i):
        return remote(
            mine.at[their0 + i], theirs.at[i], send_sem.at[i], recv_sem.at[i], {"ctx": partner}
        )

    def spread(src, dst, send_sem, recv_sem, i, part):
        size = rows if part < parts - 1 else short
        return remote(
            src.at[i, pl.ds(part * rows, size)], dst.at[chip, pl.ds(0, size)],
            send_sem.at[i * parts + part], recv_sem.at[chip],
            {"ctx": (own0 + i) * parts + part},
        )

    def deliver(src, dst, send_sem, recv_sem, z, size):
        slot = ctx - scan_core * chips
        return remote(
            src.at[z, pl.ds(0, size)], dst.at[slot, pl.ds(0, size)], send_sem.at[z],
            recv_sem.at[slot], {"ctx": 2 * z + scan_core},
        )

    def arrive(dst, recv_sem, n, size):
        piece = dst.at[n, pl.ds(0, size)]
        return remote(piece, piece, recv_sem.at[n], recv_sem.at[n], {"ctx": partner})

    def factors(h, lead):
        e_m = jnp.exp(bt[h])
        e_t = jnp.exp(bt_p[h])
        return e_m, e_t, lead.astype(F32)

    def total_to(i, part):
        return remote(
            tot.at[i], bt_all.at[chip], bt_s.at[i * parts + part], bt_r.at[chip],
            {"ctx": (own0 + i) * parts + part},
        )

    def join(mine, theirs, xs, xr, out, into, send_sem, recv_sem, lead, needed, opening):
        def one(n, _):
            i = n
            h = own0 + i
            e_m, e_t, lf = factors(h, lead)
            swap(mine, theirs, xs, xr, i).wait_recv()
            ca = lf * e_t + (1.0 - lf)
            cb = lf + (1.0 - lf) * e_m
            out[i] = (ca * mine[h] + cb * theirs[i]).astype(BF16)
            if opening:
                tot[i] = bt[h] + bt_p[h]
                low = (h * parts + 1) // 2
                high = (h * parts + parts - 1) // 2
                meet(low)

                @pl.when(high > low)
                def _():
                    meet(high)

            for part in range(parts):
                @pl.when(h * parts + part != ctx)
                def _():
                    @pl.when(needed)
                    def _():
                        spread(out, into, send_sem, recv_sem, i, part).start()

                    if opening:
                        total_to(i, part).start()

                @pl.when(h * parts + part == ctx)
                def _():
                    size = rows if part < parts - 1 else short
                    into[chip, pl.ds(0, size), :] = out[i, pl.ds(part * rows, size), :]
                    if opening:
                        bt_all[chip] = tot[i]
            return 0

        lax.fori_loop(0, half, one, 0)

    def scan(into, recv_sem, out, home, send_sem, home_sem, opening):
        def give(z, carry):
            out[z] = carry.astype(BF16)
            if opening:
                late = jnp.where(z >= chips // 2, 1, 0)

                @pl.when(late != core)
                def _():
                    meet(z)

            @pl.when(2 * z + scan_core != ctx)
            def _():
                sized(lambda size: deliver(out, home, send_sem, home_sem, z, size).start())

            @pl.when(2 * z + scan_core == ctx)
            def _():
                home[ctx - scan_core * chips] = out[z]

        def total_in(z):
            @pl.when(2 * z + scan_core != ctx)
            def _():
                remote(
                    bt_all.at[z], bt_all.at[z], bt_r.at[z], bt_r.at[z], {"ctx": partner}
                ).wait_recv()

        if not opening:
            total_in(chips - 1)

        def one(n, carry):
            z = n if opening else chips - 1 - n
            give(z, carry)
            if opening:
                total_in(z)

            @pl.when(2 * z + scan_core != ctx)
            def _():
                sized(lambda size: arrive(into, recv_sem, z, size).wait_recv())

            return jnp.exp(bt_all[z]) * carry + into[z].astype(F32)

        carry = lax.fori_loop(0, chips - 1, one, jnp.zeros((rows, hd), F32))
        give(chips - 1 if opening else 0, carry)

    def hand(stage, dest, send_sem, recv_sem, i, h):
        return remote(
            stage.at[i], dest.at[h], send_sem.at[i], recv_sem.at[i], {"ctx": partner}
        )

    def split(home, home_sem, mine, theirs, dest, stage, hs_, hr_, lead):
        def one(n, _):
            i = n
            h = own0 + i
            e_m, e_t, lf = factors(h, lead)
            pieces = []
            for part in range(parts):
                size = rows if part < parts - 1 else short

                @pl.when(h * parts + part != ctx)
                def _():
                    arrive(home, home_sem, i * parts + part, size).wait_recv()

                pieces.append(home[i * parts + part, pl.ds(0, size), :].astype(F32))
            carry = jnp.concatenate(pieces, axis=0)
            c1 = lf + (1.0 - lf) * e_t
            c2 = lf * e_m + (1.0 - lf)
            stage[i] = (c2 * carry + lf * mine[h]).astype(BF16)
            hand(stage, dest, hs_, hr_, i, h).start()
            dest[h] = (c1 * carry + (1.0 - lf) * theirs[i]).astype(BF16)
            return 0

        lax.fori_loop(0, half, one, 0)

    def handed(stage, dest, hs_, hr_, g):
        @pl.when(g >= half_steps)
        def _():
            for j in range(group):
                h = own_first(g * group + j)
                hand(stage, dest, hs_, hr_, h - their0, h).wait_recv()

    def states(g, _):
        for j in range(group):
            h = own_last(g * group + j)
            hs = lanes(h)
            conv = w_ref[pl.ds(0, 1), hs] * kext[pl.ds(HALO, toks), hs]
            for tap in range(1, taps):
                conv = conv + w_ref[pl.ds(tap, 1), hs] * kext[pl.ds(HALO - tap, toks), hs]
            keys = conv.astype(BF16)
            kc[:, hs] = keys
            scaled = (keys.astype(F32) * after[:, hs]).astype(BF16)
            s_m[h] = dot(scaled, v_ref[:, hs], TN)

        @pl.when(g < half_steps)
        def _():
            for j in range(group):
                swap(s_m, s_t, sx_s, sx_r, own_last(g * group + j) - their0).start()

        return 0

    lax.fori_loop(0, steps, states, 0)
    swap_bt.wait_recv()
    join(s_m, s_t, sx_s, sx_r, s_out, s_in, s_s, s_r, core == 0, chip < chips - 1, True)
    loads[2].wait()

    def inside(g, _):
        for j in range(group):
            h = g * group + j
            hs = lanes(h)
            scores = dot(q_ref[:, hs], kc[:, hs], NT)
            w = (scores * mix[h]).astype(BF16)
            wts[h] = w
            att[:, hs] = dot(w, v_ref[:, hs], NN)
            sq[:, hs] = (q_ref[:, hs].astype(F32) * grow[:, hs]).astype(BF16)
        return 0

    lax.fori_loop(0, steps, inside, 0)

    scan(s_in, s_r, p_out, p_in, p_s, p_r, True)
    split(p_in, p_r, s_m, s_t, p_half, p_stage, px_s, px_r, core == 0)

    loads[3].wait()
    acc_sq[...] = jnp.zeros_like(acc_sq)
    acc_dot[...] = jnp.zeros_like(acc_dot)

    def attend(g, _):
        handed(p_stage, p_half, px_s, px_r, g)
        for j in range(group):
            h = own_first(g * group + j)
            hs = lanes(h)
            a = att[:, hs] + grow[:, hs] * dot(q_ref[:, hs], p_half[h], NN)
            att[:, hs] = a
            acc_sq[...] += a * a
            acc_dot[...] += a * og_ref[:, hs].astype(F32)
        return 0

    lax.fori_loop(0, steps, attend, 0)

    sq_row = jnp.sum(acc_sq[...].T, axis=0, keepdims=True)
    dot_row = jnp.sum(acc_dot[...].T, axis=0, keepdims=True)
    first_row = lax.broadcasted_iota(jnp.int32, (8, toks), 0) == 0
    tpbuf[0] = jnp.where(first_row, sq_row, dot_row)

    def sums(step):
        return remote(
            tpbuf.at[0], tpbuf.at[step], tp_s.at[step - 1], tp_r.at[step - 1],
            {"tp": lax.rem(tp + step, tp_n)},
        )

    for step in range(1, tp_n):
        sums(step).start()
    for step in range(1, tp_n):
        sums(step).wait_recv()
    sums_all = tpbuf[0]
    for step in range(1, tp_n):
        sums_all = sums_all + tpbuf[step]
    inv_row = 1.0 / jnp.sqrt(sums_all[0:1, :] / width_all + 1e-06)
    shift_row = (sums_all[1:2, :] / width_all) * inv_row
    inv = jnp.broadcast_to(inv_row, (hd, toks)).T
    shift = jnp.broadcast_to(shift_row, (hd, toks)).T

    def adjoints(g, _):
        for j in range(group):
            h = own_last(g * group + j)
            hs = lanes(h)
            normed = att[:, hs] * inv
            grad = ((og_ref[:, hs].astype(F32) - normed * shift) * inv).astype(BF16)
            ag[:, hs] = grad
            b_m[h] = dot(sq[:, hs], grad, TN)

        @pl.when(g < half_steps)
        def _():
            for j in range(group):
                swap(b_m, b_t, bx_s, bx_r, own_last(g * group + j) - their0).start()

        return 0

    lax.fori_loop(0, steps, adjoints, 0)
    join(b_m, b_t, bx_s, bx_r, b_out, b_in, b_s, b_r, core == 1, chip > 0, False)

    def inside_grads(g, _):
        for j in range(group):
            h = g * group + j
            hs = lanes(h)
            grad = ag[:, hs]
            out_ref[:, hs] = (att[:, hs] * inv).astype(BF16)
            sg = (dot(grad, v_ref[:, hs], NT) * mix[h]).astype(BF16)
            qg = dot(sg, kc[:, hs], NN) + grow[:, hs] * dot(grad, p_half[h], NT)
            acc[:, hs] = qg + dot(wts[h], grad, TN)
            ckg[pl.ds(0, toks), hs] = dot(sg, q_ref[:, hs], TN)
        return 0

    lax.fori_loop(0, steps, inside_grads, 0)
    scan(b_in, b_r, a_out, a_in, a_s, a_r, False)
    split(a_in, a_r, b_m, b_t, a_half, a_stage, ax_s, ax_r, core == 1)

    def edge(h):
        hs = lanes(h)
        return remote(
            ckg.at[pl.ds(0, HALO), hs], ckg.at[pl.ds(toks, HALO), hs], ch_s.at[h], ch_r.at[h],
            {"ctx": lax.rem(ctx + ctx_n - 1, ctx_n)},
        )

    most = toks - LAST

    def summed(h, first, size):
        hs = lanes(h)
        total = acc[pl.ds(first, size), hs]
        for tap in range(taps):
            total = total + w_ref[pl.ds(tap, 1), hs] * ckg[pl.ds(first + tap, size), hs]
        gst[pl.ds(first, size), hs] = total.astype(BF16)

    def back(h):
        piece = (pl.ds(0, most), lanes(h))
        return remote(
            gst.at[piece], gin_ref.at[piece], pp_s.at[h], pp_r.at[h],
            {"pp": lax.rem(pp + pp_n - 1, pp_n)},
        )

    back_last = remote(
        gst.at[pl.ds(most, LAST), :], gin_ref.at[pl.ds(most, LAST), :], pl_s, pl_r,
        {"pp": lax.rem(pp + pp_n - 1, pp_n)},
    )

    def outside_grads(g, _):
        handed(a_stage, a_half, ax_s, ax_r, g)
        for j in range(group):
            h = own_first(g * group + j)
            hs = lanes(h)
            wa = after[:, hs]
            state = a_half[h]
            ckg[pl.ds(0, toks), hs] += wa * dot(v_ref[:, hs], state, NT)
            acc[:, hs] += wa * dot(kc[:, hs], state, NN)

        @pl.when(ctx > 0)
        def _():
            for j in range(group):
                edge(own_first(g * group + j)).start()

        for j in range(group):
            summed(own_first(g * group + j), 0, most)

        @pl.when(pp > 0)
        def _():
            for j in range(group):
                back(own_first(g * group + j)).start()

        return 0

    lax.fori_loop(0, steps, outside_grads, 0)

    def finish(g, _):
        @pl.when(ctx < ctx_n - 1)
        def _():
            for j in range(group):
                edge(own_last(g * group + j)).wait_recv()

        for j in range(group):
            summed(own_last(g * group + j), most, LAST)
        return 0

    lax.fori_loop(0, steps, finish, 0)

    @pl.when(pp > 0)
    def _():
        back_last.start()

    @pl.when(ctx < ctx_n - 1)
    def _():
        halo.wait_send()

    for step in range(1, tp_n):
        sums(step).wait_send()

    swap_bt.wait_send()

    def left(i, _):
        h = own0 + i
        swap(s_m, s_t, sx_s, sx_r, i).wait_send()
        swap(b_m, b_t, bx_s, bx_r, i).wait_send()
        hand(p_stage, p_half, px_s, px_r, i, h).wait_send()
        hand(a_stage, a_half, ax_s, ax_r, i, h).wait_send()
        for part in range(parts):
            @pl.when(h * parts + part != ctx)
            def _():
                total_to(i, part).wait_send()

                @pl.when(chip < chips - 1)
                def _():
                    spread(s_out, s_in, s_s, s_r, i, part).wait_send()

                @pl.when(chip > 0)
                def _():
                    spread(b_out, b_in, b_s, b_r, i, part).wait_send()

        return 0

    lax.fori_loop(0, half, left, 0)

    def given(z, _):
        @pl.when(2 * z + scan_core != ctx)
        def _():
            sized(lambda size: deliver(p_out, p_in, p_s, p_r, z, size).wait_send())
            sized(lambda size: deliver(a_out, a_in, a_s, a_r, z, size).wait_send())

        return 0

    lax.fori_loop(0, chips, given, 0)

    @pl.when(ctx > 0)
    def _():
        def leave(h, _):
            edge(h).wait_send()
            return 0

        lax.fori_loop(0, heads, leave, 0)

    @pl.when(pp > 0)
    def _():
        def leave(h, _):
            back(h).wait_send()
            return 0

        lax.fori_loop(0, heads, leave, 0)
        back_last.wait_send()

    @pl.when(pp < pp_n - 1)
    def _():
        def land(h, _):
            back(h).wait_recv()
            return 0

        lax.fori_loop(0, heads, land, 0)
        back_last.wait_recv()


def place(a_ref, b_ref, c_ref, d_ref, buf, sem_in, sem_out):
    step = a_ref.shape[0] // 4
    pieces = []
    for n, (src, dst) in enumerate(((a_ref, c_ref), (b_ref, d_ref))):
        for p in range(4):
            rows = pl.ds(p * step, step)
            held = buf.at[n, rows]
            pieces.append((
                pltpu.make_async_copy(src.at[rows], held, sem_in.at[n, p]),
                pltpu.make_async_copy(held, dst.at[rows], sem_out.at[n, p]),
            ))
    for get, _ in pieces:
        get.start()
    for get, put in pieces:
        get.wait()
        put.start()
    for _, put in pieces:
        put.wait()


def solution(mesh):
    ctx_n, tp_n, pp_n = mesh.shape["ctx"], mesh.shape["tp"], mesh.shape["pp"]

    def per_device(queries, key_input, values, log_decay, conv_weight, out_grad):
        toks, feats = queries.shape[1:]
        heads = log_decay.shape[2]
        hd = feats // heads
        parts = ctx_n // heads
        rows = -(-hd // (16 * parts)) * 16
        dma = pltpu.SemaphoreType.DMA
        flat_b = pltpu.VMEM((toks, feats), BF16)
        flat_f = pltpu.VMEM((toks, feats), F32)
        half = heads // 2
        chips = ctx_n // 2
        full_f = pltpu.VMEM((heads, hd, hd), F32)
        full_b = pltpu.VMEM((heads, hd, hd), BF16)
        half_f = pltpu.VMEM((half, hd, hd), F32)
        half_b = pltpu.VMEM((half, hd, hd), BF16)
        shares = pltpu.VMEM((chips, rows, hd), BF16)
        totals = pltpu.VMEM((heads, 1, hd), F32)
        scanned = [full_f, half_f, half_b, shares, shares, shares, full_b, half_b]
        longer = pltpu.VMEM((toks + HALO, feats), F32)
        square = pltpu.VMEM((toks, hd), F32)
        scratch = [
            flat_b, flat_b, flat_b, flat_b, pltpu.VMEM((16, feats), BF16), longer, flat_b,
            flat_f, flat_f, pltpu.VMEM((heads, toks, toks), F32),
            pltpu.VMEM((heads, toks, toks), BF16), flat_f, flat_b, flat_f, longer, flat_b, flat_b,
            totals, totals, pltpu.VMEM((half, 1, hd), F32), pltpu.VMEM((chips, 1, hd), F32),
            square, square,
            pltpu.VMEM((tp_n, 8, toks), F32),
        ]
        scratch += scanned + scanned
        scratch += [pltpu.SemaphoreType.REGULAR((chips,))]
        scratch += [dma((4,)), dma, dma, dma, dma, dma((chips,)), dma((chips,))]
        scratch += [dma((max(tp_n - 1, 1),))] * 2 + [dma((chips,))] * 8 + [dma((half,))] * 8
        scratch += [dma((heads,))] * 4 + [dma, dma]
        whole = pl.BlockSpec(memory_space=pltpu.VMEM)
        there = pl.BlockSpec(memory_space=pl.ANY)

        def body(*refs):
            kernel(ctx_n, tp_n, pp_n, *refs)

        shape = jax.ShapeDtypeStruct((toks, feats), BF16)
        out, gin = pl.pallas_call(
            body,
            out_shape=(shape, shape),
            in_specs=[there, there, there, whole, whole, there],
            out_specs=(whole, whole),
            scratch_shapes=scratch,
            compiler_params=pltpu.CompilerParams(
                collective_id=0, has_side_effects=True, vmem_limit_bytes=63 * 1024 * 1024
            ),
        )(
            queries[0], key_input[0], values[0], log_decay[0].T, conv_weight[0], out_grad[0]
        )
        out, gin = pl.pallas_call(
            place,
            out_shape=(shape, shape),
            in_specs=[there, there],
            out_specs=(there, there),
            scratch_shapes=[
                pltpu.VMEM((2, toks, feats), BF16), dma((2, 4)), dma((2, 4)),
            ],
        )(out, gin)
        return out[None], gin[None]

    placed = (
        P("pp", "ctx", "tp"),
        P("pp", "ctx", "tp"),
        P("pp", "ctx", "tp"),
        P("pp", "ctx", "tp"),
        P("pp", None, "tp"),
        P("pp", "ctx", "tp"),
    )
    return jax.shard_map(
        per_device,
        mesh=mesh,
        in_specs=placed,
        out_specs=(P("pp", "ctx", "tp"), P("pp", "ctx", "tp")),
        check_vma=False,
    )
```

```python
import jax
import jax.numpy as jnp
from jax import lax
from jax.experimental import pallas as pl
from jax.experimental.pallas import tpu as pltpu
from jax.sharding import PartitionSpec as P

MESH = pl.DeviceIdType.MESH
F32 = jnp.float32
BF16 = jnp.bfloat16
HALO = 8
LAST = 16
GROUP = 2


def remote(src, dst, send_sem, recv_sem, where):
    return pltpu.make_async_remote_copy(
        src_ref=src,
        dst_ref=dst,
        send_sem=send_sem,
        recv_sem=recv_sem,
        device_id=where,
        device_id_type=MESH,
    )


def dot(a, b, dims):
    return lax.dot_general(a, b, (dims, ((), ())), preferred_element_type=F32)


NN = ((1,), (0,))
NT = ((1,), (1,))
TN = ((0,), (0,))


def kernel(
    ctx_n, tp_n, pp_n,
    q_hbm, k_hbm, v_hbm, ld_hbm, w_hbm, og_hbm,
    out_ref, gin_ref,
    ld_ref, w_ref, q_ref, k_ref, v_ref, og_ref, halo_ref, kext, kc, grow, after, mix, wts, att, ag, acc, ckg, gst, sq,
    bt, bt_p, tot, bt_all, acc_sq, acc_dot, tpbuf,
    s_m, s_t, s_out, s_in, p_out, p_in, p_half, p_stage,
    b_m, b_t, b_out, b_in, a_out, a_in, a_half, a_stage,
    here, load_sem, halo_s, halo_r, bp_s, bp_r, bt_s, bt_r, tp_s, tp_r,
    s_s, s_r, p_s, p_r, b_s, b_r, a_s, a_r,
    sx_s, sx_r, px_s, px_r, bx_s, bx_r, ax_s, ax_r, ch_s, ch_r, pp_s, pp_r, pl_s, pl_r,
):
    toks, feats = q_hbm.shape
    heads = ld_hbm.shape[0]
    hd = feats // heads
    taps = w_hbm.shape[0]
    width_all = feats * tp_n
    parts = ctx_n // heads
    rows = s_in.shape[1]
    short = hd - rows * (parts - 1)
    group = min(GROUP, heads // 2)
    steps = heads // group
    half = heads // 2
    half_steps = half // group
    chips = ctx_n // 2
    ctx = lax.axis_index("ctx")
    tp = lax.axis_index("tp")
    pp = lax.axis_index("pp")
    core = lax.rem(ctx, 2)
    chip = ctx // 2
    partner = ctx + 1 - 2 * core
    own0 = half * core
    their0 = half * (1 - core)
    my_head = ctx // parts
    my_part = lax.rem(ctx, parts)
    scan_core = my_head // half

    def lanes(h):
        return pl.ds(pl.multiple_of(h * hd, hd), hd)

    def own_first(idx):
        return lax.rem(own0 + idx, heads)

    def own_last(idx):
        return lax.rem(their0 + idx, heads)

    barrier = pltpu.get_barrier_semaphore()
    greet = [{"ctx": partner}]
    greet += [{"tp": lax.rem(tp + step, tp_n)} for step in range(1, tp_n)]
    for where in greet:
        pl.semaphore_signal(barrier, inc=1, device_id=where, device_id_type=MESH)

    @pl.when(pp < pp_n - 1)
    def _():
        pl.semaphore_signal(
            barrier, inc=1, device_id={"pp": lax.rem(pp + 1, pp_n)}, device_id_type=MESH
        )

    def enter(peer, _):
        pl.semaphore_signal(barrier, inc=1, device_id={"ctx": peer}, device_id_type=MESH)
        return 0

    lax.fori_loop(2 * chip + 2, ctx_n, enter, 0)

    def meet(z):
        @pl.when(jnp.logical_and(z > chip, z != chip + core))
        def _():
            pl.semaphore_wait(here.at[z], 2)

    loads = [
        pltpu.make_async_copy(src, dst, load_sem.at[n])
        for n, (src, dst) in enumerate(
            (
                (k_hbm, k_ref), (v_hbm, v_ref), (q_hbm, q_ref), (og_hbm, og_ref),
                (ld_hbm, ld_ref), (w_hbm, w_ref),
            )
        )
    ]
    for n in (4, 0, 5, 1, 2, 3):
        loads[n].start()

    pl.semaphore_wait(barrier, len(greet) + 2 * chip + (pp + pp_n - 1) // pp_n)

    def answer(peer, _):
        pl.semaphore_signal(here.at[chip], inc=1, device_id={"ctx": peer}, device_id_type=MESH)
        return 0

    lax.fori_loop(0, 2 * chip, answer, 0)

    rows_i = lax.broadcasted_iota(jnp.int32, (toks, toks), 0)
    cols_i = lax.broadcasted_iota(jnp.int32, (toks, toks), 1)
    causal = rows_i >= cols_i
    tri = causal.astype(F32)
    loads[4].wait()
    ld = ld_ref[...]
    cd = lax.dot_general(
        tri, ld, (NT, ((), ())), precision=lax.Precision.HIGHEST, preferred_element_type=F32
    )
    cdt = lax.dot_general(
        ld, tri, (NT, ((), ())), precision=lax.Precision.HIGHEST, preferred_element_type=F32
    )
    for h in range(heads):
        wide = jnp.broadcast_to(cd[:, h : h + 1], (toks, hd))
        total = wide[toks - 1 : toks, :]
        bt[h] = total
        grow[:, h * hd : (h + 1) * hd] = jnp.exp(wide)
        after[:, h * hd : (h + 1) * hd] = jnp.exp(total - wide)

    tail = halo_ref.shape[0]
    halo = remote(
        k_hbm.at[pl.ds(toks - tail, tail), :], halo_ref, halo_s, halo_r,
        {"ctx": lax.rem(ctx + 1, ctx_n)},
    )

    @pl.when(jnp.logical_and(core == 1, chip < chips - 1))
    def _():
        pl.semaphore_wait(here.at[chip + 1], 2)

    @pl.when(ctx < ctx_n - 1)
    def _():
        halo.start()

    swap_bt = remote(bt, bt_p, bp_s, bp_r, {"ctx": partner})
    swap_bt.start()
    for h in range(heads):
        wide = jnp.broadcast_to(cd[:, h : h + 1], (toks, hd))
        differ = wide - cdt[h : h + 1, :]
        mix[h] = jnp.where(causal, jnp.exp(jnp.where(causal, differ, 0.0)), 0.0)

    @pl.when(ctx == 0)
    def _():
        halo_ref[...] = jnp.zeros_like(halo_ref)

    @pl.when(ctx == ctx_n - 1)
    def _():
        ckg[pl.ds(toks, HALO), :] = jnp.zeros((HALO, feats), F32)

    @pl.when(pp == pp_n - 1)
    def _():
        gin_ref[...] = jnp.zeros_like(gin_ref)

    loads[0].wait()
    loads[5].wait()
    kext[pl.ds(HALO, toks), :] = k_ref[...].astype(F32)
    loads[1].wait()

    @pl.when(ctx > 0)
    def _():
        halo.wait_recv()

    kext[pl.ds(0, HALO), :] = halo_ref[pl.ds(tail - HALO, HALO), :].astype(F32)

    def sized(call):
        @pl.when(my_part < parts - 1)
        def _():
            call(rows)

        @pl.when(my_part == parts - 1)
        def _():
            call(short)

    if short < rows:
        @pl.when(my_part == parts - 1)
        def _():
            s_in[:, pl.ds(short, rows - short), :] = jnp.zeros((chips, rows - short, hd), BF16)
            b_in[:, pl.ds(short, rows - short), :] = jnp.zeros((chips, rows - short, hd), BF16)

    def swap(mine, theirs, send_sem, recv_sem, i):
        return remote(
            mine.at[their0 + i], theirs.at[i], send_sem.at[i], recv_sem.at[i], {"ctx": partner}
        )

    def spread(src, dst, send_sem, recv_sem, i, part):
        size = rows if part < parts - 1 else short
        return remote(
            src.at[i, pl.ds(part * rows, size)], dst.at[chip, pl.ds(0, size)],
            send_sem.at[i * parts + part], recv_sem.at[chip],
            {"ctx": (own0 + i) * parts + part},
        )

    def deliver(src, dst, send_sem, recv_sem, z, size):
        slot = ctx - scan_core * chips
        return remote(
            src.at[z, pl.ds(0, size)], dst.at[slot, pl.ds(0, size)], send_sem.at[z],
            recv_sem.at[slot], {"ctx": 2 * z + scan_core},
        )

    def arrive(dst, recv_sem, n, size):
        piece = dst.at[n, pl.ds(0, size)]
        return remote(piece, piece, recv_sem.at[n], recv_sem.at[n], {"ctx": partner})

    def factors(h, lead):
        e_m = jnp.exp(bt[h])
        e_t = jnp.exp(bt_p[h])
        return e_m, e_t, lead.astype(F32)

    def total_to(i, part):
        return remote(
            tot.at[i], bt_all.at[chip], bt_s.at[i * parts + part], bt_r.at[chip],
            {"ctx": (own0 + i) * parts + part},
        )

    def join(mine, theirs, xs, xr, out, into, send_sem, recv_sem, lead, needed, opening):
        def one(n, _):
            i = n
            h = own0 + i
            e_m, e_t, lf = factors(h, lead)
            swap(mine, theirs, xs, xr, i).wait_recv()
            ca = lf * e_t + (1.0 - lf)
            cb = lf + (1.0 - lf) * e_m
            out[i] = (ca * mine[h] + cb * theirs[i]).astype(BF16)
            if opening:
                tot[i] = bt[h] + bt_p[h]
                low = (h * parts + 1) // 2
                high = (h * parts + parts - 1) // 2
                meet(low)

                @pl.when(high > low)
                def _():
                    meet(high)

            for part in range(parts):
                @pl.when(h * parts + part != ctx)
                def _():
                    @pl.when(needed)
                    def _():
                        spread(out, into, send_sem, recv_sem, i, part).start()

                    if opening:
                        total_to(i, part).start()

                @pl.when(h * parts + part == ctx)
                def _():
                    size = rows if part < parts - 1 else short
                    into[chip, pl.ds(0, size), :] = out[i, pl.ds(part * rows, size), :]
                    if opening:
                        bt_all[chip] = tot[i]
            return 0

        lax.fori_loop(0, half, one, 0)

    def scan(into, recv_sem, out, home, send_sem, home_sem, opening):
        def give(z, carry):
            out[z] = carry.astype(BF16)
            if opening:
                late = jnp.where(z >= chips // 2, 1, 0)

                @pl.when(late != core)
                def _():
                    meet(z)

            @pl.when(2 * z + scan_core != ctx)
            def _():
                sized(lambda size: deliver(out, home, send_sem, home_sem, z, size).start())

            @pl.when(2 * z + scan_core == ctx)
            def _():
                home[ctx - scan_core * chips] = out[z]

        def total_in(z):
            @pl.when(2 * z + scan_core != ctx)
            def _():
                remote(
                    bt_all.at[z], bt_all.at[z], bt_r.at[z], bt_r.at[z], {"ctx": partner}
                ).wait_recv()

        if not opening:
            total_in(chips - 1)

        def one(n, carry):
            z = n if opening else chips - 1 - n
            give(z, carry)
            if opening:
                total_in(z)

            @pl.when(2 * z + scan_core != ctx)
            def _():
                sized(lambda size: arrive(into, recv_sem, z, size).wait_recv())

            return jnp.exp(bt_all[z]) * carry + into[z].astype(F32)

        carry = lax.fori_loop(0, chips - 1, one, jnp.zeros((rows, hd), F32))
        give(chips - 1 if opening else 0, carry)

    def hand(stage, dest, send_sem, recv_sem, i, h):
        return remote(
            stage.at[i], dest.at[h], send_sem.at[i], recv_sem.at[i], {"ctx": partner}
        )

    def split(home, home_sem, mine, theirs, dest, stage, hs_, hr_, lead):
        def one(n, _):
            i = n
            h = own0 + i
            e_m, e_t, lf = factors(h, lead)
            pieces = []
            for part in range(parts):
                size = rows if part < parts - 1 else short

                @pl.when(h * parts + part != ctx)
                def _():
                    arrive(home, home_sem, i * parts + part, size).wait_recv()

                pieces.append(home[i * parts + part, pl.ds(0, size), :].astype(F32))
            carry = jnp.concatenate(pieces, axis=0)
            c1 = lf + (1.0 - lf) * e_t
            c2 = lf * e_m + (1.0 - lf)
            stage[i] = (c2 * carry + lf * mine[h]).astype(BF16)
            hand(stage, dest, hs_, hr_, i, h).start()
            dest[h] = (c1 * carry + (1.0 - lf) * theirs[i]).astype(BF16)
            return 0

        lax.fori_loop(0, half, one, 0)

    def handed(stage, dest, hs_, hr_, g):
        @pl.when(g >= half_steps)
        def _():
            for j in range(group):
                h = own_first(g * group + j)
                hand(stage, dest, hs_, hr_, h - their0, h).wait_recv()

    def states(g, _):
        for j in range(group):
            h = own_last(g * group + j)
            hs = lanes(h)
            conv = w_ref[pl.ds(0, 1), hs] * kext[pl.ds(HALO, toks), hs]
            for tap in range(1, taps):
                conv = conv + w_ref[pl.ds(tap, 1), hs] * kext[pl.ds(HALO - tap, toks), hs]
            keys = conv.astype(BF16)
            kc[:, hs] = keys
            scaled = (keys.astype(F32) * after[:, hs]).astype(BF16)
            s_m[h] = dot(scaled, v_ref[:, hs], TN)

        @pl.when(g < half_steps)
        def _():
            for j in range(group):
                swap(s_m, s_t, sx_s, sx_r, own_last(g * group + j) - their0).start()

        return 0

    lax.fori_loop(0, steps, states, 0)
    swap_bt.wait_recv()
    join(s_m, s_t, sx_s, sx_r, s_out, s_in, s_s, s_r, core == 0, chip < chips - 1, True)
    loads[2].wait()

    def inside(g, _):
        for j in range(group):
            h = g * group + j
            hs = lanes(h)
            scores = dot(q_ref[:, hs], kc[:, hs], NT)
            w = (scores * mix[h]).astype(BF16)
            wts[h] = w
            att[:, hs] = dot(w, v_ref[:, hs], NN)
            sq[:, hs] = (q_ref[:, hs].astype(F32) * grow[:, hs]).astype(BF16)
        return 0

    lax.fori_loop(0, steps, inside, 0)

    scan(s_in, s_r, p_out, p_in, p_s, p_r, True)
    split(p_in, p_r, s_m, s_t, p_half, p_stage, px_s, px_r, core == 0)

    loads[3].wait()
    acc_sq[...] = jnp.zeros_like(acc_sq)
    acc_dot[...] = jnp.zeros_like(acc_dot)

    def attend(g, _):
        handed(p_stage, p_half, px_s, px_r, g)
        for j in range(group):
            h = own_first(g * group + j)
            hs = lanes(h)
            a = att[:, hs] + grow[:, hs] * dot(q_ref[:, hs], p_half[h], NN)
            att[:, hs] = a
            acc_sq[...] += a * a
            acc_dot[...] += a * og_ref[:, hs].astype(F32)
        return 0

    lax.fori_loop(0, steps, attend, 0)

    sq_row = jnp.sum(acc_sq[...].T, axis=0, keepdims=True)
    dot_row = jnp.sum(acc_dot[...].T, axis=0, keepdims=True)
    first_row = lax.broadcasted_iota(jnp.int32, (8, toks), 0) == 0
    tpbuf[0] = jnp.where(first_row, sq_row, dot_row)

    def sums(step):
        return remote(
            tpbuf.at[0], tpbuf.at[step], tp_s.at[step - 1], tp_r.at[step - 1],
            {"tp": lax.rem(tp + step, tp_n)},
        )

    for step in range(1, tp_n):
        sums(step).start()
    for step in range(1, tp_n):
        sums(step).wait_recv()
    sums_all = tpbuf[0]
    for step in range(1, tp_n):
        sums_all = sums_all + tpbuf[step]
    inv_row = 1.0 / jnp.sqrt(sums_all[0:1, :] / width_all + 1e-06)
    shift_row = (sums_all[1:2, :] / width_all) * inv_row
    inv = jnp.broadcast_to(inv_row, (hd, toks)).T
    shift = jnp.broadcast_to(shift_row, (hd, toks)).T

    def adjoints(g, _):
        for j in range(group):
            h = own_last(g * group + j)
            hs = lanes(h)
            normed = att[:, hs] * inv
            grad = ((og_ref[:, hs].astype(F32) - normed * shift) * inv).astype(BF16)
            ag[:, hs] = grad
            b_m[h] = dot(sq[:, hs], grad, TN)

        @pl.when(g < half_steps)
        def _():
            for j in range(group):
                swap(b_m, b_t, bx_s, bx_r, own_last(g * group + j) - their0).start()

        return 0

    lax.fori_loop(0, steps, adjoints, 0)
    join(b_m, b_t, bx_s, bx_r, b_out, b_in, b_s, b_r, core == 1, chip > 0, False)

    def inside_grads(g, _):
        for j in range(group):
            h = g * group + j
            hs = lanes(h)
            grad = ag[:, hs]
            out_ref[:, hs] = (att[:, hs] * inv).astype(BF16)
            sg = (dot(grad, v_ref[:, hs], NT) * mix[h]).astype(BF16)
            qg = dot(sg, kc[:, hs], NN) + grow[:, hs] * dot(grad, p_half[h], NT)
            acc[:, hs] = qg + dot(wts[h], grad, TN)
            ckg[pl.ds(0, toks), hs] = dot(sg, q_ref[:, hs], TN)
        return 0

    lax.fori_loop(0, steps, inside_grads, 0)
    scan(b_in, b_r, a_out, a_in, a_s, a_r, False)
    split(a_in, a_r, b_m, b_t, a_half, a_stage, ax_s, ax_r, core == 1)

    def edge(h):
        hs = lanes(h)
        return remote(
            ckg.at[pl.ds(0, HALO), hs], ckg.at[pl.ds(toks, HALO), hs], ch_s.at[h], ch_r.at[h],
            {"ctx": lax.rem(ctx + ctx_n - 1, ctx_n)},
        )

    most = toks - LAST

    def summed(h, first, size):
        hs = lanes(h)
        total = acc[pl.ds(first, size), hs]
        for tap in range(taps):
            total = total + w_ref[pl.ds(tap, 1), hs] * ckg[pl.ds(first + tap, size), hs]
        gst[pl.ds(first, size), hs] = total.astype(BF16)

    def back(h):
        piece = (pl.ds(0, most), lanes(h))
        return remote(
            gst.at[piece], gin_ref.at[piece], pp_s.at[h], pp_r.at[h],
            {"pp": lax.rem(pp + pp_n - 1, pp_n)},
        )

    back_last = remote(
        gst.at[pl.ds(most, LAST), :], gin_ref.at[pl.ds(most, LAST), :], pl_s, pl_r,
        {"pp": lax.rem(pp + pp_n - 1, pp_n)},
    )

    def outside_grads(g, _):
        handed(a_stage, a_half, ax_s, ax_r, g)
        for j in range(group):
            h = own_first(g * group + j)
            hs = lanes(h)
            wa = after[:, hs]
            state = a_half[h]
            ckg[pl.ds(0, toks), hs] += wa * dot(v_ref[:, hs], state, NT)
            acc[:, hs] += wa * dot(kc[:, hs], state, NN)

        @pl.when(ctx > 0)
        def _():
            for j in range(group):
                edge(own_first(g * group + j)).start()

        for j in range(group):
            summed(own_first(g * group + j), 0, most)

        @pl.when(pp > 0)
        def _():
            for j in range(group):
                back(own_first(g * group + j)).start()

        return 0

    lax.fori_loop(0, steps, outside_grads, 0)

    def finish(g, _):
        @pl.when(ctx < ctx_n - 1)
        def _():
            for j in range(group):
                edge(own_last(g * group + j)).wait_recv()

        for j in range(group):
            summed(own_last(g * group + j), most, LAST)
        return 0

    lax.fori_loop(0, steps, finish, 0)

    @pl.when(pp > 0)
    def _():
        back_last.start()

    @pl.when(ctx < ctx_n - 1)
    def _():
        halo.wait_send()

    for step in range(1, tp_n):
        sums(step).wait_send()

    swap_bt.wait_send()

    def left(i, _):
        h = own0 + i
        swap(s_m, s_t, sx_s, sx_r, i).wait_send()
        swap(b_m, b_t, bx_s, bx_r, i).wait_send()
        hand(p_stage, p_half, px_s, px_r, i, h).wait_send()
        hand(a_stage, a_half, ax_s, ax_r, i, h).wait_send()
        for part in range(parts):
            @pl.when(h * parts + part != ctx)
            def _():
                total_to(i, part).wait_send()

                @pl.when(chip < chips - 1)
                def _():
                    spread(s_out, s_in, s_s, s_r, i, part).wait_send()

                @pl.when(chip > 0)
                def _():
                    spread(b_out, b_in, b_s, b_r, i, part).wait_send()

        return 0

    lax.fori_loop(0, half, left, 0)

    def given(z, _):
        @pl.when(2 * z + scan_core != ctx)
        def _():
            sized(lambda size: deliver(p_out, p_in, p_s, p_r, z, size).wait_send())
            sized(lambda size: deliver(a_out, a_in, a_s, a_r, z, size).wait_send())

        return 0

    lax.fori_loop(0, chips, given, 0)

    @pl.when(ctx > 0)
    def _():
        def leave(h, _):
            edge(h).wait_send()
            return 0

        lax.fori_loop(0, heads, leave, 0)

    @pl.when(pp > 0)
    def _():
        def leave(h, _):
            back(h).wait_send()
            return 0

        lax.fori_loop(0, heads, leave, 0)
        back_last.wait_send()

    @pl.when(pp < pp_n - 1)
    def _():
        def land(h, _):
            back(h).wait_recv()
            return 0

        lax.fori_loop(0, heads, land, 0)
        back_last.wait_recv()


def place(a_ref, b_ref, c_ref, d_ref, sems):
    puts = [
        pltpu.make_async_copy(src, dst, sems.at[n])
        for n, (src, dst) in enumerate(((a_ref, c_ref), (b_ref, d_ref)))
    ]
    for put in puts:
        put.start()
    for put in puts:
        put.wait()


def solution(mesh):
    ctx_n, tp_n, pp_n = mesh.shape["ctx"], mesh.shape["tp"], mesh.shape["pp"]

    def per_device(queries, key_input, values, log_decay, conv_weight, out_grad):
        toks, feats = queries.shape[1:]
        heads = log_decay.shape[2]
        hd = feats // heads
        parts = ctx_n // heads
        rows = -(-hd // (16 * parts)) * 16
        dma = pltpu.SemaphoreType.DMA
        flat_b = pltpu.VMEM((toks, feats), BF16)
        flat_f = pltpu.VMEM((toks, feats), F32)
        half = heads // 2
        chips = ctx_n // 2
        full_f = pltpu.VMEM((heads, hd, hd), F32)
        full_b = pltpu.VMEM((heads, hd, hd), BF16)
        half_f = pltpu.VMEM((half, hd, hd), F32)
        half_b = pltpu.VMEM((half, hd, hd), BF16)
        shares = pltpu.VMEM((chips, rows, hd), BF16)
        totals = pltpu.VMEM((heads, 1, hd), F32)
        scanned = [full_f, half_f, half_b, shares, shares, shares, full_b, half_b]
        longer = pltpu.VMEM((toks + HALO, feats), F32)
        square = pltpu.VMEM((toks, hd), F32)
        scratch = [
            pltpu.VMEM((heads, toks), F32), pltpu.VMEM((conv_weight.shape[1], feats), F32),
            flat_b, flat_b, flat_b, flat_b, pltpu.VMEM((16, feats), BF16), longer, flat_b,
            flat_f, flat_f, pltpu.VMEM((heads, toks, toks), F32),
            pltpu.VMEM((heads, toks, toks), BF16), flat_f, flat_b, flat_f, longer, flat_b, flat_b,
            totals, totals, pltpu.VMEM((half, 1, hd), F32), pltpu.VMEM((chips, 1, hd), F32),
            square, square,
            pltpu.VMEM((tp_n, 8, toks), F32),
        ]
        scratch += scanned + scanned
        scratch += [pltpu.SemaphoreType.REGULAR((chips,))]
        scratch += [dma((6,)), dma, dma, dma, dma, dma((chips,)), dma((chips,))]
        scratch += [dma((max(tp_n - 1, 1),))] * 2 + [dma((chips,))] * 8 + [dma((half,))] * 8
        scratch += [dma((heads,))] * 4 + [dma, dma]
        whole = pl.BlockSpec(memory_space=pltpu.VMEM)
        there = pl.BlockSpec(memory_space=pl.ANY)

        def stay(x):
            return pltpu.with_memory_space_constraint(x, pltpu.HBM)

        def body(*refs):
            kernel(ctx_n, tp_n, pp_n, *refs)

        shape = jax.ShapeDtypeStruct((toks, feats), BF16)
        out, gin = pl.pallas_call(
            body,
            out_shape=(shape, shape),
            in_specs=[there] * 6,
            out_specs=(whole, whole),
            scratch_shapes=scratch,
            compiler_params=pltpu.CompilerParams(
                collective_id=0, has_side_effects=True, vmem_limit_bytes=40 * 1024 * 1024
            ),
        )(
            stay(queries[0]), stay(key_input[0]), stay(values[0]), stay(log_decay[0].T),
            stay(conv_weight[0]), stay(out_grad[0]),
        )
        out, gin = pl.pallas_call(
            place,
            out_shape=(shape, shape),
            in_specs=[whole, whole],
            out_specs=(there, there),
            scratch_shapes=[dma((2,))],
            compiler_params=pltpu.CompilerParams(vmem_limit_bytes=1024 * 1024),
        )(out, gin)
        return out[None], gin[None]

    placed = (
        P("pp", "ctx", "tp"),
        P("pp", "ctx", "tp"),
        P("pp", "ctx", "tp"),
        P("pp", "ctx", "tp"),
        P("pp", None, "tp"),
        P("pp", "ctx", "tp"),
    )
    return jax.shard_map(
        per_device,
        mesh=mesh,
        in_specs=placed,
        out_specs=(P("pp", "ctx", "tp"), P("pp", "ctx", "tp")),
        check_vma=False,
    )
```

```python
import jax
import jax.numpy as jnp
from jax import lax
from jax.experimental import pallas as pl
from jax.experimental.pallas import tpu as pltpu
from jax.sharding import PartitionSpec as P

MESH = pl.DeviceIdType.MESH
F32 = jnp.float32
BF16 = jnp.bfloat16
HALO = 8
LAST = 16
GROUP = 2


def remote(src, dst, send_sem, recv_sem, where):
    return pltpu.make_async_remote_copy(
        src_ref=src,
        dst_ref=dst,
        send_sem=send_sem,
        recv_sem=recv_sem,
        device_id=where,
        device_id_type=MESH,
    )


def dot(a, b, dims):
    return lax.dot_general(a, b, (dims, ((), ())), preferred_element_type=F32)


NN = ((1,), (0,))
NT = ((1,), (1,))
TN = ((0,), (0,))


def kernel(
    ctx_n, tp_n, pp_n,
    q_hbm, k_hbm, v_hbm, ld_hbm, w_hbm, og_hbm,
    out_ref, gin_ref,
    ld_ref, w_ref, q_ref, k_ref, v_ref, og_ref, halo_ref, kext, kc, grow, after, mix, wts, att, ag, acc, ckg, gst, sq,
    bt, bt_p, tot, bt_all, acc_sq, acc_dot, tpbuf,
    s_m, s_t, s_out, s_in, p_out, p_in, p_half, p_stage,
    b_m, b_t, b_out, b_in, a_out, a_in, a_half, a_stage,
    here, load_sem, halo_s, halo_r, bp_s, bp_r, bt_s, bt_r, tp_s, tp_r,
    s_s, s_r, p_s, p_r, b_s, b_r, a_s, a_r,
    sx_s, sx_r, px_s, px_r, bx_s, bx_r, ax_s, ax_r, ch_s, ch_r, pp_s, pp_r, pl_s, pl_r,
):
    toks, feats = q_hbm.shape
    heads = ld_hbm.shape[0]
    hd = feats // heads
    taps = w_hbm.shape[0]
    width_all = feats * tp_n
    parts = ctx_n // heads
    rows = s_in.shape[1]
    short = hd - rows * (parts - 1)
    group = min(GROUP, heads // 2)
    steps = heads // group
    half = heads // 2
    half_steps = half // group
    chips = ctx_n // 2
    ctx = lax.axis_index("ctx")
    tp = lax.axis_index("tp")
    pp = lax.axis_index("pp")
    core = lax.rem(ctx, 2)
    chip = ctx // 2
    partner = ctx + 1 - 2 * core
    own0 = half * core
    their0 = half * (1 - core)
    my_head = ctx // parts
    my_part = lax.rem(ctx, parts)
    scan_core = my_head // half

    def lanes(h):
        return pl.ds(pl.multiple_of(h * hd, hd), hd)

    def own_first(idx):
        return lax.rem(own0 + idx, heads)

    def own_last(idx):
        return lax.rem(their0 + idx, heads)

    barrier = pltpu.get_barrier_semaphore()
    greet = [{"ctx": partner}]
    greet += [{"tp": lax.rem(tp + step, tp_n)} for step in range(1, tp_n)]
    for where in greet:
        pl.semaphore_signal(barrier, inc=1, device_id=where, device_id_type=MESH)

    @pl.when(pp < pp_n - 1)
    def _():
        pl.semaphore_signal(
            barrier, inc=1, device_id={"pp": lax.rem(pp + 1, pp_n)}, device_id_type=MESH
        )

    def enter(peer, _):
        pl.semaphore_signal(barrier, inc=1, device_id={"ctx": peer}, device_id_type=MESH)
        return 0

    lax.fori_loop(2 * chip + 2, ctx_n, enter, 0)

    def meet(z):
        @pl.when(jnp.logical_and(z > chip, z != chip + core))
        def _():
            pl.semaphore_wait(here.at[z], 2)

    loads = [
        pltpu.make_async_copy(src, dst, load_sem.at[n])
        for n, (src, dst) in enumerate(
            (
                (k_hbm, k_ref), (v_hbm, v_ref), (q_hbm, q_ref), (og_hbm, og_ref),
                (ld_hbm, ld_ref), (w_hbm, w_ref),
            )
        )
    ]
    for n in (4, 0, 5, 1, 2, 3):
        loads[n].start()

    pl.semaphore_wait(barrier, len(greet) + 2 * chip + (pp + pp_n - 1) // pp_n)

    def answer(peer, _):
        pl.semaphore_signal(here.at[chip], inc=1, device_id={"ctx": peer}, device_id_type=MESH)
        return 0

    lax.fori_loop(0, 2 * chip, answer, 0)

    rows_i = lax.broadcasted_iota(jnp.int32, (toks, toks), 0)
    cols_i = lax.broadcasted_iota(jnp.int32, (toks, toks), 1)
    causal = rows_i >= cols_i
    tri = causal.astype(F32)
    loads[4].wait()
    ld = ld_ref[...]
    cd = lax.dot_general(
        tri, ld, (NT, ((), ())), precision=lax.Precision.HIGHEST, preferred_element_type=F32
    )
    cdt = lax.dot_general(
        ld, tri, (NT, ((), ())), precision=lax.Precision.HIGHEST, preferred_element_type=F32
    )
    for h in range(heads):
        wide = jnp.broadcast_to(cd[:, h : h + 1], (toks, hd))
        total = wide[toks - 1 : toks, :]
        bt[h] = total
        grow[:, h * hd : (h + 1) * hd] = jnp.exp(wide)
        after[:, h * hd : (h + 1) * hd] = jnp.exp(total - wide)

    tail = halo_ref.shape[0]
    halo = remote(
        k_hbm.at[pl.ds(toks - tail, tail), :], halo_ref, halo_s, halo_r,
        {"ctx": lax.rem(ctx + 1, ctx_n)},
    )

    @pl.when(jnp.logical_and(core == 1, chip < chips - 1))
    def _():
        pl.semaphore_wait(here.at[chip + 1], 2)

    @pl.when(ctx < ctx_n - 1)
    def _():
        halo.start()

    swap_bt = remote(bt, bt_p, bp_s, bp_r, {"ctx": partner})
    swap_bt.start()
    for h in range(heads):
        wide = jnp.broadcast_to(cd[:, h : h + 1], (toks, hd))
        differ = wide - cdt[h : h + 1, :]
        mix[h] = jnp.where(causal, jnp.exp(jnp.where(causal, differ, 0.0)), 0.0)

    @pl.when(ctx == 0)
    def _():
        halo_ref[...] = jnp.zeros_like(halo_ref)

    @pl.when(ctx == ctx_n - 1)
    def _():
        ckg[pl.ds(toks, HALO), :] = jnp.zeros((HALO, feats), F32)

    @pl.when(pp == pp_n - 1)
    def _():
        gin_ref[...] = jnp.zeros_like(gin_ref)

    loads[0].wait()
    loads[5].wait()
    kext[pl.ds(HALO, toks), :] = k_ref[...].astype(F32)
    loads[1].wait()

    @pl.when(ctx > 0)
    def _():
        halo.wait_recv()

    kext[pl.ds(0, HALO), :] = halo_ref[pl.ds(tail - HALO, HALO), :].astype(F32)

    def sized(call):
        @pl.when(my_part < parts - 1)
        def _():
            call(rows)

        @pl.when(my_part == parts - 1)
        def _():
            call(short)

    if short < rows:
        @pl.when(my_part == parts - 1)
        def _():
            s_in[:, pl.ds(short, rows - short), :] = jnp.zeros((chips, rows - short, hd), BF16)
            b_in[:, pl.ds(short, rows - short), :] = jnp.zeros((chips, rows - short, hd), BF16)

    def swap(mine, theirs, send_sem, recv_sem, i):
        return remote(
            mine.at[their0 + i], theirs.at[i], send_sem.at[i], recv_sem.at[i], {"ctx": partner}
        )

    def spread(src, dst, send_sem, recv_sem, i, part):
        size = rows if part < parts - 1 else short
        return remote(
            src.at[i, pl.ds(part * rows, size)], dst.at[chip, pl.ds(0, size)],
            send_sem.at[i * parts + part], recv_sem.at[chip],
            {"ctx": (own0 + i) * parts + part},
        )

    def deliver(src, dst, send_sem, recv_sem, z, size):
        slot = ctx - scan_core * chips
        return remote(
            src.at[z, pl.ds(0, size)], dst.at[slot, pl.ds(0, size)], send_sem.at[z],
            recv_sem.at[slot], {"ctx": 2 * z + scan_core},
        )

    def arrive(dst, recv_sem, n, size):
        piece = dst.at[n, pl.ds(0, size)]
        return remote(piece, piece, recv_sem.at[n], recv_sem.at[n], {"ctx": partner})

    def factors(h, lead):
        e_m = jnp.exp(bt[h])
        e_t = jnp.exp(bt_p[h])
        return e_m, e_t, lead.astype(F32)

    def total_to(i, part):
        return remote(
            tot.at[i], bt_all.at[chip], bt_s.at[i * parts + part], bt_r.at[chip],
            {"ctx": (own0 + i) * parts + part},
        )

    def join(mine, theirs, xs, xr, out, into, send_sem, recv_sem, lead, needed, opening):
        def one(n, _):
            i = n
            h = own0 + i
            e_m, e_t, lf = factors(h, lead)
            swap(mine, theirs, xs, xr, i).wait_recv()
            ca = lf * e_t + (1.0 - lf)
            cb = lf + (1.0 - lf) * e_m
            out[i] = (ca * mine[h] + cb * theirs[i]).astype(BF16)
            if opening:
                tot[i] = bt[h] + bt_p[h]
                low = (h * parts + 1) // 2
                high = (h * parts + parts - 1) // 2
                meet(low)

                @pl.when(high > low)
                def _():
                    meet(high)

            for part in range(parts):
                @pl.when(h * parts + part != ctx)
                def _():
                    @pl.when(needed)
                    def _():
                        spread(out, into, send_sem, recv_sem, i, part).start()

                @pl.when(h * parts + part == ctx)
                def _():
                    size = rows if part < parts - 1 else short
                    into[chip, pl.ds(0, size), :] = out[i, pl.ds(part * rows, size), :]
                    if opening:
                        bt_all[chip] = tot[i]
            return 0

        lax.fori_loop(0, half, one, 0)

        def tell(i, _):
            for part in range(parts):
                @pl.when((own0 + i) * parts + part != ctx)
                def _():
                    total_to(i, part).start()

            return 0

        if opening:
            lax.fori_loop(0, half, tell, 0)

    def scan(into, recv_sem, out, home, send_sem, home_sem, opening):
        def give(z, carry):
            out[z] = carry.astype(BF16)
            late = jnp.where(z >= chips // 2, 1, 0)

            @pl.when(late != core)
            def _():
                meet(z)

            send(z)

        def send(z):
            @pl.when(2 * z + scan_core != ctx)
            def _():
                sized(lambda size: deliver(out, home, send_sem, home_sem, z, size).start())

            @pl.when(2 * z + scan_core == ctx)
            def _():
                home[ctx - scan_core * chips] = out[z]

        def total_in(z):
            @pl.when(2 * z + scan_core != ctx)
            def _():
                remote(
                    bt_all.at[z], bt_all.at[z], bt_r.at[z], bt_r.at[z], {"ctx": partner}
                ).wait_recv()

        if not opening:
            total_in(chips - 1)

            def ready(z, _):
                @pl.when(2 * z + scan_core != ctx)
                def _():
                    sized(lambda size: arrive(into, recv_sem, z, size).wait_recv())

                return 0

            lax.fori_loop(1, chips, ready, 0)
            carry = jnp.zeros((rows, hd), F32)
            for z in range(chips - 1, -1, -1):
                out[z] = carry.astype(BF16)
                if z > 0:
                    carry = jnp.exp(bt_all[z]) * carry + into[z].astype(F32)

            def serve(z, _):
                send(z)
                return 0

            lax.fori_loop(0, chips, serve, 0)
            return

        def one(n, carry):
            z = n
            give(z, carry)
            total_in(z)

            @pl.when(2 * z + scan_core != ctx)
            def _():
                sized(lambda size: arrive(into, recv_sem, z, size).wait_recv())

            return jnp.exp(bt_all[z]) * carry + into[z].astype(F32)

        carry = lax.fori_loop(0, chips - 1, one, jnp.zeros((rows, hd), F32))
        give(chips - 1, carry)

    def hand(stage, dest, send_sem, recv_sem, i, h):
        return remote(
            stage.at[i], dest.at[h], send_sem.at[i], recv_sem.at[i], {"ctx": partner}
        )

    def split(home, home_sem, mine, theirs, dest, stage, hs_, hr_, lead):
        def one(n, _):
            i = n
            h = own0 + i
            e_m, e_t, lf = factors(h, lead)
            pieces = []
            for part in range(parts):
                size = rows if part < parts - 1 else short

                @pl.when(h * parts + part != ctx)
                def _():
                    arrive(home, home_sem, i * parts + part, size).wait_recv()

                pieces.append(home[i * parts + part, pl.ds(0, size), :].astype(F32))
            carry = jnp.concatenate(pieces, axis=0)
            c1 = lf + (1.0 - lf) * e_t
            c2 = lf * e_m + (1.0 - lf)
            stage[i] = (c2 * carry + lf * mine[h]).astype(BF16)
            hand(stage, dest, hs_, hr_, i, h).start()
            dest[h] = (c1 * carry + (1.0 - lf) * theirs[i]).astype(BF16)
            return 0

        lax.fori_loop(0, half, one, 0)

    def handed(stage, dest, hs_, hr_, g):
        @pl.when(g >= half_steps)
        def _():
            for j in range(group):
                h = own_first(g * group + j)
                hand(stage, dest, hs_, hr_, h - their0, h).wait_recv()

    def states(g, _):
        for j in range(group):
            h = own_last(g * group + j)
            hs = lanes(h)
            conv = w_ref[pl.ds(0, 1), hs] * kext[pl.ds(HALO, toks), hs]
            for tap in range(1, taps):
                conv = conv + w_ref[pl.ds(tap, 1), hs] * kext[pl.ds(HALO - tap, toks), hs]
            keys = conv.astype(BF16)
            kc[:, hs] = keys
            scaled = (keys.astype(F32) * after[:, hs]).astype(BF16)
            s_m[h] = dot(scaled, v_ref[:, hs], TN)

        @pl.when(g < half_steps)
        def _():
            for j in range(group):
                swap(s_m, s_t, sx_s, sx_r, own_last(g * group + j) - their0).start()

        return 0

    lax.fori_loop(0, steps, states, 0)
    swap_bt.wait_recv()
    join(s_m, s_t, sx_s, sx_r, s_out, s_in, s_s, s_r, core == 0, chip < chips - 1, True)
    loads[2].wait()

    def inside(g, _):
        for j in range(group):
            h = g * group + j
            hs = lanes(h)
            scores = dot(q_ref[:, hs], kc[:, hs], NT)
            w = (scores * mix[h]).astype(BF16)
            wts[h] = w
            att[:, hs] = dot(w, v_ref[:, hs], NN)
            sq[:, hs] = (q_ref[:, hs].astype(F32) * grow[:, hs]).astype(BF16)
        return 0

    lax.fori_loop(0, steps, inside, 0)

    scan(s_in, s_r, p_out, p_in, p_s, p_r, True)
    split(p_in, p_r, s_m, s_t, p_half, p_stage, px_s, px_r, core == 0)

    loads[3].wait()
    acc_sq[...] = jnp.zeros_like(acc_sq)
    acc_dot[...] = jnp.zeros_like(acc_dot)

    def attend(g, _):
        handed(p_stage, p_half, px_s, px_r, g)
        for j in range(group):
            h = own_first(g * group + j)
            hs = lanes(h)
            a = att[:, hs] + grow[:, hs] * dot(q_ref[:, hs], p_half[h], NN)
            att[:, hs] = a
            acc_sq[...] += a * a
            acc_dot[...] += a * og_ref[:, hs].astype(F32)
        return 0

    lax.fori_loop(0, steps, attend, 0)

    sq_row = jnp.sum(acc_sq[...].T, axis=0, keepdims=True)
    dot_row = jnp.sum(acc_dot[...].T, axis=0, keepdims=True)
    first_row = lax.broadcasted_iota(jnp.int32, (8, toks), 0) == 0
    tpbuf[0] = jnp.where(first_row, sq_row, dot_row)

    def sums(step):
        return remote(
            tpbuf.at[0], tpbuf.at[step], tp_s.at[step - 1], tp_r.at[step - 1],
            {"tp": lax.rem(tp + step, tp_n)},
        )

    for step in range(1, tp_n):
        sums(step).start()
    for step in range(1, tp_n):
        sums(step).wait_recv()
    sums_all = tpbuf[0]
    for step in range(1, tp_n):
        sums_all = sums_all + tpbuf[step]
    inv_row = 1.0 / jnp.sqrt(sums_all[0:1, :] / width_all + 1e-06)
    shift_row = (sums_all[1:2, :] / width_all) * inv_row
    inv = jnp.broadcast_to(inv_row, (hd, toks)).T
    shift = jnp.broadcast_to(shift_row, (hd, toks)).T

    def adjoints(g, _):
        for j in range(group):
            h = own_last(g * group + j)
            hs = lanes(h)
            normed = att[:, hs] * inv
            grad = ((og_ref[:, hs].astype(F32) - normed * shift) * inv).astype(BF16)
            ag[:, hs] = grad
            b_m[h] = dot(sq[:, hs], grad, TN)

        @pl.when(g < half_steps)
        def _():
            for j in range(group):
                swap(b_m, b_t, bx_s, bx_r, own_last(g * group + j) - their0).start()

        return 0

    lax.fori_loop(0, steps, adjoints, 0)
    join(b_m, b_t, bx_s, bx_r, b_out, b_in, b_s, b_r, core == 1, chip > 0, False)

    def inside_grads(g, _):
        for j in range(group):
            h = g * group + j
            hs = lanes(h)
            grad = ag[:, hs]
            out_ref[:, hs] = (att[:, hs] * inv).astype(BF16)
            sg = (dot(grad, v_ref[:, hs], NT) * mix[h]).astype(BF16)
            qg = dot(sg, kc[:, hs], NN) + grow[:, hs] * dot(grad, p_half[h], NT)
            acc[:, hs] = qg + dot(wts[h], grad, TN)
            ckg[pl.ds(0, toks), hs] = dot(sg, q_ref[:, hs], TN)
        return 0

    lax.fori_loop(0, steps, inside_grads, 0)
    scan(b_in, b_r, a_out, a_in, a_s, a_r, False)
    split(a_in, a_r, b_m, b_t, a_half, a_stage, ax_s, ax_r, core == 1)

    def edge(h):
        hs = lanes(h)
        return remote(
            ckg.at[pl.ds(0, HALO), hs], ckg.at[pl.ds(toks, HALO), hs], ch_s.at[h], ch_r.at[h],
            {"ctx": lax.rem(ctx + ctx_n - 1, ctx_n)},
        )

    most = toks - LAST

    def summed(h, first, size):
        hs = lanes(h)
        total = acc[pl.ds(first, size), hs]
        for tap in range(taps):
            total = total + w_ref[pl.ds(tap, 1), hs] * ckg[pl.ds(first + tap, size), hs]
        gst[pl.ds(first, size), hs] = total.astype(BF16)

    def back(h):
        piece = (pl.ds(0, most), lanes(h))
        return remote(
            gst.at[piece], gin_ref.at[piece], pp_s.at[h], pp_r.at[h],
            {"pp": lax.rem(pp + pp_n - 1, pp_n)},
        )

    back_last = remote(
        gst.at[pl.ds(most, LAST), :], gin_ref.at[pl.ds(most, LAST), :], pl_s, pl_r,
        {"pp": lax.rem(pp + pp_n - 1, pp_n)},
    )

    def outside_grads(g, _):
        handed(a_stage, a_half, ax_s, ax_r, g)
        for j in range(group):
            h = own_first(g * group + j)
            hs = lanes(h)
            wa = after[:, hs]
            state = a_half[h]
            ckg[pl.ds(0, toks), hs] += wa * dot(v_ref[:, hs], state, NT)
            acc[:, hs] += wa * dot(kc[:, hs], state, NN)

        @pl.when(ctx > 0)
        def _():
            for j in range(group):
                edge(own_first(g * group + j)).start()

        for j in range(group):
            summed(own_first(g * group + j), 0, most)

        @pl.when(pp > 0)
        def _():
            for j in range(group):
                back(own_first(g * group + j)).start()

        return 0

    lax.fori_loop(0, steps, outside_grads, 0)

    def finish(g, _):
        @pl.when(ctx < ctx_n - 1)
        def _():
            for j in range(group):
                edge(own_last(g * group + j)).wait_recv()

        for j in range(group):
            summed(own_last(g * group + j), most, LAST)
        return 0

    lax.fori_loop(0, steps, finish, 0)

    @pl.when(pp > 0)
    def _():
        back_last.start()

    @pl.when(ctx < ctx_n - 1)
    def _():
        halo.wait_send()

    for step in range(1, tp_n):
        sums(step).wait_send()

    swap_bt.wait_send()

    def left(i, _):
        h = own0 + i
        swap(s_m, s_t, sx_s, sx_r, i).wait_send()
        swap(b_m, b_t, bx_s, bx_r, i).wait_send()
        hand(p_stage, p_half, px_s, px_r, i, h).wait_send()
        hand(a_stage, a_half, ax_s, ax_r, i, h).wait_send()
        for part in range(parts):
            @pl.when(h * parts + part != ctx)
            def _():
                total_to(i, part).wait_send()

                @pl.when(chip < chips - 1)
                def _():
                    spread(s_out, s_in, s_s, s_r, i, part).wait_send()

                @pl.when(chip > 0)
                def _():
                    spread(b_out, b_in, b_s, b_r, i, part).wait_send()

        return 0

    lax.fori_loop(0, half, left, 0)

    def given(z, _):
        @pl.when(2 * z + scan_core != ctx)
        def _():
            sized(lambda size: deliver(p_out, p_in, p_s, p_r, z, size).wait_send())
            sized(lambda size: deliver(a_out, a_in, a_s, a_r, z, size).wait_send())

        return 0

    lax.fori_loop(0, chips, given, 0)

    @pl.when(ctx > 0)
    def _():
        def leave(h, _):
            edge(h).wait_send()
            return 0

        lax.fori_loop(0, heads, leave, 0)

    @pl.when(pp > 0)
    def _():
        def leave(h, _):
            back(h).wait_send()
            return 0

        lax.fori_loop(0, heads, leave, 0)
        back_last.wait_send()

    @pl.when(pp < pp_n - 1)
    def _():
        def land(h, _):
            back(h).wait_recv()
            return 0

        lax.fori_loop(0, heads, land, 0)
        back_last.wait_recv()


def place(a_ref, b_ref, c_ref, d_ref, sems):
    puts = [
        pltpu.make_async_copy(src, dst, sems.at[n])
        for n, (src, dst) in enumerate(((a_ref, c_ref), (b_ref, d_ref)))
    ]
    for put in puts:
        put.start()
    for put in puts:
        put.wait()


def solution(mesh):
    ctx_n, tp_n, pp_n = mesh.shape["ctx"], mesh.shape["tp"], mesh.shape["pp"]

    def per_device(queries, key_input, values, log_decay, conv_weight, out_grad):
        toks, feats = queries.shape[1:]
        heads = log_decay.shape[2]
        hd = feats // heads
        parts = ctx_n // heads
        rows = -(-hd // (16 * parts)) * 16
        dma = pltpu.SemaphoreType.DMA
        flat_b = pltpu.VMEM((toks, feats), BF16)
        flat_f = pltpu.VMEM((toks, feats), F32)
        half = heads // 2
        chips = ctx_n // 2
        full_f = pltpu.VMEM((heads, hd, hd), F32)
        full_b = pltpu.VMEM((heads, hd, hd), BF16)
        half_f = pltpu.VMEM((half, hd, hd), F32)
        half_b = pltpu.VMEM((half, hd, hd), BF16)
        shares = pltpu.VMEM((chips, rows, hd), BF16)
        totals = pltpu.VMEM((heads, 1, hd), F32)
        scanned = [full_f, half_f, half_b, shares, shares, shares, full_b, half_b]
        longer = pltpu.VMEM((toks + HALO, feats), F32)
        square = pltpu.VMEM((toks, hd), F32)
        scratch = [
            pltpu.VMEM((heads, toks), F32), pltpu.VMEM((conv_weight.shape[1], feats), F32),
            flat_b, flat_b, flat_b, flat_b, pltpu.VMEM((16, feats), BF16), longer, flat_b,
            flat_f, flat_f, pltpu.VMEM((heads, toks, toks), F32),
            pltpu.VMEM((heads, toks, toks), BF16), flat_f, flat_b, flat_f, longer, flat_b, flat_b,
            totals, totals, pltpu.VMEM((half, 1, hd), F32), pltpu.VMEM((chips, 1, hd), F32),
            square, square,
            pltpu.VMEM((tp_n, 8, toks), F32),
        ]
        scratch += scanned + scanned
        scratch += [pltpu.SemaphoreType.REGULAR((chips,))]
        scratch += [dma((6,)), dma, dma, dma, dma, dma((chips,)), dma((chips,))]
        scratch += [dma((max(tp_n - 1, 1),))] * 2 + [dma((chips,))] * 8 + [dma((half,))] * 8
        scratch += [dma((heads,))] * 4 + [dma, dma]
        whole = pl.BlockSpec(memory_space=pltpu.VMEM)
        there = pl.BlockSpec(memory_space=pl.ANY)

        def stay(x):
            return pltpu.with_memory_space_constraint(x, pltpu.HBM)

        def body(*refs):
            kernel(ctx_n, tp_n, pp_n, *refs)

        shape = jax.ShapeDtypeStruct((toks, feats), BF16)
        out, gin = pl.pallas_call(
            body,
            out_shape=(shape, shape),
            in_specs=[there] * 6,
            out_specs=(whole, whole),
            scratch_shapes=scratch,
            compiler_params=pltpu.CompilerParams(
                collective_id=0, has_side_effects=True, vmem_limit_bytes=40 * 1024 * 1024
            ),
        )(
            stay(queries[0]), stay(key_input[0]), stay(values[0]), stay(log_decay[0].T),
            stay(conv_weight[0]), stay(out_grad[0]),
        )
        out, gin = pl.pallas_call(
            place,
            out_shape=(shape, shape),
            in_specs=[whole, whole],
            out_specs=(there, there),
            scratch_shapes=[dma((2,))],
            compiler_params=pltpu.CompilerParams(vmem_limit_bytes=1024 * 1024),
        )(out, gin)
        return out[None], gin[None]

    placed = (
        P("pp", "ctx", "tp"),
        P("pp", "ctx", "tp"),
        P("pp", "ctx", "tp"),
        P("pp", "ctx", "tp"),
        P("pp", None, "tp"),
        P("pp", "ctx", "tp"),
    )
    return jax.shard_map(
        per_device,
        mesh=mesh,
        in_specs=placed,
        out_specs=(P("pp", "ctx", "tp"), P("pp", "ctx", "tp")),
        check_vma=False,
    )
```

```python
import jax
import jax.numpy as jnp
from jax import lax
from jax.experimental import pallas as pl
from jax.experimental.pallas import tpu as pltpu
from jax.sharding import PartitionSpec as P

MESH = pl.DeviceIdType.MESH
F32 = jnp.float32
BF16 = jnp.bfloat16
HALO = 8
LAST = 16
GROUP = 2


def remote(src, dst, send_sem, recv_sem, where):
    return pltpu.make_async_remote_copy(
        src_ref=src,
        dst_ref=dst,
        send_sem=send_sem,
        recv_sem=recv_sem,
        device_id=where,
        device_id_type=MESH,
    )


def dot(a, b, dims):
    return lax.dot_general(a, b, (dims, ((), ())), preferred_element_type=F32)


NN = ((1,), (0,))
NT = ((1,), (1,))
TN = ((0,), (0,))


def kernel(
    ctx_n, tp_n, pp_n,
    q_hbm, k_hbm, v_hbm, ld_hbm, w_hbm, og_hbm,
    out_ref, gin_ref,
    ld_ref, w_ref, q_ref, k_ref, v_ref, og_ref, halo_ref, kext, kc, grow, after, mix, wts, att, ag, acc, ckg, gst, sq,
    bt, bt_p, tot, bt_all, acc_sq, acc_dot, tpbuf,
    s_m, s_t, s_out, s_in, p_out, p_in, p_half, p_stage,
    b_m, b_t, b_out, b_in, a_out, a_in, a_half, a_stage,
    here, load_sem, halo_s, halo_r, bp_s, bp_r, bt_s, bt_r, tp_s, tp_r,
    s_s, s_r, p_s, p_r, b_s, b_r, a_s, a_r,
    sx_s, sx_r, px_s, px_r, bx_s, bx_r, ax_s, ax_r, ch_s, ch_r, pp_s, pp_r, pl_s, pl_r,
):
    toks, feats = q_hbm.shape
    heads = ld_hbm.shape[0]
    hd = feats // heads
    taps = w_hbm.shape[0]
    width_all = feats * tp_n
    parts = ctx_n // heads
    rows = s_in.shape[1]
    short = hd - rows * (parts - 1)
    group = min(GROUP, heads // 2)
    steps = heads // group
    half = heads // 2
    half_steps = half // group
    chips = ctx_n // 2
    ctx = lax.axis_index("ctx")
    tp = lax.axis_index("tp")
    pp = lax.axis_index("pp")
    core = lax.rem(ctx, 2)
    chip = ctx // 2
    partner = ctx + 1 - 2 * core
    own0 = half * core
    their0 = half * (1 - core)
    my_head = ctx // parts
    my_part = lax.rem(ctx, parts)
    scan_core = my_head // half

    def lanes(h):
        return pl.ds(pl.multiple_of(h * hd, hd), hd)

    def own_first(idx):
        return lax.rem(own0 + idx, heads)

    def own_last(idx):
        return lax.rem(their0 + idx, heads)

    barrier = pltpu.get_barrier_semaphore()
    greet = [{"ctx": partner}]
    greet += [{"tp": lax.rem(tp + step, tp_n)} for step in range(1, tp_n)]
    loads = [
        pltpu.make_async_copy(src, dst, load_sem.at[n])
        for n, (src, dst) in enumerate(
            (
                (k_hbm, k_ref), (v_hbm, v_ref), (q_hbm, q_ref), (og_hbm, og_ref),
                (ld_hbm, ld_ref), (w_hbm, w_ref),
            )
        )
    ]
    loads[4].start()
    loads[0].start()
    for where in greet:
        pl.semaphore_signal(barrier, inc=1, device_id=where, device_id_type=MESH)

    @pl.when(pp < pp_n - 1)
    def _():
        pl.semaphore_signal(
            barrier, inc=1, device_id={"pp": lax.rem(pp + 1, pp_n)}, device_id_type=MESH
        )

    def enter(peer, _):
        pl.semaphore_signal(barrier, inc=1, device_id={"ctx": peer}, device_id_type=MESH)
        return 0

    lax.fori_loop(2 * chip + 2, ctx_n, enter, 0)

    def meet(z):
        @pl.when(jnp.logical_and(z > chip, z != chip + core))
        def _():
            pl.semaphore_wait(here.at[z], 2)

    for n in (5, 1, 2, 3):
        loads[n].start()

    pl.semaphore_wait(barrier, len(greet) + 2 * chip + (pp + pp_n - 1) // pp_n)

    def answer(peer, _):
        near = 2 * chip - 1 - peer
        pl.semaphore_signal(here.at[chip], inc=1, device_id={"ctx": near}, device_id_type=MESH)
        return 0

    lax.fori_loop(0, 2 * chip, answer, 0)

    rows_i = lax.broadcasted_iota(jnp.int32, (toks, toks), 0)
    cols_i = lax.broadcasted_iota(jnp.int32, (toks, toks), 1)
    causal = rows_i >= cols_i
    tri = causal.astype(F32)
    loads[4].wait()
    ld = ld_ref[...]
    cd = lax.dot_general(
        tri, ld, (NT, ((), ())), precision=lax.Precision.HIGHEST, preferred_element_type=F32
    )
    cdt = lax.dot_general(
        ld, tri, (NT, ((), ())), precision=lax.Precision.HIGHEST, preferred_element_type=F32
    )
    for h in range(heads):
        wide = jnp.broadcast_to(cd[:, h : h + 1], (toks, hd))
        total = wide[toks - 1 : toks, :]
        bt[h] = total
        grow[:, h * hd : (h + 1) * hd] = jnp.exp(wide)
        after[:, h * hd : (h + 1) * hd] = jnp.exp(total - wide)

    tail = halo_ref.shape[0]
    halo = remote(
        k_hbm.at[pl.ds(toks - tail, tail), :], halo_ref, halo_s, halo_r,
        {"ctx": lax.rem(ctx + 1, ctx_n)},
    )

    @pl.when(jnp.logical_and(core == 1, chip < chips - 1))
    def _():
        pl.semaphore_wait(here.at[chip + 1], 2)

    @pl.when(ctx < ctx_n - 1)
    def _():
        halo.start()

    swap_bt = remote(bt, bt_p, bp_s, bp_r, {"ctx": partner})
    swap_bt.start()
    for h in range(heads):
        wide = jnp.broadcast_to(cd[:, h : h + 1], (toks, hd))
        differ = wide - cdt[h : h + 1, :]
        mix[h] = jnp.where(causal, jnp.exp(jnp.where(causal, differ, 0.0)), 0.0)

    @pl.when(ctx == 0)
    def _():
        halo_ref[...] = jnp.zeros_like(halo_ref)

    @pl.when(ctx == ctx_n - 1)
    def _():
        ckg[pl.ds(toks, HALO), :] = jnp.zeros((HALO, feats), F32)

    @pl.when(pp == pp_n - 1)
    def _():
        gin_ref[...] = jnp.zeros_like(gin_ref)

    loads[0].wait()
    loads[5].wait()
    kext[pl.ds(HALO, toks), :] = k_ref[...].astype(F32)
    loads[1].wait()

    @pl.when(ctx > 0)
    def _():
        halo.wait_recv()

    kext[pl.ds(0, HALO), :] = halo_ref[pl.ds(tail - HALO, HALO), :].astype(F32)

    def sized(call):
        @pl.when(my_part < parts - 1)
        def _():
            call(rows)

        @pl.when(my_part == parts - 1)
        def _():
            call(short)

    if short < rows:
        @pl.when(my_part == parts - 1)
        def _():
            s_in[:, pl.ds(short, rows - short), :] = jnp.zeros((chips, rows - short, hd), BF16)
            b_in[:, pl.ds(short, rows - short), :] = jnp.zeros((chips, rows - short, hd), BF16)

    def swap(mine, theirs, send_sem, recv_sem, i):
        return remote(
            mine.at[their0 + i], theirs.at[i], send_sem.at[i], recv_sem.at[i], {"ctx": partner}
        )

    def spread(src, dst, send_sem, recv_sem, i, part):
        size = rows if part < parts - 1 else short
        return remote(
            src.at[i, pl.ds(part * rows, size)], dst.at[chip, pl.ds(0, size)],
            send_sem.at[i * parts + part], recv_sem.at[chip],
            {"ctx": (own0 + i) * parts + part},
        )

    def deliver(src, dst, send_sem, recv_sem, z, size):
        slot = ctx - scan_core * chips
        return remote(
            src.at[z, pl.ds(0, size)], dst.at[slot, pl.ds(0, size)], send_sem.at[z],
            recv_sem.at[slot], {"ctx": 2 * z + scan_core},
        )

    def arrive(dst, recv_sem, n, size):
        piece = dst.at[n, pl.ds(0, size)]
        return remote(piece, piece, recv_sem.at[n], recv_sem.at[n], {"ctx": partner})

    def factors(h, lead):
        e_m = jnp.exp(bt[h])
        e_t = jnp.exp(bt_p[h])
        return e_m, e_t, lead.astype(F32)

    def total_to(i, part):
        return remote(
            tot.at[i], bt_all.at[chip], bt_s.at[i * parts + part], bt_r.at[chip],
            {"ctx": (own0 + i) * parts + part},
        )

    def join(mine, theirs, xs, xr, out, into, send_sem, recv_sem, lead, needed, opening):
        def one(n, _):
            i = n
            h = own0 + i
            e_m, e_t, lf = factors(h, lead)
            swap(mine, theirs, xs, xr, i).wait_recv()
            ca = lf * e_t + (1.0 - lf)
            cb = lf + (1.0 - lf) * e_m
            out[i] = (ca * mine[h] + cb * theirs[i]).astype(BF16)
            if opening:
                tot[i] = bt[h] + bt_p[h]
                low = (h * parts + 1) // 2
                high = (h * parts + parts - 1) // 2
                meet(low)

                @pl.when(high > low)
                def _():
                    meet(high)

            for part in range(parts):
                @pl.when(h * parts + part != ctx)
                def _():
                    @pl.when(needed)
                    def _():
                        spread(out, into, send_sem, recv_sem, i, part).start()

                @pl.when(h * parts + part == ctx)
                def _():
                    size = rows if part < parts - 1 else short
                    into[chip, pl.ds(0, size), :] = out[i, pl.ds(part * rows, size), :]
                    if opening:
                        bt_all[chip] = tot[i]
            return 0

        lax.fori_loop(0, half, one, 0)

        def tell(i, _):
            for part in range(parts):
                @pl.when((own0 + i) * parts + part != ctx)
                def _():
                    total_to(i, part).start()

            return 0

        if opening:
            lax.fori_loop(0, half, tell, 0)

    def scan(into, recv_sem, out, home, send_sem, home_sem, opening):
        def give(z, carry):
            out[z] = carry.astype(BF16)
            late = jnp.where(z >= chips // 2, 1, 0)

            @pl.when(late != core)
            def _():
                meet(z)

            send(z)

        def send(z):
            @pl.when(2 * z + scan_core != ctx)
            def _():
                sized(lambda size: deliver(out, home, send_sem, home_sem, z, size).start())

            @pl.when(2 * z + scan_core == ctx)
            def _():
                home[ctx - scan_core * chips] = out[z]

        def total_in(z):
            @pl.when(2 * z + scan_core != ctx)
            def _():
                remote(
                    bt_all.at[z], bt_all.at[z], bt_r.at[z], bt_r.at[z], {"ctx": partner}
                ).wait_recv()

        if not opening:
            total_in(chips - 1)

            def ready(z, _):
                @pl.when(2 * z + scan_core != ctx)
                def _():
                    sized(lambda size: arrive(into, recv_sem, z, size).wait_recv())

                return 0

            lax.fori_loop(1, chips, ready, 0)
            carry = jnp.zeros((rows, hd), F32)
            for z in range(chips - 1, -1, -1):
                out[z] = carry.astype(BF16)
                if z > 0:
                    carry = jnp.exp(bt_all[z]) * carry + into[z].astype(F32)

            def serve(z, _):
                send(z)
                return 0

            lax.fori_loop(0, chips, serve, 0)
            return

        def one(n, carry):
            z = n
            give(z, carry)
            total_in(z)

            @pl.when(2 * z + scan_core != ctx)
            def _():
                sized(lambda size: arrive(into, recv_sem, z, size).wait_recv())

            return jnp.exp(bt_all[z]) * carry + into[z].astype(F32)

        carry = lax.fori_loop(0, chips - 1, one, jnp.zeros((rows, hd), F32))
        give(chips - 1, carry)

    def hand(stage, dest, send_sem, recv_sem, i, h):
        return remote(
            stage.at[i], dest.at[h], send_sem.at[i], recv_sem.at[i], {"ctx": partner}
        )

    def split(home, home_sem, mine, theirs, dest, stage, hs_, hr_, lead):
        def one(n, _):
            i = n
            h = own0 + i
            e_m, e_t, lf = factors(h, lead)
            pieces = []
            for part in range(parts):
                size = rows if part < parts - 1 else short

                @pl.when(h * parts + part != ctx)
                def _():
                    arrive(home, home_sem, i * parts + part, size).wait_recv()

                pieces.append(home[i * parts + part, pl.ds(0, size), :].astype(F32))
            carry = jnp.concatenate(pieces, axis=0)
            c1 = lf + (1.0 - lf) * e_t
            c2 = lf * e_m + (1.0 - lf)
            stage[i] = (c2 * carry + lf * mine[h]).astype(BF16)
            hand(stage, dest, hs_, hr_, i, h).start()
            dest[h] = (c1 * carry + (1.0 - lf) * theirs[i]).astype(BF16)
            return 0

        lax.fori_loop(0, half, one, 0)

    def handed(stage, dest, hs_, hr_, g):
        @pl.when(g >= half_steps)
        def _():
            for j in range(group):
                h = own_first(g * group + j)
                hand(stage, dest, hs_, hr_, h - their0, h).wait_recv()

    def states(g, _):
        for j in range(group):
            h = own_last(g * group + j)
            hs = lanes(h)
            conv = w_ref[pl.ds(0, 1), hs] * kext[pl.ds(HALO, toks), hs]
            for tap in range(1, taps):
                conv = conv + w_ref[pl.ds(tap, 1), hs] * kext[pl.ds(HALO - tap, toks), hs]
            keys = conv.astype(BF16)
            kc[:, hs] = keys
            scaled = (keys.astype(F32) * after[:, hs]).astype(BF16)
            s_m[h] = dot(scaled, v_ref[:, hs], TN)

        @pl.when(g < half_steps)
        def _():
            for j in range(group):
                swap(s_m, s_t, sx_s, sx_r, own_last(g * group + j) - their0).start()

        return 0

    lax.fori_loop(0, steps, states, 0)
    swap_bt.wait_recv()
    join(s_m, s_t, sx_s, sx_r, s_out, s_in, s_s, s_r, core == 0, chip < chips - 1, True)
    loads[2].wait()

    def inside(g, _):
        for j in range(group):
            h = g * group + j
            hs = lanes(h)
            scores = dot(q_ref[:, hs], kc[:, hs], NT)
            w = (scores * mix[h]).astype(BF16)
            wts[h] = w
            att[:, hs] = dot(w, v_ref[:, hs], NN)
            sq[:, hs] = (q_ref[:, hs].astype(F32) * grow[:, hs]).astype(BF16)
        return 0

    lax.fori_loop(0, steps, inside, 0)

    scan(s_in, s_r, p_out, p_in, p_s, p_r, True)
    split(p_in, p_r, s_m, s_t, p_half, p_stage, px_s, px_r, core == 0)

    loads[3].wait()
    acc_sq[...] = jnp.zeros_like(acc_sq)
    acc_dot[...] = jnp.zeros_like(acc_dot)

    def attend(g, _):
        handed(p_stage, p_half, px_s, px_r, g)
        for j in range(group):
            h = own_first(g * group + j)
            hs = lanes(h)
            a = att[:, hs] + grow[:, hs] * dot(q_ref[:, hs], p_half[h], NN)
            att[:, hs] = a
            acc_sq[...] += a * a
            acc_dot[...] += a * og_ref[:, hs].astype(F32)
        return 0

    lax.fori_loop(0, steps, attend, 0)

    sq_row = jnp.sum(acc_sq[...].T, axis=0, keepdims=True)
    dot_row = jnp.sum(acc_dot[...].T, axis=0, keepdims=True)
    first_row = lax.broadcasted_iota(jnp.int32, (8, toks), 0) == 0
    tpbuf[0] = jnp.where(first_row, sq_row, dot_row)

    def sums(step):
        return remote(
            tpbuf.at[0], tpbuf.at[step], tp_s.at[step - 1], tp_r.at[step - 1],
            {"tp": lax.rem(tp + step, tp_n)},
        )

    for step in range(1, tp_n):
        sums(step).start()
    for step in range(1, tp_n):
        sums(step).wait_recv()
    sums_all = tpbuf[0]
    for step in range(1, tp_n):
        sums_all = sums_all + tpbuf[step]
    inv_row = 1.0 / jnp.sqrt(sums_all[0:1, :] / width_all + 1e-06)
    shift_row = (sums_all[1:2, :] / width_all) * inv_row
    inv = jnp.broadcast_to(inv_row, (hd, toks)).T
    shift = jnp.broadcast_to(shift_row, (hd, toks)).T

    def adjoints(g, _):
        for j in range(group):
            h = own_last(g * group + j)
            hs = lanes(h)
            normed = att[:, hs] * inv
            grad = ((og_ref[:, hs].astype(F32) - normed * shift) * inv).astype(BF16)
            ag[:, hs] = grad
            b_m[h] = dot(sq[:, hs], grad, TN)

        @pl.when(g < half_steps)
        def _():
            for j in range(group):
                swap(b_m, b_t, bx_s, bx_r, own_last(g * group + j) - their0).start()

        return 0

    lax.fori_loop(0, steps, adjoints, 0)
    join(b_m, b_t, bx_s, bx_r, b_out, b_in, b_s, b_r, core == 1, chip > 0, False)

    def inside_grads(g, _):
        for j in range(group):
            h = g * group + j
            hs = lanes(h)
            grad = ag[:, hs]
            out_ref[:, hs] = (att[:, hs] * inv).astype(BF16)
            sg = (dot(grad, v_ref[:, hs], NT) * mix[h]).astype(BF16)
            qg = dot(sg, kc[:, hs], NN) + grow[:, hs] * dot(grad, p_half[h], NT)
            acc[:, hs] = qg + dot(wts[h], grad, TN)
            ckg[pl.ds(0, toks), hs] = dot(sg, q_ref[:, hs], TN)
        return 0

    lax.fori_loop(0, steps, inside_grads, 0)
    scan(b_in, b_r, a_out, a_in, a_s, a_r, False)
    split(a_in, a_r, b_m, b_t, a_half, a_stage, ax_s, ax_r, core == 1)

    def edge(h):
        hs = lanes(h)
        return remote(
            ckg.at[pl.ds(0, HALO), hs], ckg.at[pl.ds(toks, HALO), hs], ch_s.at[h], ch_r.at[h],
            {"ctx": lax.rem(ctx + ctx_n - 1, ctx_n)},
        )

    most = toks - LAST

    def summed(h, first, size):
        hs = lanes(h)
        total = acc[pl.ds(first, size), hs]
        for tap in range(taps):
            total = total + w_ref[pl.ds(tap, 1), hs] * ckg[pl.ds(first + tap, size), hs]
        gst[pl.ds(first, size), hs] = total.astype(BF16)

    def back(h):
        piece = (pl.ds(0, most), lanes(h))
        return remote(
            gst.at[piece], gin_ref.at[piece], pp_s.at[h], pp_r.at[h],
            {"pp": lax.rem(pp + pp_n - 1, pp_n)},
        )

    back_last = remote(
        gst.at[pl.ds(most, LAST), :], gin_ref.at[pl.ds(most, LAST), :], pl_s, pl_r,
        {"pp": lax.rem(pp + pp_n - 1, pp_n)},
    )

    def outside_grads(g, _):
        handed(a_stage, a_half, ax_s, ax_r, g)
        for j in range(group):
            h = own_first(g * group + j)
            hs = lanes(h)
            wa = after[:, hs]
            state = a_half[h]
            ckg[pl.ds(0, toks), hs] += wa * dot(v_ref[:, hs], state, NT)
            acc[:, hs] += wa * dot(kc[:, hs], state, NN)

        @pl.when(ctx > 0)
        def _():
            for j in range(group):
                edge(own_first(g * group + j)).start()

        for j in range(group):
            summed(own_first(g * group + j), 0, most)

        @pl.when(pp > 0)
        def _():
            for j in range(group):
                back(own_first(g * group + j)).start()

        return 0

    lax.fori_loop(0, steps, outside_grads, 0)

    def finish(g, _):
        @pl.when(ctx < ctx_n - 1)
        def _():
            for j in range(group):
                edge(own_last(g * group + j)).wait_recv()

        for j in range(group):
            summed(own_last(g * group + j), most, LAST)
        return 0

    lax.fori_loop(0, steps, finish, 0)

    @pl.when(pp > 0)
    def _():
        back_last.start()

    @pl.when(ctx < ctx_n - 1)
    def _():
        halo.wait_send()

    for step in range(1, tp_n):
        sums(step).wait_send()

    swap_bt.wait_send()

    def left(i, _):
        h = own0 + i
        swap(s_m, s_t, sx_s, sx_r, i).wait_send()
        swap(b_m, b_t, bx_s, bx_r, i).wait_send()
        hand(p_stage, p_half, px_s, px_r, i, h).wait_send()
        hand(a_stage, a_half, ax_s, ax_r, i, h).wait_send()
        for part in range(parts):
            @pl.when(h * parts + part != ctx)
            def _():
                total_to(i, part).wait_send()

                @pl.when(chip < chips - 1)
                def _():
                    spread(s_out, s_in, s_s, s_r, i, part).wait_send()

                @pl.when(chip > 0)
                def _():
                    spread(b_out, b_in, b_s, b_r, i, part).wait_send()

        return 0

    lax.fori_loop(0, half, left, 0)

    def given(z, _):
        @pl.when(2 * z + scan_core != ctx)
        def _():
            sized(lambda size: deliver(p_out, p_in, p_s, p_r, z, size).wait_send())
            sized(lambda size: deliver(a_out, a_in, a_s, a_r, z, size).wait_send())

        return 0

    lax.fori_loop(0, chips, given, 0)

    @pl.when(ctx > 0)
    def _():
        def leave(h, _):
            edge(h).wait_send()
            return 0

        lax.fori_loop(0, heads, leave, 0)

    @pl.when(pp > 0)
    def _():
        def leave(h, _):
            back(h).wait_send()
            return 0

        lax.fori_loop(0, heads, leave, 0)
        back_last.wait_send()

    @pl.when(pp < pp_n - 1)
    def _():
        def land(h, _):
            back(h).wait_recv()
            return 0

        lax.fori_loop(0, heads, land, 0)
        back_last.wait_recv()


def place(a_ref, b_ref, c_ref, d_ref, sems):
    puts = [
        pltpu.make_async_copy(src, dst, sems.at[n])
        for n, (src, dst) in enumerate(((a_ref, c_ref), (b_ref, d_ref)))
    ]
    for put in puts:
        put.start()
    for put in puts:
        put.wait()


def solution(mesh):
    ctx_n, tp_n, pp_n = mesh.shape["ctx"], mesh.shape["tp"], mesh.shape["pp"]

    def per_device(queries, key_input, values, log_decay, conv_weight, out_grad):
        toks, feats = queries.shape[1:]
        heads = log_decay.shape[2]
        hd = feats // heads
        parts = ctx_n // heads
        rows = -(-hd // (16 * parts)) * 16
        dma = pltpu.SemaphoreType.DMA
        flat_b = pltpu.VMEM((toks, feats), BF16)
        flat_f = pltpu.VMEM((toks, feats), F32)
        half = heads // 2
        chips = ctx_n // 2
        full_f = pltpu.VMEM((heads, hd, hd), F32)
        full_b = pltpu.VMEM((heads, hd, hd), BF16)
        half_f = pltpu.VMEM((half, hd, hd), F32)
        half_b = pltpu.VMEM((half, hd, hd), BF16)
        shares = pltpu.VMEM((chips, rows, hd), BF16)
        totals = pltpu.VMEM((heads, 1, hd), F32)
        scanned = [full_f, half_f, half_b, shares, shares, shares, full_b, half_b]
        longer = pltpu.VMEM((toks + HALO, feats), F32)
        square = pltpu.VMEM((toks, hd), F32)
        scratch = [
            pltpu.VMEM((heads, toks), F32), pltpu.VMEM((conv_weight.shape[1], feats), F32),
            flat_b, flat_b, flat_b, flat_b, pltpu.VMEM((16, feats), BF16), longer, flat_b,
            flat_f, flat_f, pltpu.VMEM((heads, toks, toks), F32),
            pltpu.VMEM((heads, toks, toks), BF16), flat_f, flat_b, flat_f, longer, flat_b, flat_b,
            totals, totals, pltpu.VMEM((half, 1, hd), F32), pltpu.VMEM((chips, 1, hd), F32),
            square, square,
            pltpu.VMEM((tp_n, 8, toks), F32),
        ]
        scratch += scanned + scanned
        scratch += [pltpu.SemaphoreType.REGULAR((chips,))]
        scratch += [dma((6,)), dma, dma, dma, dma, dma((chips,)), dma((chips,))]
        scratch += [dma((max(tp_n - 1, 1),))] * 2 + [dma((chips,))] * 8 + [dma((half,))] * 8
        scratch += [dma((heads,))] * 4 + [dma, dma]
        whole = pl.BlockSpec(memory_space=pltpu.VMEM)
        there = pl.BlockSpec(memory_space=pl.ANY)

        def stay(x):
            return pltpu.with_memory_space_constraint(x, pltpu.HBM)

        def body(*refs):
            kernel(ctx_n, tp_n, pp_n, *refs)

        shape = jax.ShapeDtypeStruct((toks, feats), BF16)
        out, gin = pl.pallas_call(
            body,
            out_shape=(shape, shape),
            in_specs=[there] * 6,
            out_specs=(whole, whole),
            scratch_shapes=scratch,
            compiler_params=pltpu.CompilerParams(
                collective_id=0, has_side_effects=True, vmem_limit_bytes=40 * 1024 * 1024
            ),
        )(
            stay(queries[0]), stay(key_input[0]), stay(values[0]), stay(log_decay[0].T),
            stay(conv_weight[0]), stay(out_grad[0]),
        )
        out, gin = pl.pallas_call(
            place,
            out_shape=(shape, shape),
            in_specs=[whole, whole],
            out_specs=(there, there),
            scratch_shapes=[dma((2,))],
            compiler_params=pltpu.CompilerParams(vmem_limit_bytes=1024 * 1024),
        )(out, gin)
        return out[None], gin[None]

    placed = (
        P("pp", "ctx", "tp"),
        P("pp", "ctx", "tp"),
        P("pp", "ctx", "tp"),
        P("pp", "ctx", "tp"),
        P("pp", None, "tp"),
        P("pp", "ctx", "tp"),
    )
    return jax.shard_map(
        per_device,
        mesh=mesh,
        in_specs=placed,
        out_specs=(P("pp", "ctx", "tp"), P("pp", "ctx", "tp")),
        check_vma=False,
    )
```
